32 devices in a mesh: dp: 2 (over core), seq: 4 (over y, x), tensor: 4 (over z).
Axes of the slice: x: 2, y: 2, z: 4, core: 2. Of those that a mesh axis runs over, the one named last changes fastest.
Arguments:
- hidden: float32 [2, 3120, 1536], P('dp', 'seq'), may hold values from -6 to 6
- teacher: float32 [2, 3120, 1536], P('dp', 'seq'), may hold values from -6 to 6
- text: float32 [2, 512, 1536], P('dp', 'seq'), may hold values from -6 to 6
- time_embed: float32 [2, 6, 1536], P('dp'), may hold values from -3 to 3
- lengths: int32 [2], replicated, may hold values from 780 to 3120, as said below
- positions: int32 [3, 2, 3120], P(None, 'dp', 'seq'), may hold values from 0 to 63
- modulation: float32 [6, 1536], replicated, may hold values from -2 to 2
- self_in: bfloat16 [3, 1536, 1536], P(None, None, 'tensor'), may hold values from -0.15625 to 0.15625
- self_bias: float32 [3, 1536], P(None, 'tensor'), may hold values from -2 to 2
- self_out: bfloat16 [1536, 1536], P('tensor'), may hold values from -0.875 to 0.875
- norm_gains: float32 [4, 1536], P(None, 'tensor'), may hold values from 1 to 2
- cross_gain: float32 [1536], replicated, may hold values from 0.5 to 1.5
- cross_shift: float32 [1536], replicated, may hold values from -2 to 2
- cross_q: bfloat16 [1536, 1536], P(None, 'tensor'), may hold values from -0.15625 to 0.15625
- cross_kv: bfloat16 [2, 1536, 1536], P(None, None, 'tensor'), may hold values from -0.15625 to 0.15625
- cross_bias: float32 [3, 1536], P(None, 'tensor'), may hold values from -2 to 2
- cross_out: bfloat16 [1536, 1536], P('tensor'), may hold values from -0.4375 to 0.4375
- ffn_in: bfloat16 [1536, 8960], P(None, 'tensor'), may hold values from -0.15625 to 0.15625
- ffn_in_bias: float32 [8960], P('tensor'), may hold values from -2 to 2
- ffn_out: bfloat16 [8960, 1536], P('tensor'), may hold values from -0.0625 to 0.0625
- out_bias: float32 [3, 1536], replicated, may hold values from -2 to 2
Outputs:
- result: float32 [2, 3120, 1536], P('dp', 'seq')
- loss: float32 [], replicated
- grad_hidden: float32 [2, 3120, 1536], P('dp', 'seq')
- grad_text: float32 [2, 512, 1536], P('dp', 'seq')
- grad_time: float32 [2, 6, 1536], P('dp')
- grad_modulation: float32 [6, 1536], replicated
- grad_self_in: float32 [3, 1536, 1536], P(None, ('dp', 'seq'), 'tensor')
- grad_self_bias: float32 [3, 1536], P(None, 'tensor')
- grad_self_out: float32 [1536, 1536], P('tensor', ('dp', 'seq'))
- grad_norm_gains: float32 [4, 1536], P(None, 'tensor')
- grad_cross_gain: float32 [1536], replicated
- grad_cross_shift: float32 [1536], replicated
- grad_cross_q: float32 [1536, 1536], P(('dp', 'seq'), 'tensor')
- grad_cross_kv: float32 [2, 1536, 1536], P(None, ('dp', 'seq'), 'tensor')
- grad_cross_bias: float32 [3, 1536], P(None, 'tensor')
- grad_cross_out: float32 [1536, 1536], P('tensor', ('dp', 'seq'))
- grad_ffn_in: float32 [1536, 8960], P(('dp', 'seq'), 'tensor')
- grad_ffn_in_bias: float32 [8960], P('tensor')
- grad_ffn_out: float32 [8960, 1536], P('tensor', ('dp', 'seq'))
- grad_out_bias: float32 [3, 1536], replicated
The draws below stay inside these ranges and needn't reach their ends.
Inputs may be any that keep to these rules, and one draw needn't show every extreme that they name: Each clip's first lengths slots are valid and the rest are padding; some clip is full (3120 slots) and some clip has exactly 780.
All inputs are finite; a program needn't handle non-finite values.
Results may differ from the reference program's by a relative error of at most 0.017.
The reference program's roundings to bfloat16 on the way count: a program that leaves them out, or rounds other values in their place, can miss the bound.
Values may be sent and summed in bfloat16 or wider, within the bound.
A program may use at most 448 MiB of HBM per device.

```python
import math
from functools import partial
import jax
import jax.numpy as jnp
from jax import lax

D = 1536
HEADS = 12
HEAD_DIM = 128
FF = 8960
TEXT = 512
L = 3120
CLIPS = 2


def draw_lengths(key, part):
    drawn_len = jax.random.randint(jax.random.fold_in(key, 11), (CLIPS,), L // 4, L + 1)
    shuffled = jax.random.permutation(jax.random.fold_in(key, 12), CLIPS)
    drawn_len = drawn_len.at[shuffled[0]].set(L)
    drawn_len = drawn_len.at[shuffled[1]].set(L // 4)
    return drawn_len.astype(jnp.int32)


def plant(drawn, rng, low, high):
    longest = drawn.shape.index(max(drawn.shape))
    spots = []
    for shift in (0, 1):
        where = [jax.random.randint(jax.random.fold_in(rng, axis), (), 0, length) for axis, length in enumerate(drawn.shape)]
        where[longest] = (where[longest] + shift) % drawn.shape[longest]
        spots.append(tuple(where))
    return drawn.at[spots[0]].set(low).at[spots[1]].set(high)


def shard_levels(stream_key, shape, split, smallest, top_value):
    level = 1.0
    for position, parts in split:
        steps = jax.random.uniform(jax.random.fold_in(jax.random.fold_in(stream_key, 6), position), (parts,), jnp.float32, smallest / len(split), top_value / len(split))
        level = level * jnp.repeat(jnp.exp(steps), shape[position] // parts).reshape((-1,) + (1,) * (len(shape) - 1 - position))
    return level


def noise(own_key, dims, spread, most, split=(), kind=jnp.bfloat16):
    values = jax.random.normal(own_key, dims, jnp.float32) * spread
    if len(split) > 0:
        values = shard_levels(own_key, dims, split, -0.22, 0.18) * values
    return jnp.clip(values, min=-most, max=most).astype(kind)


def setup_inputs(seed: int = 0) -> dict:
    key_list = jax.random.split(jax.random.key(seed), 22)
    return {
        "hidden": noise(key_list[0], (CLIPS, L, D), 1.0, 6.0, ((0, 2), (1, 4)), jnp.float32),
        "teacher": noise(key_list[1], (CLIPS, L, D), 1.0, 6.0, ((0, 2), (1, 4)), jnp.float32),
        "text": noise(key_list[2], (CLIPS, TEXT, D), 1.0, 6.0, ((0, 2), (1, 4)), jnp.float32),
        "time_embed": noise(key_list[3], (CLIPS, 6, D), 0.5, 3.0, ((0, 2),), jnp.float32),
        "lengths": draw_lengths(jax.random.fold_in(key_list[21], 71), 0),
        "positions": plant(jax.random.randint(key_list[5], (3, CLIPS, L), 0, 64), jax.random.fold_in(key_list[5], 1), 0, 63).astype(jnp.int32),
        "modulation": noise(key_list[6], (6, D), 0.3, 2.0, (), jnp.float32),
        "self_in": noise(key_list[7], (3, D, D), D ** -0.5, 0.15625, ((2, 4),)),
        "self_bias": noise(key_list[8], (3, D), 0.3, 2.0, ((1, 4),), jnp.float32),
        "self_out": noise(key_list[9], (D, D), (D // 32) ** -0.5, 0.875, ((0, 4),)),
        "norm_gains": jnp.clip(1.0 + 1.0 * jax.random.uniform(key_list[10], (4, D), jnp.float32) ** shard_levels(key_list[10], (4, D), ((1, 4),), -0.2, 0.2), 1.0, 2.0),
        "cross_gain": jnp.clip(1.0 + 0.1 * jax.random.normal(key_list[11], (D,), jnp.float32), 0.5, 1.5),
        "cross_shift": noise(key_list[12], (D,), 0.3, 2.0, (), jnp.float32),
        "cross_q": noise(key_list[13], (D, D), D ** -0.5, 0.15625, ((1, 4),)),
        "cross_kv": noise(key_list[14], (2, D, D), D ** -0.5, 0.15625, ((2, 4),)),
        "cross_bias": noise(key_list[15], (3, D), 0.3, 2.0, ((1, 4),), jnp.float32),
        "cross_out": noise(key_list[16], (D, D), (D // 8) ** -0.5, 0.4375, ((0, 4),)),
        "ffn_in": noise(key_list[17], (D, FF), D ** -0.5, 0.15625, ((1, 4),)),
        "ffn_in_bias": noise(key_list[18], (FF,), 0.3, 2.0, ((0, 4),), jnp.float32),
        "ffn_out": noise(key_list[19], (FF, D), FF ** -0.5, 0.0625, ((0, 4),)),
        "out_bias": noise(key_list[20], (3, D), 0.3, 2.0, (), jnp.float32),
    }


@jax.custom_vjp
def low(v):
    return lax.optimization_barrier(v.astype(jnp.bfloat16)).astype(jnp.float32)

@jax.custom_vjp
def low_back(v):
    return v

def low_keep(v):
    return (low(v), None)

def low_pass(kept, grad):
    return (grad,)

def back_keep(v):
    return (v, None)

def back_low(kept, grad):
    return (low(grad),)
low.defvjp(low_keep, low_pass)
low_back.defvjp(back_keep, back_low)
eps_norm = 1e-06

def round_both(values):
    return low_back(low(values))

def product_high(left_side, right_side):
    return jnp.matmul(left_side, right_side, precision=lax.Precision.HIGHEST)

def layer_norm(values):
    centred = values - lax.optimization_barrier(jnp.mean(values, axis=-1, keepdims=True))
    return centred * lax.rsqrt(lax.optimization_barrier(jnp.mean(centred * centred, axis=-1, keepdims=True)) + eps_norm)

def rms_norm(values, gain_row):
    return values * lax.rsqrt(lax.optimization_barrier(jnp.mean(values * values, axis=-1, keepdims=True)) + eps_norm) * gain_row

def gelu_tanh(values):
    return 0.5 * values * (1.0 + jnp.tanh(0.7978845608028654 * (values + 0.044715 * values * values * values)))

def rope_angles(positions, head_size):
    sixth_part = head_size // 6
    part_spans = (head_size - 4 * sixth_part, 2 * sixth_part, 2 * sixth_part)
    pieces = []
    for axis_no in range(3):
        span_now = part_spans[axis_no]
        inverse = 1.0 / 10000.0 ** (jnp.arange(0, span_now, 2).astype(jnp.float32) / span_now)
        pieces.append(positions[axis_no].astype(jnp.float32)[..., None] * inverse)
    angles = jnp.concatenate(pieces, axis=-1)
    return (jnp.cos(angles)[..., None, :], jnp.sin(angles)[..., None, :])

def rotate(values, cosine_half, sine_half):
    dims_in = values.shape
    paired = values.reshape(dims_in[:-1] + (dims_in[-1] // 2, 2))
    even_part = paired[..., 0]
    odd_part = paired[..., 1]
    turned = jnp.stack([even_part * cosine_half - odd_part * sine_half, even_part * sine_half + odd_part * cosine_half], axis=-1)
    return turned.reshape(dims_in)

def attend_head(head_items):
    query, keys, values, key_ok = head_items
    scores = low_back(product_high(query, keys.T) * (1.0 / math.sqrt(HEAD_DIM)))
    scores = jnp.where(key_ok[None, :], scores, -jnp.inf)
    row_peak = lax.optimization_barrier(jnp.max(scores, axis=-1, keepdims=True))
    exp_terms = jnp.exp(scores - row_peak)
    probs = exp_terms / lax.optimization_barrier(jnp.sum(exp_terms, axis=-1, keepdims=True))
    return product_high(low(probs), values)

def heads_first(values):
    return values.reshape(values.shape[0], HEADS, HEAD_DIM).transpose(1, 0, 2)

def attention(query, keys, values, key_ok):
    masks = jnp.broadcast_to(key_ok, (HEADS,) + key_ok.shape)
    attended = lax.map(jax.checkpoint(attend_head), (heads_first(query), heads_first(keys), heads_first(values), masks))
    return attended.transpose(1, 0, 2).reshape(query.shape[0], HEADS * HEAD_DIM)

def clip_forward(tokens, text_in, time_in, params, cosine_half, sine_half, key_ok):
    modulation, self_in, self_bias, self_out, norm_gains, cross_gain, cross_shift, cross_q, cross_kv, cross_bias, cross_out, ffn_in, ffn_in_bias, ffn_out, out_bias = params
    slot_total = tokens.shape[0]
    modulated = modulation + time_in
    attn_in = low(layer_norm(tokens) * (1.0 + modulated[1]) + modulated[0])
    query_pre = low_back(product_high(attn_in, self_in[0])) + self_bias[0]
    key_pre = low_back(product_high(attn_in, self_in[1])) + self_bias[1]
    value_pre = low_back(product_high(attn_in, self_in[2])) + self_bias[2]
    head_shape = (slot_total, HEADS, HEAD_DIM)
    query_low = low(rotate(rms_norm(query_pre, norm_gains[0]).reshape(head_shape), cosine_half, sine_half).reshape(slot_total, HEADS * HEAD_DIM))
    key_low = low(rotate(rms_norm(key_pre, norm_gains[1]).reshape(head_shape), cosine_half, sine_half).reshape(slot_total, HEADS * HEAD_DIM))
    value_low = low(value_pre)
    attn_low = round_both(attention(query_low, key_low, value_low, key_ok))
    branch_one = low_back(product_high(attn_low, self_out)) + out_bias[0]
    after_one = tokens + branch_one * modulated[2]
    cross_in = low(layer_norm(after_one) * cross_gain + cross_shift)
    cross_query_pre = low_back(product_high(cross_in, cross_q)) + cross_bias[0]
    cross_query_low = low(rms_norm(cross_query_pre, norm_gains[2]))
    text_low = low(text_in)
    text_key_pre = low_back(product_high(text_low, cross_kv[0])) + cross_bias[1]
    text_key_low = low(rms_norm(text_key_pre, norm_gains[3]))
    text_value_low = low(low_back(product_high(text_low, cross_kv[1])) + cross_bias[2])
    text_ok = jnp.ones((TEXT,), dtype=jnp.bool_)
    cross_att_low = round_both(attention(cross_query_low, text_key_low, text_value_low, text_ok))
    branch_two = low_back(product_high(cross_att_low, cross_out)) + out_bias[1]
    after_two = after_one + branch_two
    ffn_input = low(layer_norm(after_two) * (1.0 + modulated[4]) + modulated[3])
    pre_act = low_back(product_high(ffn_input, ffn_in)) + ffn_in_bias
    branch_three = low_back(product_high(low(gelu_tanh(pre_act)), ffn_out)) + out_bias[2]
    return after_two + branch_three * modulated[5]

def reference(hidden, teacher, text, time_embed, lengths, positions, modulation, self_in, self_bias, self_out, norm_gains, cross_gain, cross_shift, cross_q, cross_kv, cross_bias, cross_out, ffn_in, ffn_in_bias, ffn_out, out_bias):
    params = (modulation, self_in.astype(jnp.float32), self_bias, self_out.astype(jnp.float32), norm_gains, cross_gain, cross_shift, cross_q.astype(jnp.float32), cross_kv.astype(jnp.float32), cross_bias, cross_out.astype(jnp.float32), ffn_in.astype(jnp.float32), ffn_in_bias, ffn_out.astype(jnp.float32), out_bias)
    slot_ids = jnp.arange(hidden.shape[1], dtype=jnp.int32)

    def one_clip(carry, clip_items):
        grads_sum, square_sum = carry
        tokens, target, text_in, time_in, length, clip_pos = clip_items
        cosine_half, sine_half = rope_angles(clip_pos, HEAD_DIM)
        key_ok = slot_ids < length
        forward = partial(clip_forward, cosine_half=cosine_half, sine_half=sine_half, key_ok=key_ok)
        result, pullback = jax.vjp(forward, tokens, text_in, time_in, params)
        residue = jnp.where(key_ok[:, None], result - target, 0.0)
        grad_tokens, grad_text_in, grad_time_in, grad_params = pullback(residue)
        grads_sum = jax.tree.map(jnp.add, grads_sum, grad_params)
        square_sum = square_sum + jnp.sum(residue * residue)
        return ((grads_sum, square_sum), (result, grad_tokens, grad_text_in, grad_time_in))
    empty_grads = jax.tree.map(jnp.zeros_like, params)
    clip_inputs = (hidden, teacher, text, time_embed, lengths, jnp.transpose(positions, (1, 0, 2)))
    (grad_params, square_sum), (result, grad_hidden, grad_text, grad_time) = lax.scan(one_clip, (empty_grads, jnp.zeros((), jnp.float32)), clip_inputs)
    loss = square_sum / (jnp.sum(lengths).astype(jnp.float32) * D)
    return (result, loss, grad_hidden, grad_text, grad_time, grad_params[0], grad_params[1], grad_params[2], grad_params[3], grad_params[4], grad_params[5], grad_params[6], grad_params[7], grad_params[8], grad_params[9], grad_params[10], grad_params[11], grad_params[12], grad_params[13], grad_params[14])
```

```python
import functools
import math

import jax
import jax.numpy as jnp
from jax import lax
from jax.sharding import PartitionSpec as P

HEAD_DIM = 128


eps_norm = 1e-06


def layer_norm(values):
    centred = values - jnp.mean(values, axis=-1, keepdims=True)
    return centred * lax.rsqrt(jnp.mean(centred * centred, axis=-1, keepdims=True) + eps_norm)


def gelu_tanh(values):
    return (
        0.5
        * values
        * (1.0 + jnp.tanh(0.7978845608028654 * (values + 0.044715 * values * values * values)))
    )


def rope_tables(positions, head_size):
    sixth_part = head_size // 6
    part_spans = (head_size - 4 * sixth_part, 2 * sixth_part, 2 * sixth_part)
    pieces = []
    for axis_no in range(3):
        span_now = part_spans[axis_no]
        inverse = 1.0 / 10000.0 ** (jnp.arange(0, span_now, 2).astype(jnp.float32) / span_now)
        pieces.append(positions[axis_no].astype(jnp.float32)[..., None] * inverse)
    angles = jnp.concatenate(pieces, axis=-1)
    cosine_rep = jnp.repeat(jnp.cos(angles), 2, axis=-1)[..., None, :]
    sine_rep = jnp.repeat(jnp.sin(angles), 2, axis=-1)[..., None, :]
    return (cosine_rep, sine_rep)


def swap_table(head_size):
    row_no = jnp.arange(head_size)[:, None]
    col_no = jnp.arange(head_size)[None, :]
    upward = jnp.where((row_no % 2 == 0) & (col_no == row_no + 1), 1.0, 0.0)
    downward = jnp.where((row_no % 2 == 1) & (col_no == row_no - 1), -1.0, 0.0)
    return (upward + downward).astype(jnp.float32)


def rotate(values, cosine_rep, sine_rep, swap_matrix):
    swapped = jnp.matmul(values, swap_matrix, precision=lax.Precision.HIGHEST)
    return values * cosine_rep + swapped * sine_rep


def tensor_pair(first_term, second_term):
    return lax.psum((first_term, second_term), "tensor")


def stream_sum(partial_out):
    return lax.psum(partial_out.astype(jnp.bfloat16), "tensor").astype(jnp.float32)


def head_forward(query, keys, values, key_ok, score_scale):
    scores = (
        jnp.einsum("csh,clh->csl", query, keys, preferred_element_type=jnp.float32) * score_scale
    )
    scores = jnp.where(key_ok[:, None, :], scores, -jnp.inf)
    row_peak = jnp.max(scores, axis=-1, keepdims=True)
    exp_terms = jnp.exp(scores - row_peak)
    summed = jnp.sum(exp_terms, axis=-1, keepdims=True)
    probs_low = (exp_terms / summed).astype(jnp.bfloat16)
    attended = jnp.einsum("csl,clh->csh", probs_low, values, preferred_element_type=jnp.float32)
    return (attended, row_peak[..., 0] + jnp.log(summed[..., 0]))


def head_backward(query, keys, values, key_ok, log_total, grad_att, score_scale):
    scores = (
        jnp.einsum("csh,clh->csl", query, keys, preferred_element_type=jnp.float32) * score_scale
    )
    probs = jnp.where(key_ok[:, None, :], jnp.exp(scores - log_total[..., None]), 0.0)
    grad_probs = jnp.einsum("csh,clh->csl", grad_att, values, preferred_element_type=jnp.float32)
    centre = jnp.sum(probs * grad_probs, axis=-1)
    grad_scores = (probs * (grad_probs - centre[..., None])).astype(jnp.bfloat16)
    grad_query = (
        jnp.einsum("csl,clh->csh", grad_scores, keys, preferred_element_type=jnp.float32)
        * score_scale
    )
    grad_keys = (
        jnp.einsum("csl,csh->clh", grad_scores, query, preferred_element_type=jnp.float32)
        * score_scale
    )
    grad_values = jnp.einsum(
        "csl,csh->clh", probs.astype(jnp.bfloat16), grad_att, preferred_element_type=jnp.float32
    )
    return (grad_query, centre, grad_keys, grad_values)


def shards(
    hidden,
    teacher,
    text,
    time_embed,
    lengths,
    positions,
    modulation,
    self_in,
    self_bias,
    self_out,
    norm_gains,
    cross_gain,
    cross_shift,
    cross_q,
    cross_kv,
    cross_bias,
    cross_out,
    ffn_in,
    ffn_in_bias,
    ffn_out,
    out_bias,
):
    low_type = jnp.bfloat16
    wide_type = jnp.float32
    clip_count, seq_rows, model_width = hidden.shape
    local_width = self_in.shape[2]
    local_heads = local_width // HEAD_DIM
    text_local = text.shape[1]
    seq_count = lax.axis_size("seq")
    slot_count = seq_rows * seq_count
    text_count = text_local * seq_count
    flat_rows = clip_count * seq_rows
    score_scale = 1.0 / math.sqrt(HEAD_DIM)
    seq_place = lax.axis_index("seq")
    clip_first = lax.axis_index("dp") * clip_count
    clip_lengths = lax.dynamic_slice_in_dim(lengths, clip_first, clip_count)
    key_valid = jnp.arange(slot_count, dtype=jnp.int32)[None, :] < clip_lengths[:, None]
    row_ids = seq_place * seq_rows + jnp.arange(seq_rows, dtype=jnp.int32)
    row_valid = row_ids[None, :] < clip_lengths[:, None]
    text_valid = jnp.ones((clip_count, text_count), dtype=jnp.bool_)
    valid_total = jnp.sum(lengths).astype(wide_type)
    modulated = modulation[None] + time_embed
    cosine_rep, sine_rep = rope_tables(positions, HEAD_DIM)
    rotate_now = functools.partial(
        rotate, cosine_rep=cosine_rep, sine_rep=sine_rep, swap_matrix=swap_table(HEAD_DIM)
    )
    head_shape = (clip_count, seq_rows, local_heads, HEAD_DIM)
    clip_ids = jnp.arange(flat_rows, dtype=jnp.int32) // seq_rows
    clip_table = (clip_ids[:, None] == jnp.arange(clip_count, dtype=jnp.int32)[None, :]).astype(
        wide_type
    )
    valid_rows = row_valid.reshape(flat_rows)
    hidden_rows = hidden.reshape(flat_rows, model_width)
    teacher_rows = teacher.reshape(flat_rows, model_width)

    def per_row(index_no):
        return jnp.dot(clip_table, modulated[:, index_no], precision=lax.Precision.HIGHEST)

    def per_clip(values):
        return jnp.dot(clip_table.T, values, precision=lax.Precision.HIGHEST)

    scale_one = per_row(1)
    gate_one = per_row(2)
    scale_two = per_row(4)
    gate_two = per_row(5)
    normed_one = layer_norm(hidden_rows)
    attn_in = (normed_one * (1.0 + scale_one) + per_row(0)).astype(low_type)
    projected = (
        jnp.einsum("rd,kde->kre", attn_in, self_in, preferred_element_type=wide_type)
        + self_bias[:, None, :]
    )
    query_pre = projected[0]
    key_pre = projected[1]
    value_pre = projected[2]
    query_sq, key_sq = tensor_pair(
        jnp.sum(query_pre * query_pre, axis=-1), jnp.sum(key_pre * key_pre, axis=-1)
    )
    query_rate = lax.rsqrt(query_sq / model_width + eps_norm)[:, None]
    key_rate = lax.rsqrt(key_sq / model_width + eps_norm)[:, None]
    query_norm = (query_pre * query_rate * norm_gains[0]).reshape(head_shape)
    key_norm = (key_pre * key_rate * norm_gains[1]).reshape(head_shape)
    query_low = rotate_now(query_norm).astype(low_type)
    key_low = rotate_now(key_norm).astype(low_type)
    value_low = value_pre.astype(low_type).reshape(head_shape)
    local_kv = jnp.stack(
        [
            key_low.reshape(clip_count, seq_rows, local_width),
            value_low.reshape(clip_count, seq_rows, local_width),
        ]
    )
    whole_kv = lax.all_gather(local_kv, "seq", axis=2, tiled=True)
    keys_all = whole_kv[0].reshape(clip_count, slot_count, local_heads, HEAD_DIM)
    values_all = whole_kv[1].reshape(clip_count, slot_count, local_heads, HEAD_DIM)
    att_heads = []
    total_heads = []
    for head_no in range(local_heads):
        attended, log_total = head_forward(
            query_low[:, :, head_no],
            keys_all[:, :, head_no],
            values_all[:, :, head_no],
            key_valid,
            score_scale,
        )
        att_heads.append(attended)
        total_heads.append(log_total)
    attn_low = jnp.stack(att_heads, axis=2).astype(low_type).reshape(flat_rows, local_width)
    self_totals = jnp.stack(total_heads)
    branch_one = (
        stream_sum(jnp.dot(attn_low, self_out, preferred_element_type=wide_type)) + out_bias[0]
    )
    after_one = hidden_rows + branch_one * gate_one
    normed_three = layer_norm(after_one)
    cross_in = (normed_three * cross_gain + cross_shift).astype(low_type)
    cross_query_pre = jnp.dot(cross_in, cross_q, preferred_element_type=wide_type) + cross_bias[0]
    text_low = text.astype(low_type)
    text_start = seq_place * text_local
    text_all = lax.all_gather(text_low, "seq", axis=1, tiled=True)
    text_proj = (
        jnp.einsum("ctd,kde->kcte", text_all, cross_kv, preferred_element_type=wide_type)
        + cross_bias[1:, None, None, :]
    )
    cross_sq, text_sq = tensor_pair(
        jnp.sum(cross_query_pre * cross_query_pre, axis=-1),
        jnp.sum(text_proj[0] * text_proj[0], axis=-1),
    )
    text_rate_all = lax.rsqrt(text_sq / model_width + eps_norm)[..., None]
    text_key_low = (text_proj[0] * text_rate_all * norm_gains[3]).astype(low_type)
    text_value_low = text_proj[1].astype(low_type)
    text_key_pre = lax.dynamic_slice_in_dim(text_proj[0], text_start, text_local, 1)
    text_key_rate = lax.dynamic_slice_in_dim(text_rate_all, text_start, text_local, 1)
    cross_rate = lax.rsqrt(cross_sq / model_width + eps_norm)[:, None]
    cross_query_low = (
        (cross_query_pre * cross_rate * norm_gains[2]).astype(low_type).reshape(head_shape)
    )
    text_key_heads = text_key_low.reshape(clip_count, text_count, local_heads, HEAD_DIM)
    text_value_heads = text_value_low.reshape(clip_count, text_count, local_heads, HEAD_DIM)
    cross_heads = []
    cross_total_heads = []
    for head_no in range(local_heads):
        attended, log_total = head_forward(
            cross_query_low[:, :, head_no],
            text_key_heads[:, :, head_no],
            text_value_heads[:, :, head_no],
            text_valid,
            score_scale,
        )
        cross_heads.append(attended)
        cross_total_heads.append(log_total)
    cross_att_low = jnp.stack(cross_heads, axis=2).astype(low_type).reshape(flat_rows, local_width)
    cross_totals = jnp.stack(cross_total_heads)
    branch_two = (
        stream_sum(jnp.dot(cross_att_low, cross_out, preferred_element_type=wide_type))
        + out_bias[1]
    )
    after_two = after_one + branch_two
    normed_two = layer_norm(after_two)
    ffn_input = (normed_two * (1.0 + scale_two) + per_row(3)).astype(low_type)
    pre_act = jnp.dot(ffn_input, ffn_in, preferred_element_type=wide_type) + ffn_in_bias
    act_low = gelu_tanh(pre_act).astype(low_type)
    branch_three = (
        stream_sum(jnp.dot(act_low, ffn_out, preferred_element_type=wide_type)) + out_bias[2]
    )
    result = after_two + branch_three * gate_two
    residue = jnp.where(valid_rows[:, None], result - teacher_rows, 0.0)
    grad_three = residue * gate_two
    grad_three_low = grad_three.astype(low_type)
    grad_ffn_out = jnp.dot(act_low.T, grad_three_low, preferred_element_type=wide_type)
    grad_act = jnp.dot(grad_three_low, ffn_out.T, preferred_element_type=wide_type)
    grad_pre = jax.vjp(gelu_tanh, pre_act)[1](grad_act)[0]
    grad_pre_low = grad_pre.astype(low_type)
    grad_ffn_in = jnp.dot(ffn_input.T, grad_pre_low, preferred_element_type=wide_type)
    grad_ffn_bias = jnp.sum(grad_pre, axis=0)
    grad_ffn_input = stream_sum(jnp.dot(grad_pre_low, ffn_in.T, preferred_element_type=wide_type))
    grad_after_two = (
        residue + jax.vjp(layer_norm, after_two)[1](grad_ffn_input * (1.0 + scale_two))[0]
    )
    grad_two_low = grad_after_two.astype(low_type)
    grad_cross_out = jnp.dot(cross_att_low.T, grad_two_low, preferred_element_type=wide_type)
    grad_cross_att = (
        jnp.dot(grad_two_low, cross_out.T, preferred_element_type=wide_type)
        .astype(low_type)
        .reshape(head_shape)
    )
    cross_query_grads = []
    text_key_grads = []
    text_value_grads = []
    for head_no in range(local_heads):
        head_grads = head_backward(
            cross_query_low[:, :, head_no],
            text_key_heads[:, :, head_no],
            text_value_heads[:, :, head_no],
            text_valid,
            cross_totals[head_no],
            grad_cross_att[:, :, head_no],
            score_scale,
        )
        cross_query_grads.append(head_grads[0])
        text_key_grads.append(head_grads[2])
        text_value_grads.append(head_grads[3])
    grad_cross_query = jnp.stack(cross_query_grads, axis=2).reshape(flat_rows, local_width)
    text_grads_all = jnp.stack(
        [
            jnp.stack(text_key_grads, axis=2).reshape(clip_count, text_count, local_width),
            jnp.stack(text_value_grads, axis=2).reshape(clip_count, text_count, local_width),
        ]
    )
    text_grads = lax.psum_scatter(
        text_grads_all.astype(jnp.bfloat16), "seq", scatter_dimension=2, tiled=True
    ).astype(jnp.float32)
    query_term, key_term = tensor_pair(
        jnp.sum(grad_cross_query * norm_gains[2] * cross_query_pre, axis=-1),
        jnp.sum(text_grads[0] * norm_gains[3] * text_key_pre, axis=-1),
    )
    grad_cross_query_pre = (
        grad_cross_query * norm_gains[2] * cross_rate
        - cross_query_pre * cross_rate**3 * query_term[:, None] / model_width
    )
    grad_text_key_pre = (
        text_grads[0] * norm_gains[3] * text_key_rate
        - text_key_pre * text_key_rate**3 * key_term[..., None] / model_width
    )
    gain_cross_query = jnp.sum(grad_cross_query * cross_query_pre * cross_rate, axis=0)
    gain_text_key = jnp.sum(text_grads[0] * text_key_pre * text_key_rate, axis=(0, 1))
    grad_cross_bias = jnp.stack(
        [
            jnp.sum(grad_cross_query_pre, axis=0),
            jnp.sum(grad_text_key_pre, axis=(0, 1)),
            jnp.sum(text_grads[1], axis=(0, 1)),
        ]
    )
    grad_cross_query_low = grad_cross_query_pre.astype(low_type)
    text_grad_low = jnp.stack([grad_text_key_pre, text_grads[1]]).astype(low_type)
    grad_cross_q = jnp.dot(cross_in.T, grad_cross_query_low, preferred_element_type=wide_type)
    grad_cross_kv = jnp.einsum(
        "ctd,kcte->kde", text_low, text_grad_low, preferred_element_type=wide_type
    )
    grad_text = lax.psum(
        jnp.einsum(
            "kcte,kde->ctd", text_grad_low, cross_kv, preferred_element_type=wide_type
        ).astype(jnp.bfloat16),
        "tensor",
    ).astype(jnp.float32)
    grad_cross_in = stream_sum(
        jnp.dot(grad_cross_query_low, cross_q.T, preferred_element_type=wide_type)
    )
    grad_cross_gain = jnp.sum(grad_cross_in * normed_three, axis=0)
    grad_cross_shift = jnp.sum(grad_cross_in, axis=0)
    grad_after_one = (
        grad_after_two + jax.vjp(layer_norm, after_one)[1](grad_cross_in * cross_gain)[0]
    )
    grad_one = grad_after_one * gate_one
    grad_one_low = grad_one.astype(low_type)
    grad_self_out = jnp.dot(attn_low.T, grad_one_low, preferred_element_type=wide_type)
    grad_attn = (
        jnp.dot(grad_one_low, self_out.T, preferred_element_type=wide_type)
        .astype(low_type)
        .reshape(head_shape)
    )
    query_grads = []
    key_grads = []
    value_grads = []
    for head_no in range(local_heads):
        head_grads = head_backward(
            query_low[:, :, head_no],
            keys_all[:, :, head_no],
            values_all[:, :, head_no],
            key_valid,
            self_totals[head_no],
            grad_attn[:, :, head_no],
            score_scale,
        )
        query_grads.append(head_grads[0])
        key_grads.append(head_grads[2])
        value_grads.append(head_grads[3])
    owner_grads = [
        jnp.stack(parts, axis=2)
        .astype(jnp.bfloat16)
        .reshape(clip_count, seq_count, seq_rows, local_width)
        for parts in (key_grads, value_grads)
    ]
    owner_grads = jnp.concatenate(
        [
            jnp.swapaxes(part, 0, 1).reshape(seq_count, flat_rows, local_width)
            for part in owner_grads
        ],
        axis=-1,
    )
    pad_rows = -flat_rows % 16
    owner_grads = jnp.pad(owner_grads, ((0, 0), (0, pad_rows), (0, 0)))
    kv_rows = lax.psum_scatter(
        owner_grads.reshape(seq_count * (flat_rows + pad_rows), 2 * local_width),
        "seq",
        scatter_dimension=0,
        tiled=True,
    )[:flat_rows].astype(jnp.float32)
    kv_grads = (kv_rows[:, :local_width], kv_rows[:, local_width:])
    rotate_back = jax.vjp(rotate_now, query_norm)[1]
    grad_query_norm = rotate_back(jnp.stack(query_grads, axis=2))[0].reshape(flat_rows, local_width)
    grad_key_norm = rotate_back(kv_grads[0].reshape(head_shape))[0].reshape(flat_rows, local_width)
    query_back, key_back = tensor_pair(
        jnp.sum(grad_query_norm * norm_gains[0] * query_pre, axis=-1),
        jnp.sum(grad_key_norm * norm_gains[1] * key_pre, axis=-1),
    )
    grad_query_pre = (
        grad_query_norm * norm_gains[0] * query_rate
        - query_pre * query_rate**3 * query_back[:, None] / model_width
    )
    grad_key_pre = (
        grad_key_norm * norm_gains[1] * key_rate
        - key_pre * key_rate**3 * key_back[:, None] / model_width
    )
    gain_query = jnp.sum(grad_query_norm * query_pre * query_rate, axis=0)
    gain_key = jnp.sum(grad_key_norm * key_pre * key_rate, axis=0)
    grad_proj = jnp.stack(
        [grad_query_pre, grad_key_pre, kv_grads[1].reshape(flat_rows, local_width)]
    )
    grad_self_bias = jnp.sum(grad_proj, axis=1)
    grad_proj_low = grad_proj.astype(low_type)
    grad_self_in = jnp.einsum(
        "rd,kre->kde", attn_in, grad_proj_low, preferred_element_type=wide_type
    )
    grad_attn_in = stream_sum(
        jnp.einsum("kre,kde->rd", grad_proj_low, self_in, preferred_element_type=wide_type)
    )
    grad_hidden = (
        grad_after_one + jax.vjp(layer_norm, hidden_rows)[1](grad_attn_in * (1.0 + scale_one))[0]
    )
    grad_time_local = jnp.stack(
        [
            per_clip(grad_attn_in),
            per_clip(grad_attn_in * normed_one),
            per_clip(grad_after_one * branch_one),
            per_clip(grad_ffn_input),
            per_clip(grad_ffn_input * normed_two),
            per_clip(residue * branch_three),
        ],
        axis=1,
    )
    grad_out_bias = jnp.stack(
        [jnp.sum(grad_one, axis=0), jnp.sum(grad_after_two, axis=0), jnp.sum(grad_three, axis=0)]
    )
    stream_values = (
        grad_time_local,
        grad_cross_gain,
        grad_cross_shift,
        grad_out_bias,
        jnp.sum(residue * residue),
    )
    grad_time_local, grad_cross_gain, grad_cross_shift, grad_out_bias, square_local = stream_values
    grad_time = lax.psum(grad_time_local.astype(jnp.bfloat16), "seq").astype(jnp.float32)
    grad_norm_gains = jnp.stack([gain_query, gain_key, gain_cross_query, gain_text_key])
    (
        sum_self_bias,
        sum_gains,
        sum_cross_gain,
        sum_cross_shift,
        sum_cross_bias,
        sum_ffn_bias,
        sum_out_bias,
        sum_modulation,
        square_sum,
    ) = (
        lax.psum(grad_self_bias.astype(jnp.bfloat16), ("dp", "seq")).astype(jnp.float32),
        lax.psum(grad_norm_gains.astype(jnp.bfloat16), ("dp", "seq")).astype(jnp.float32),
        lax.psum(grad_cross_gain.astype(jnp.bfloat16), ("dp", "seq")).astype(jnp.float32),
        lax.psum(grad_cross_shift.astype(jnp.bfloat16), ("dp", "seq")).astype(jnp.float32),
        lax.psum(grad_cross_bias.astype(jnp.bfloat16), ("dp", "seq")).astype(jnp.float32),
        lax.psum(grad_ffn_bias.astype(jnp.bfloat16), ("dp", "seq")).astype(jnp.float32),
        lax.psum(grad_out_bias.astype(jnp.bfloat16), ("dp", "seq")).astype(jnp.float32),
        lax.psum(jnp.sum(grad_time_local, axis=0).astype(jnp.bfloat16), ("dp", "seq")).astype(
            jnp.float32
        ),
        lax.psum(square_local.astype(jnp.bfloat16), ("dp", "seq")).astype(jnp.float32),
    )
    loss = square_sum / (valid_total * model_width)
    (
        part_self_in,
        part_self_out,
        part_cross_q,
        part_cross_kv,
        part_cross_out,
        part_ffn_in,
        part_ffn_out,
    ) = (
        lax.psum_scatter(
            grad_self_in.astype(jnp.bfloat16), ("dp", "seq"), scatter_dimension=1, tiled=True
        ).astype(jnp.float32),
        lax.psum_scatter(
            grad_self_out.astype(jnp.bfloat16), ("dp", "seq"), scatter_dimension=1, tiled=True
        ).astype(jnp.float32),
        lax.psum_scatter(
            grad_cross_q.astype(jnp.bfloat16), ("dp", "seq"), scatter_dimension=0, tiled=True
        ).astype(jnp.float32),
        lax.psum_scatter(
            jnp.concatenate([grad_cross_kv[0], grad_cross_kv[1]], axis=-1).astype(jnp.bfloat16),
            ("dp", "seq"),
            scatter_dimension=0,
            tiled=True,
        ).astype(jnp.float32),
        lax.psum_scatter(
            grad_cross_out.astype(jnp.bfloat16), ("dp", "seq"), scatter_dimension=1, tiled=True
        ).astype(jnp.float32),
        lax.psum_scatter(
            grad_ffn_in.astype(jnp.bfloat16), ("dp", "seq"), scatter_dimension=0, tiled=True
        ).astype(jnp.float32),
        lax.psum_scatter(
            grad_ffn_out.astype(jnp.bfloat16), ("dp", "seq"), scatter_dimension=1, tiled=True
        ).astype(jnp.float32),
    )
    part_cross_kv = jnp.stack([part_cross_kv[:, :local_width], part_cross_kv[:, local_width:]])
    result_out = result.reshape(clip_count, seq_rows, model_width)
    grad_hidden_out = grad_hidden.reshape(clip_count, seq_rows, model_width)
    return (
        result_out,
        loss,
        grad_hidden_out,
        grad_text,
        grad_time,
        sum_modulation,
        part_self_in,
        sum_self_bias,
        part_self_out,
        sum_gains,
        sum_cross_gain,
        sum_cross_shift,
        part_cross_q,
        part_cross_kv,
        sum_cross_bias,
        part_cross_out,
        part_ffn_in,
        sum_ffn_bias,
        part_ffn_out,
        sum_out_bias,
    )


def solution(mesh):
    placed = (
        P("dp", "seq", None),
        P("dp", "seq", None),
        P("dp", "seq", None),
        P("dp", None, None),
        P(),
        P(None, "dp", "seq"),
        P(),
        P(None, None, "tensor"),
        P(None, "tensor"),
        P("tensor", None),
        P(None, "tensor"),
        P(),
        P(),
        P(None, "tensor"),
        P(None, None, "tensor"),
        P(None, "tensor"),
        P("tensor", None),
        P(None, "tensor"),
        P("tensor"),
        P("tensor", None),
        P(),
    )
    return jax.shard_map(
        shards,
        mesh=mesh,
        in_specs=placed,
        out_specs=(
            P("dp", "seq", None),
            P(),
            P("dp", "seq", None),
            P("dp", "seq", None),
            P("dp", None, None),
            P(),
            P(None, ("dp", "seq"), "tensor"),
            P(None, "tensor"),
            P("tensor", ("dp", "seq")),
            P(None, "tensor"),
            P(),
            P(),
            P(("dp", "seq"), "tensor"),
            P(None, ("dp", "seq"), "tensor"),
            P(None, "tensor"),
            P("tensor", ("dp", "seq")),
            P(("dp", "seq"), "tensor"),
            P("tensor"),
            P("tensor", ("dp", "seq")),
            P(),
        ),
        check_vma=False,
    )
```

```python
import functools
import math

import jax
import jax.numpy as jnp
from jax import lax
from jax.experimental import pallas as pl
from jax.experimental.pallas import tpu as pltpu
from jax.sharding import PartitionSpec as P

HEAD_DIM = 128
LOW = jnp.bfloat16
WIDE = jnp.float32


eps_norm = 1e-06


def layer_norm(values):
    centred = values - jnp.mean(values, axis=-1, keepdims=True)
    return centred * lax.rsqrt(jnp.mean(centred * centred, axis=-1, keepdims=True) + eps_norm)


def gelu_tanh(values):
    return (
        0.5
        * values
        * (1.0 + jnp.tanh(0.7978845608028654 * (values + 0.044715 * values * values * values)))
    )


def rope_tables(positions, head_size):
    sixth_part = head_size // 6
    part_spans = (head_size - 4 * sixth_part, 2 * sixth_part, 2 * sixth_part)
    pieces = []
    for axis_no in range(3):
        span_now = part_spans[axis_no]
        inverse = 1.0 / 10000.0 ** (jnp.arange(0, span_now, 2).astype(jnp.float32) / span_now)
        pieces.append(positions[axis_no].astype(jnp.float32)[..., None] * inverse)
    angles = jnp.concatenate(pieces, axis=-1)
    cosine_rep = jnp.repeat(jnp.cos(angles), 2, axis=-1)[..., None, :]
    sine_rep = jnp.repeat(jnp.sin(angles), 2, axis=-1)[..., None, :]
    return (cosine_rep, sine_rep)


def swap_table(head_size):
    row_no = jnp.arange(head_size)[:, None]
    col_no = jnp.arange(head_size)[None, :]
    upward = jnp.where((row_no % 2 == 0) & (col_no == row_no + 1), 1.0, 0.0)
    downward = jnp.where((row_no % 2 == 1) & (col_no == row_no - 1), -1.0, 0.0)
    return (upward + downward).astype(jnp.float32)


def rotate(values, cosine_rep, sine_rep, swap_matrix):
    swapped = jnp.matmul(values, swap_matrix, precision=lax.Precision.HIGHEST)
    return values * cosine_rep + swapped * sine_rep


def line_kernel(count, block, group, lag, lag2, turned, *refs):
    lhs_refs = refs[:count]
    rhs_refs = refs[count:2 * count]
    out_ref, raw, part, stage, cross, raw_s, raw_r, mid_s, mid_r, far_s, far_r, near_s, near_r = refs[2 * count:]
    steps = out_ref.shape[0] // block
    me = lax.axis_index("tensor")
    inner = (me == 1) | (me == 2)
    outer = jnp.logical_not(inner)
    leaf = jnp.where(me < 2, 0, 3)
    hub = jnp.where(me < 2, 1, 2)
    mate = 3 - me
    side = jnp.where(me < 2, 0, 1)

    def signal(where):
        pl.semaphore_signal(
            pltpu.get_barrier_semaphore(), inc=1, device_id={"tensor": where},
            device_id_type=pl.DeviceIdType.MESH)

    @pl.when(outer)
    def _():
        signal(hub)
        pl.semaphore_wait(pltpu.get_barrier_semaphore(), 1)

    @pl.when(inner)
    def _():
        signal(leaf)
        signal(mate)
        pl.semaphore_wait(pltpu.get_barrier_semaphore(), 2)

    def rows_of(step):
        return pl.ds(pl.multiple_of(step * block, 16), block)

    def remote(src, dst, send, recv, step, where):
        at = rows_of(step)
        return pltpu.make_async_remote_copy(
            src_ref=src.at[at], dst_ref=dst.at[at], send_sem=send.at[step], recv_sem=recv.at[step],
            device_id={"tensor": where}, device_id_type=pl.DeviceIdType.MESH)

    def raw_copy(step):
        return remote(raw, raw, raw_s, raw_r, step, hub)

    def mid_copy(step):
        return remote(stage, cross, mid_s, mid_r, step, mate)

    def far_copy(step):
        return remote(out_ref, out_ref, far_s, far_r, step, mate)

    def near_copy(step):
        return remote(out_ref, out_ref, near_s, near_r, step, leaf)

    def body(step, carry):
        @pl.when((step < steps) & (lax.rem(step, group) == 0))
        def _():
            at = pl.ds(pl.multiple_of(step * block, 16), block * group)
            total = None
            for lhs, rhs in zip(lhs_refs, rhs_refs):
                term = lax.dot_general(lhs[at], rhs[...], (((1,), (1 if turned else 0,)), ((), ())),
                    preferred_element_type=WIDE)
                total = term if total is None else total + term
            part[at] = total

        @pl.when(outer & (step < steps))
        def _():
            at = rows_of(step)
            raw[at] = part[at].astype(LOW)
            raw_copy(step).start()

        late = step - lag2
        @pl.when(inner & (late >= 0) & (late < steps) & (lax.rem(late + 2 * lag2, 2) != side))
        def _():
            far_copy(late).wait_recv()
            near_copy(late).start()

        near = step - lag
        @pl.when(inner & (near >= 0) & (near < steps) & (lax.rem(near + 2 * lag2, 2) == side))
        def _():
            at = rows_of(near)
            mid_copy(near).wait_recv()
            out_ref[at] = (part[at] + cross[at].astype(WIDE)).astype(LOW)
            far_copy(near).start()
            near_copy(near).start()

        @pl.when(inner & (step < steps))
        def _():
            at = rows_of(step)
            raw_copy(step).wait_recv()

            @pl.when(lax.rem(step, 2) == side)
            def _():
                part[at] = part[at] + raw[at].astype(WIDE)

            @pl.when(lax.rem(step, 2) != side)
            def _():
                stage[at] = (part[at] + raw[at].astype(WIDE)).astype(LOW)
                mid_copy(step).start()

        return carry

    lax.fori_loop(0, steps + lag2, body, 0)

    def drain(step, carry):
        @pl.when(outer)
        def _():
            near_copy(step).wait_recv()
            raw_copy(step).wait_send()

        @pl.when(inner)
        def _():
            near_copy(step).wait_send()

            @pl.when(lax.rem(step, 2) == side)
            def _():
                far_copy(step).wait_send()

            @pl.when(lax.rem(step, 2) != side)
            def _():
                mid_copy(step).wait_send()

        return carry

    lax.fori_loop(0, steps, drain, 0)

def line_sum(pairs, turned, ident, block=32, group=5, lag=3, lag2=6):
    true_rows = pairs[0][0].shape[0]
    width = pairs[0][1].shape[0 if turned else 1]
    unit = block * group
    rows = -(-true_rows // unit) * unit
    pairs = [(jnp.pad(lhs, ((0, rows - true_rows), (0, 0))), rhs) for lhs, rhs in pairs]
    steps = rows // block
    dma = pltpu.SemaphoreType.DMA
    depth = sum(p[0].shape[1] for p in pairs)
    return pl.pallas_call(
        functools.partial(line_kernel, len(pairs), block, group, lag, lag2, turned),
        out_shape=jax.ShapeDtypeStruct((rows, width), LOW),
        in_specs=[pl.BlockSpec(memory_space=pltpu.VMEM)] * (2 * len(pairs)),
        out_specs=pl.BlockSpec(memory_space=pltpu.VMEM),
        scratch_shapes=[
            pltpu.VMEM((rows, width), LOW),
            pltpu.VMEM((rows, width), WIDE),
            pltpu.VMEM((rows, width), LOW),
            pltpu.VMEM((rows, width), LOW),
        ] + [dma((steps,))] * 8,
        compiler_params=pltpu.CompilerParams(collective_id=ident, has_side_effects=True, vmem_limit_bytes=60 << 20),
        cost_estimate=pl.CostEstimate(flops=2 * rows * width * depth, bytes_accessed=2*(rows*depth+width*depth+rows*width), transcendentals=0),
        name=f"line_sum_{ident}",
    )(*[p[0] for p in pairs], *[p[1] for p in pairs])[:true_rows].astype(WIDE)

def small_kernel(value_ref, out_ref, slots, send_sem, recv_sem):
    count = slots.shape[0]
    me = lax.axis_index("tensor")
    barrier = pltpu.get_barrier_semaphore()
    for hop in range(1, count):
        pl.semaphore_signal(
            barrier, inc=1, device_id={"tensor": lax.rem(me + hop, count)},
            device_id_type=pl.DeviceIdType.MESH)
    pl.semaphore_wait(barrier, count - 1)
    copies = []
    for hop in range(1, count):
        copy = pltpu.make_async_remote_copy(
            src_ref=value_ref, dst_ref=slots.at[me], send_sem=send_sem.at[hop - 1],
            recv_sem=recv_sem.at[hop - 1], device_id={"tensor": lax.rem(me + hop, count)},
            device_id_type=pl.DeviceIdType.MESH)
        copy.start()
        copies.append(copy)
    slots[pl.ds(me, 1)] = value_ref[...][None]
    for hop in range(1, count):
        origin = lax.rem(me + count - hop, count)
        pltpu.make_async_remote_copy(
            src_ref=value_ref, dst_ref=slots.at[origin], send_sem=send_sem.at[hop - 1],
            recv_sem=recv_sem.at[hop - 1], device_id={"tensor": origin},
            device_id_type=pl.DeviceIdType.MESH).wait_recv()
    for copy in copies:
        copy.wait_send()
    total = slots[0]
    for slot in range(1, count):
        total = total + slots[slot]
    out_ref[...] = total


def small_sum(values, ident):
    count = lax.axis_size("tensor")
    flat = jnp.concatenate([value.reshape(-1) for value in values])
    size = flat.shape[0]
    lines = -(-size // 1024) * 8
    packed = jnp.pad(flat, (0, lines * 128 - size)).reshape(lines, 128)
    summed = pl.pallas_call(
        small_kernel,
        out_shape=jax.ShapeDtypeStruct((lines, 128), WIDE),
        in_specs=[pl.BlockSpec(memory_space=pltpu.VMEM)],
        out_specs=pl.BlockSpec(memory_space=pltpu.VMEM),
        scratch_shapes=[
            pltpu.VMEM((count, lines, 128), WIDE),
            pltpu.SemaphoreType.DMA((count - 1,)),
            pltpu.SemaphoreType.DMA((count - 1,)),
        ],
        compiler_params=pltpu.CompilerParams(collective_id=ident, has_side_effects=True),
        name=f"small_sum_{ident}",
    )(packed).reshape(-1)
    outs = []
    start = 0
    for value in values:
        outs.append(summed[start : start + value.size].reshape(value.shape))
        start += value.size
    return outs


def head_forward(query, keys, values, key_ok, score_scale):
    scores = (
        jnp.einsum("csh,clh->csl", query, keys, preferred_element_type=jnp.float32) * score_scale
    )
    scores = jnp.where(key_ok[:, None, :], scores, -jnp.inf)
    row_peak = jnp.max(scores, axis=-1, keepdims=True)
    exp_terms = jnp.exp(scores - row_peak)
    summed = jnp.sum(exp_terms, axis=-1, keepdims=True)
    probs_low = (exp_terms / summed).astype(jnp.bfloat16)
    attended = jnp.einsum("csl,clh->csh", probs_low, values, preferred_element_type=jnp.float32)
    return (attended, row_peak[..., 0] + jnp.log(summed[..., 0]))


def head_backward(query, keys, values, key_ok, log_total, grad_att, score_scale):
    scores = (
        jnp.einsum("csh,clh->csl", query, keys, preferred_element_type=jnp.float32) * score_scale
    )
    probs = jnp.where(key_ok[:, None, :], jnp.exp(scores - log_total[..., None]), 0.0)
    grad_probs = jnp.einsum("csh,clh->csl", grad_att, values, preferred_element_type=jnp.float32)
    centre = jnp.sum(probs * grad_probs, axis=-1)
    grad_scores = (probs * (grad_probs - centre[..., None])).astype(jnp.bfloat16)
    grad_query = (
        jnp.einsum("csl,clh->csh", grad_scores, keys, preferred_element_type=jnp.float32)
        * score_scale
    )
    grad_keys = (
        jnp.einsum("csl,csh->clh", grad_scores, query, preferred_element_type=jnp.float32)
        * score_scale
    )
    grad_values = jnp.einsum(
        "csl,csh->clh", probs.astype(jnp.bfloat16), grad_att, preferred_element_type=jnp.float32
    )
    return (grad_query, centre, grad_keys, grad_values)


def shards(
    hidden,
    teacher,
    text,
    time_embed,
    lengths,
    positions,
    modulation,
    self_in,
    self_bias,
    self_out,
    norm_gains,
    cross_gain,
    cross_shift,
    cross_q,
    cross_kv,
    cross_bias,
    cross_out,
    ffn_in,
    ffn_in_bias,
    ffn_out,
    out_bias,
):
    low_type = jnp.bfloat16
    wide_type = jnp.float32
    clip_count, seq_rows, model_width = hidden.shape
    local_width = self_in.shape[2]
    local_heads = local_width // HEAD_DIM
    text_local = text.shape[1]
    seq_count = lax.axis_size("seq")
    slot_count = seq_rows * seq_count
    text_count = text_local * seq_count
    flat_rows = clip_count * seq_rows
    score_scale = 1.0 / math.sqrt(HEAD_DIM)
    seq_place = lax.axis_index("seq")
    clip_first = lax.axis_index("dp") * clip_count
    clip_lengths = lax.dynamic_slice_in_dim(lengths, clip_first, clip_count)
    key_valid = jnp.arange(slot_count, dtype=jnp.int32)[None, :] < clip_lengths[:, None]
    row_ids = seq_place * seq_rows + jnp.arange(seq_rows, dtype=jnp.int32)
    row_valid = row_ids[None, :] < clip_lengths[:, None]
    text_valid = jnp.ones((clip_count, text_count), dtype=jnp.bool_)
    valid_total = jnp.sum(lengths).astype(wide_type)
    modulated = modulation[None] + time_embed
    cosine_rep, sine_rep = rope_tables(positions, HEAD_DIM)
    rotate_now = functools.partial(
        rotate, cosine_rep=cosine_rep, sine_rep=sine_rep, swap_matrix=swap_table(HEAD_DIM)
    )
    head_shape = (clip_count, seq_rows, local_heads, HEAD_DIM)
    clip_ids = jnp.arange(flat_rows, dtype=jnp.int32) // seq_rows
    clip_table = (clip_ids[:, None] == jnp.arange(clip_count, dtype=jnp.int32)[None, :]).astype(
        wide_type
    )
    valid_rows = row_valid.reshape(flat_rows)
    hidden_rows = hidden.reshape(flat_rows, model_width)
    teacher_rows = teacher.reshape(flat_rows, model_width)

    def per_row(index_no):
        return jnp.dot(clip_table, modulated[:, index_no], precision=lax.Precision.HIGHEST)

    def per_clip(values):
        return jnp.dot(clip_table.T, values, precision=lax.Precision.HIGHEST)

    scale_one = per_row(1)
    gate_one = per_row(2)
    scale_two = per_row(4)
    gate_two = per_row(5)
    normed_one = layer_norm(hidden_rows)
    attn_in = (normed_one * (1.0 + scale_one) + per_row(0)).astype(low_type)
    projected = (
        jnp.einsum("rd,kde->kre", attn_in, self_in, preferred_element_type=wide_type)
        + self_bias[:, None, :]
    )
    query_pre = projected[0]
    key_pre = projected[1]
    value_pre = projected[2]
    query_sq, key_sq = small_sum(
        [jnp.sum(query_pre * query_pre, axis=-1), jnp.sum(key_pre * key_pre, axis=-1)], 6
    )
    query_rate = lax.rsqrt(query_sq / model_width + eps_norm)[:, None]
    key_rate = lax.rsqrt(key_sq / model_width + eps_norm)[:, None]
    query_norm = (query_pre * query_rate * norm_gains[0]).reshape(head_shape)
    key_norm = (key_pre * key_rate * norm_gains[1]).reshape(head_shape)
    query_low = rotate_now(query_norm).astype(low_type)
    key_low = rotate_now(key_norm).astype(low_type)
    value_low = value_pre.astype(low_type).reshape(head_shape)
    local_kv = jnp.stack(
        [
            key_low.reshape(clip_count, seq_rows, local_width),
            value_low.reshape(clip_count, seq_rows, local_width),
        ]
    )
    whole_kv = lax.all_gather(local_kv, "seq", axis=2, tiled=True)
    keys_all = whole_kv[0].reshape(clip_count, slot_count, local_heads, HEAD_DIM)
    values_all = whole_kv[1].reshape(clip_count, slot_count, local_heads, HEAD_DIM)
    att_heads = []
    total_heads = []
    for head_no in range(local_heads):
        attended, log_total = head_forward(
            query_low[:, :, head_no],
            keys_all[:, :, head_no],
            values_all[:, :, head_no],
            key_valid,
            score_scale,
        )
        att_heads.append(attended)
        total_heads.append(log_total)
    attn_low = jnp.stack(att_heads, axis=2).astype(low_type).reshape(flat_rows, local_width)
    self_totals = jnp.stack(total_heads)
    branch_one = (
        line_sum([(attn_low, self_out)], False, 0) + out_bias[0]
    )
    after_one = hidden_rows + branch_one * gate_one
    normed_three = layer_norm(after_one)
    cross_in = (normed_three * cross_gain + cross_shift).astype(low_type)
    cross_query_pre = jnp.dot(cross_in, cross_q, preferred_element_type=wide_type) + cross_bias[0]
    text_low = text.astype(low_type)
    text_start = seq_place * text_local
    text_all = lax.all_gather(text_low, "seq", axis=1, tiled=True)
    text_proj = (
        jnp.einsum("ctd,kde->kcte", text_all, cross_kv, preferred_element_type=wide_type)
        + cross_bias[1:, None, None, :]
    )
    cross_sq, text_sq = small_sum(
        [
            jnp.sum(cross_query_pre * cross_query_pre, axis=-1),
            jnp.sum(text_proj[0] * text_proj[0], axis=-1),
        ],
        7,
    )
    text_rate_all = lax.rsqrt(text_sq / model_width + eps_norm)[..., None]
    text_key_low = (text_proj[0] * text_rate_all * norm_gains[3]).astype(low_type)
    text_value_low = text_proj[1].astype(low_type)
    text_key_pre = lax.dynamic_slice_in_dim(text_proj[0], text_start, text_local, 1)
    text_key_rate = lax.dynamic_slice_in_dim(text_rate_all, text_start, text_local, 1)
    cross_rate = lax.rsqrt(cross_sq / model_width + eps_norm)[:, None]
    cross_query_low = (
        (cross_query_pre * cross_rate * norm_gains[2]).astype(low_type).reshape(head_shape)
    )
    text_key_heads = text_key_low.reshape(clip_count, text_count, local_heads, HEAD_DIM)
    text_value_heads = text_value_low.reshape(clip_count, text_count, local_heads, HEAD_DIM)
    cross_heads = []
    cross_total_heads = []
    for head_no in range(local_heads):
        attended, log_total = head_forward(
            cross_query_low[:, :, head_no],
            text_key_heads[:, :, head_no],
            text_value_heads[:, :, head_no],
            text_valid,
            score_scale,
        )
        cross_heads.append(attended)
        cross_total_heads.append(log_total)
    cross_att_low = jnp.stack(cross_heads, axis=2).astype(low_type).reshape(flat_rows, local_width)
    cross_totals = jnp.stack(cross_total_heads)
    branch_two = (
        line_sum([(cross_att_low, cross_out)], False, 1)
        + out_bias[1]
    )
    after_two = after_one + branch_two
    normed_two = layer_norm(after_two)
    ffn_input = (normed_two * (1.0 + scale_two) + per_row(3)).astype(low_type)
    pre_act = jnp.dot(ffn_input, ffn_in, preferred_element_type=wide_type) + ffn_in_bias
    act_low = gelu_tanh(pre_act).astype(low_type)
    branch_three = (
        line_sum([(act_low, ffn_out)], False, 2) + out_bias[2]
    )
    result = after_two + branch_three * gate_two
    residue = jnp.where(valid_rows[:, None], result - teacher_rows, 0.0)
    grad_three = residue * gate_two
    grad_three_low = grad_three.astype(low_type)
    grad_ffn_out = jnp.dot(act_low.T, grad_three_low, preferred_element_type=wide_type)
    grad_act = jnp.dot(grad_three_low, ffn_out.T, preferred_element_type=wide_type)
    grad_pre = jax.vjp(gelu_tanh, pre_act)[1](grad_act)[0]
    grad_pre_low = grad_pre.astype(low_type)
    grad_ffn_in = jnp.dot(ffn_input.T, grad_pre_low, preferred_element_type=wide_type)
    grad_ffn_bias = jnp.sum(grad_pre, axis=0)
    grad_ffn_input = line_sum([(grad_pre_low, ffn_in)], True, 3)
    grad_after_two = (
        residue + jax.vjp(layer_norm, after_two)[1](grad_ffn_input * (1.0 + scale_two))[0]
    )
    grad_two_low = grad_after_two.astype(low_type)
    grad_cross_out = jnp.dot(cross_att_low.T, grad_two_low, preferred_element_type=wide_type)
    grad_cross_att = (
        jnp.dot(grad_two_low, cross_out.T, preferred_element_type=wide_type)
        .astype(low_type)
        .reshape(head_shape)
    )
    cross_query_grads = []
    text_key_grads = []
    text_value_grads = []
    for head_no in range(local_heads):
        head_grads = head_backward(
            cross_query_low[:, :, head_no],
            text_key_heads[:, :, head_no],
            text_value_heads[:, :, head_no],
            text_valid,
            cross_totals[head_no],
            grad_cross_att[:, :, head_no],
            score_scale,
        )
        cross_query_grads.append(head_grads[0])
        text_key_grads.append(head_grads[2])
        text_value_grads.append(head_grads[3])
    grad_cross_query = jnp.stack(cross_query_grads, axis=2).reshape(flat_rows, local_width)
    text_grads_all = jnp.stack(
        [
            jnp.stack(text_key_grads, axis=2).reshape(clip_count, text_count, local_width),
            jnp.stack(text_value_grads, axis=2).reshape(clip_count, text_count, local_width),
        ]
    )
    text_grads = lax.psum_scatter(
        text_grads_all.astype(jnp.bfloat16), "seq", scatter_dimension=2, tiled=True
    ).astype(jnp.float32)
    query_term, key_term = small_sum(
        [
            jnp.sum(grad_cross_query * norm_gains[2] * cross_query_pre, axis=-1),
            jnp.sum(text_grads[0] * norm_gains[3] * text_key_pre, axis=-1),
        ],
        8,
    )
    grad_cross_query_pre = (
        grad_cross_query * norm_gains[2] * cross_rate
        - cross_query_pre * cross_rate**3 * query_term[:, None] / model_width
    )
    grad_text_key_pre = (
        text_grads[0] * norm_gains[3] * text_key_rate
        - text_key_pre * text_key_rate**3 * key_term[..., None] / model_width
    )
    gain_cross_query = jnp.sum(grad_cross_query * cross_query_pre * cross_rate, axis=0)
    gain_text_key = jnp.sum(text_grads[0] * text_key_pre * text_key_rate, axis=(0, 1))
    grad_cross_bias = jnp.stack(
        [
            jnp.sum(grad_cross_query_pre, axis=0),
            jnp.sum(grad_text_key_pre, axis=(0, 1)),
            jnp.sum(text_grads[1], axis=(0, 1)),
        ]
    )
    grad_cross_query_low = grad_cross_query_pre.astype(low_type)
    text_grad_low = jnp.stack([grad_text_key_pre, text_grads[1]]).astype(low_type)
    grad_cross_q = jnp.dot(cross_in.T, grad_cross_query_low, preferred_element_type=wide_type)
    grad_cross_kv = jnp.einsum(
        "ctd,kcte->kde", text_low, text_grad_low, preferred_element_type=wide_type
    )
    grad_text = lax.psum(
        jnp.einsum(
            "kcte,kde->ctd", text_grad_low, cross_kv, preferred_element_type=wide_type
        ).astype(jnp.bfloat16),
        "tensor",
    ).astype(jnp.float32)
    grad_cross_in = line_sum([(grad_cross_query_low, cross_q)], True, 4)
    grad_cross_gain = jnp.sum(grad_cross_in * normed_three, axis=0)
    grad_cross_shift = jnp.sum(grad_cross_in, axis=0)
    grad_after_one = (
        grad_after_two + jax.vjp(layer_norm, after_one)[1](grad_cross_in * cross_gain)[0]
    )
    grad_one = grad_after_one * gate_one
    grad_one_low = grad_one.astype(low_type)
    grad_self_out = jnp.dot(attn_low.T, grad_one_low, preferred_element_type=wide_type)
    grad_attn = (
        jnp.dot(grad_one_low, self_out.T, preferred_element_type=wide_type)
        .astype(low_type)
        .reshape(head_shape)
    )
    query_grads = []
    key_grads = []
    value_grads = []
    for head_no in range(local_heads):
        head_grads = head_backward(
            query_low[:, :, head_no],
            keys_all[:, :, head_no],
            values_all[:, :, head_no],
            key_valid,
            self_totals[head_no],
            grad_attn[:, :, head_no],
            score_scale,
        )
        query_grads.append(head_grads[0])
        key_grads.append(head_grads[2])
        value_grads.append(head_grads[3])
    owner_grads = [
        jnp.stack(parts, axis=2)
        .astype(jnp.bfloat16)
        .reshape(clip_count, seq_count, seq_rows, local_width)
        for parts in (key_grads, value_grads)
    ]
    owner_grads = jnp.concatenate(
        [
            jnp.swapaxes(part, 0, 1).reshape(seq_count, flat_rows, local_width)
            for part in owner_grads
        ],
        axis=-1,
    )
    pad_rows = -flat_rows % 16
    owner_grads = jnp.pad(owner_grads, ((0, 0), (0, pad_rows), (0, 0)))
    kv_rows = lax.psum_scatter(
        owner_grads.reshape(seq_count * (flat_rows + pad_rows), 2 * local_width),
        "seq",
        scatter_dimension=0,
        tiled=True,
    )[:flat_rows].astype(jnp.float32)
    kv_grads = (kv_rows[:, :local_width], kv_rows[:, local_width:])
    rotate_back = jax.vjp(rotate_now, query_norm)[1]
    grad_query_norm = rotate_back(jnp.stack(query_grads, axis=2))[0].reshape(flat_rows, local_width)
    grad_key_norm = rotate_back(kv_grads[0].reshape(head_shape))[0].reshape(flat_rows, local_width)
    query_back, key_back = small_sum(
        [
            jnp.sum(grad_query_norm * norm_gains[0] * query_pre, axis=-1),
            jnp.sum(grad_key_norm * norm_gains[1] * key_pre, axis=-1),
        ],
        9,
    )
    grad_query_pre = (
        grad_query_norm * norm_gains[0] * query_rate
        - query_pre * query_rate**3 * query_back[:, None] / model_width
    )
    grad_key_pre = (
        grad_key_norm * norm_gains[1] * key_rate
        - key_pre * key_rate**3 * key_back[:, None] / model_width
    )
    gain_query = jnp.sum(grad_query_norm * query_pre * query_rate, axis=0)
    gain_key = jnp.sum(grad_key_norm * key_pre * key_rate, axis=0)
    grad_proj = jnp.stack(
        [grad_query_pre, grad_key_pre, kv_grads[1].reshape(flat_rows, local_width)]
    )
    grad_self_bias = jnp.sum(grad_proj, axis=1)
    grad_proj_low = grad_proj.astype(low_type)
    grad_self_in = jnp.einsum(
        "rd,kre->kde", attn_in, grad_proj_low, preferred_element_type=wide_type
    )
    grad_attn_in = line_sum([(grad_proj_low[j], self_in[j]) for j in range(3)], True, 5)
    grad_hidden = (
        grad_after_one + jax.vjp(layer_norm, hidden_rows)[1](grad_attn_in * (1.0 + scale_one))[0]
    )
    grad_time_local = jnp.stack(
        [
            per_clip(grad_attn_in),
            per_clip(grad_attn_in * normed_one),
            per_clip(grad_after_one * branch_one),
            per_clip(grad_ffn_input),
            per_clip(grad_ffn_input * normed_two),
            per_clip(residue * branch_three),
        ],
        axis=1,
    )
    grad_out_bias = jnp.stack(
        [jnp.sum(grad_one, axis=0), jnp.sum(grad_after_two, axis=0), jnp.sum(grad_three, axis=0)]
    )
    stream_values = (
        grad_time_local,
        grad_cross_gain,
        grad_cross_shift,
        grad_out_bias,
        jnp.sum(residue * residue),
    )
    grad_time_local, grad_cross_gain, grad_cross_shift, grad_out_bias, square_local = stream_values
    grad_time = lax.psum(grad_time_local.astype(jnp.bfloat16), "seq").astype(jnp.float32)
    grad_norm_gains = jnp.stack([gain_query, gain_key, gain_cross_query, gain_text_key])
    (
        sum_self_bias,
        sum_gains,
        sum_cross_gain,
        sum_cross_shift,
        sum_cross_bias,
        sum_ffn_bias,
        sum_out_bias,
        sum_modulation,
        square_sum,
    ) = (
        lax.psum(grad_self_bias.astype(jnp.bfloat16), ("dp", "seq")).astype(jnp.float32),
        lax.psum(grad_norm_gains.astype(jnp.bfloat16), ("dp", "seq")).astype(jnp.float32),
        lax.psum(grad_cross_gain.astype(jnp.bfloat16), ("dp", "seq")).astype(jnp.float32),
        lax.psum(grad_cross_shift.astype(jnp.bfloat16), ("dp", "seq")).astype(jnp.float32),
        lax.psum(grad_cross_bias.astype(jnp.bfloat16), ("dp", "seq")).astype(jnp.float32),
        lax.psum(grad_ffn_bias.astype(jnp.bfloat16), ("dp", "seq")).astype(jnp.float32),
        lax.psum(grad_out_bias.astype(jnp.bfloat16), ("dp", "seq")).astype(jnp.float32),
        lax.psum(jnp.sum(grad_time_local, axis=0).astype(jnp.bfloat16), ("dp", "seq")).astype(
            jnp.float32
        ),
        lax.psum(square_local.astype(jnp.bfloat16), ("dp", "seq")).astype(jnp.float32),
    )
    loss = square_sum / (valid_total * model_width)
    (
        part_self_in,
        part_self_out,
        part_cross_q,
        part_cross_kv,
        part_cross_out,
        part_ffn_in,
        part_ffn_out,
    ) = (
        lax.psum_scatter(
            grad_self_in.astype(jnp.bfloat16), ("dp", "seq"), scatter_dimension=1, tiled=True
        ).astype(jnp.float32),
        lax.psum_scatter(
            grad_self_out.astype(jnp.bfloat16), ("dp", "seq"), scatter_dimension=1, tiled=True
        ).astype(jnp.float32),
        lax.psum_scatter(
            grad_cross_q.astype(jnp.bfloat16), ("dp", "seq"), scatter_dimension=0, tiled=True
        ).astype(jnp.float32),
        lax.psum_scatter(
            jnp.concatenate([grad_cross_kv[0], grad_cross_kv[1]], axis=-1).astype(jnp.bfloat16),
            ("dp", "seq"),
            scatter_dimension=0,
            tiled=True,
        ).astype(jnp.float32),
        lax.psum_scatter(
            grad_cross_out.astype(jnp.bfloat16), ("dp", "seq"), scatter_dimension=1, tiled=True
        ).astype(jnp.float32),
        lax.psum_scatter(
            grad_ffn_in.astype(jnp.bfloat16), ("dp", "seq"), scatter_dimension=0, tiled=True
        ).astype(jnp.float32),
        lax.psum_scatter(
            grad_ffn_out.astype(jnp.bfloat16), ("dp", "seq"), scatter_dimension=1, tiled=True
        ).astype(jnp.float32),
    )
    part_cross_kv = jnp.stack([part_cross_kv[:, :local_width], part_cross_kv[:, local_width:]])
    result_out = result.reshape(clip_count, seq_rows, model_width)
    grad_hidden_out = grad_hidden.reshape(clip_count, seq_rows, model_width)
    return (
        result_out,
        loss,
        grad_hidden_out,
        grad_text,
        grad_time,
        sum_modulation,
        part_self_in,
        sum_self_bias,
        part_self_out,
        sum_gains,
        sum_cross_gain,
        sum_cross_shift,
        part_cross_q,
        part_cross_kv,
        sum_cross_bias,
        part_cross_out,
        part_ffn_in,
        sum_ffn_bias,
        part_ffn_out,
        sum_out_bias,
    )


def solution(mesh):
    placed = (
        P("dp", "seq", None),
        P("dp", "seq", None),
        P("dp", "seq", None),
        P("dp", None, None),
        P(),
        P(None, "dp", "seq"),
        P(),
        P(None, None, "tensor"),
        P(None, "tensor"),
        P("tensor", None),
        P(None, "tensor"),
        P(),
        P(),
        P(None, "tensor"),
        P(None, None, "tensor"),
        P(None, "tensor"),
        P("tensor", None),
        P(None, "tensor"),
        P("tensor"),
        P("tensor", None),
        P(),
    )
    return jax.shard_map(
        shards,
        mesh=mesh,
        in_specs=placed,
        out_specs=(
            P("dp", "seq", None),
            P(),
            P("dp", "seq", None),
            P("dp", "seq", None),
            P("dp", None, None),
            P(),
            P(None, ("dp", "seq"), "tensor"),
            P(None, "tensor"),
            P("tensor", ("dp", "seq")),
            P(None, "tensor"),
            P(),
            P(),
            P(("dp", "seq"), "tensor"),
            P(None, ("dp", "seq"), "tensor"),
            P(None, "tensor"),
            P("tensor", ("dp", "seq")),
            P(("dp", "seq"), "tensor"),
            P("tensor"),
            P("tensor", ("dp", "seq")),
            P(),
        ),
        check_vma=False,
    )
```

```python
import functools
import math

import jax
import jax.numpy as jnp
from jax import lax
from jax.experimental import pallas as pl
from jax.experimental.pallas import tpu as pltpu
from jax.sharding import PartitionSpec as P

HEAD_DIM = 128
LOW = jnp.bfloat16
WIDE = jnp.float32


eps_norm = 1e-06


def layer_norm(values):
    centred = values - jnp.mean(values, axis=-1, keepdims=True)
    return centred * lax.rsqrt(jnp.mean(centred * centred, axis=-1, keepdims=True) + eps_norm)


def gelu_tanh(values):
    return (
        0.5
        * values
        * (1.0 + jnp.tanh(0.7978845608028654 * (values + 0.044715 * values * values * values)))
    )


def rope_tables(positions, head_size):
    sixth_part = head_size // 6
    part_spans = (head_size - 4 * sixth_part, 2 * sixth_part, 2 * sixth_part)
    pieces = []
    for axis_no in range(3):
        span_now = part_spans[axis_no]
        inverse = 1.0 / 10000.0 ** (jnp.arange(0, span_now, 2).astype(jnp.float32) / span_now)
        pieces.append(positions[axis_no].astype(jnp.float32)[..., None] * inverse)
    angles = jnp.concatenate(pieces, axis=-1)
    cosine_rep = jnp.repeat(jnp.cos(angles), 2, axis=-1)[..., None, :]
    sine_rep = jnp.repeat(jnp.sin(angles), 2, axis=-1)[..., None, :]
    return (cosine_rep, sine_rep)


def swap_table(head_size):
    row_no = jnp.arange(head_size)[:, None]
    col_no = jnp.arange(head_size)[None, :]
    upward = jnp.where((row_no % 2 == 0) & (col_no == row_no + 1), 1.0, 0.0)
    downward = jnp.where((row_no % 2 == 1) & (col_no == row_no - 1), -1.0, 0.0)
    return (upward + downward).astype(jnp.float32)


def rotate(values, cosine_rep, sine_rep, swap_matrix):
    swapped = jnp.matmul(values, swap_matrix, precision=lax.Precision.HIGHEST)
    return values * cosine_rep + swapped * sine_rep


def line_kernel(count, block, group, lag, lag2, turned, *refs):
    lhs_refs = refs[:count]
    rhs_refs = refs[count:2 * count]
    out_ref, raw, part, stage, cross, raw_s, raw_r, mid_s, mid_r, far_s, far_r, near_s, near_r = refs[2 * count:]
    steps = out_ref.shape[0] // block
    me = lax.axis_index("tensor")
    inner = (me == 1) | (me == 2)
    outer = jnp.logical_not(inner)
    leaf = jnp.where(me < 2, 0, 3)
    hub = jnp.where(me < 2, 1, 2)
    mate = 3 - me
    side = jnp.where(me < 2, 0, 1)

    def signal(where):
        pl.semaphore_signal(
            pltpu.get_barrier_semaphore(), inc=1, device_id={"tensor": where},
            device_id_type=pl.DeviceIdType.MESH)

    @pl.when(outer)
    def _():
        signal(hub)
        pl.semaphore_wait(pltpu.get_barrier_semaphore(), 1)

    @pl.when(inner)
    def _():
        signal(leaf)
        signal(mate)
        pl.semaphore_wait(pltpu.get_barrier_semaphore(), 2)

    def rows_of(step):
        return pl.ds(pl.multiple_of(step * block, 16), block)

    def remote(src, dst, send, recv, step, where):
        at = rows_of(step)
        return pltpu.make_async_remote_copy(
            src_ref=src.at[at], dst_ref=dst.at[at], send_sem=send.at[step], recv_sem=recv.at[step],
            device_id={"tensor": where}, device_id_type=pl.DeviceIdType.MESH)

    def raw_copy(step):
        return remote(raw, raw, raw_s, raw_r, step, hub)

    def mid_copy(step):
        return remote(stage, cross, mid_s, mid_r, step, mate)

    def far_copy(step):
        return remote(out_ref, out_ref, far_s, far_r, step, mate)

    def near_copy(step):
        return remote(out_ref, out_ref, near_s, near_r, step, leaf)

    def body(step, carry):
        @pl.when((step < steps) & (lax.rem(step, group) == 0))
        def _():
            at = pl.ds(pl.multiple_of(step * block, 16), block * group)
            total = None
            for lhs, rhs in zip(lhs_refs, rhs_refs):
                term = lax.dot_general(lhs[at], rhs[...], (((1,), (1 if turned else 0,)), ((), ())),
                    preferred_element_type=WIDE)
                total = term if total is None else total + term
            part[at] = total

        @pl.when(outer & (step < steps))
        def _():
            at = rows_of(step)
            raw[at] = part[at].astype(LOW)
            raw_copy(step).start()

        late = step - lag2
        @pl.when(inner & (late >= 0) & (late < steps) & (lax.rem(late + 2 * lag2, 2) != side))
        def _():
            far_copy(late).wait_recv()
            near_copy(late).start()

        near = step - lag
        @pl.when(inner & (near >= 0) & (near < steps) & (lax.rem(near + 2 * lag2, 2) == side))
        def _():
            at = rows_of(near)
            mid_copy(near).wait_recv()
            out_ref[at] = (part[at] + cross[at].astype(WIDE)).astype(LOW)
            far_copy(near).start()
            near_copy(near).start()

        @pl.when(inner & (step < steps))
        def _():
            at = rows_of(step)
            raw_copy(step).wait_recv()

            @pl.when(lax.rem(step, 2) == side)
            def _():
                part[at] = part[at] + raw[at].astype(WIDE)

            @pl.when(lax.rem(step, 2) != side)
            def _():
                stage[at] = (part[at] + raw[at].astype(WIDE)).astype(LOW)
                mid_copy(step).start()

        return carry

    lax.fori_loop(0, steps + lag2, body, 0)

    def drain(step, carry):
        @pl.when(outer)
        def _():
            near_copy(step).wait_recv()
            raw_copy(step).wait_send()

        @pl.when(inner)
        def _():
            near_copy(step).wait_send()

            @pl.when(lax.rem(step, 2) == side)
            def _():
                far_copy(step).wait_send()

            @pl.when(lax.rem(step, 2) != side)
            def _():
                mid_copy(step).wait_send()

        return carry

    lax.fori_loop(0, steps, drain, 0)

def line_sum(pairs, turned, ident, block=32, group=5, lag=3, lag2=6):
    true_rows = pairs[0][0].shape[0]
    width = pairs[0][1].shape[0 if turned else 1]
    unit = block * group
    rows = -(-true_rows // unit) * unit
    pairs = [(jnp.pad(lhs, ((0, rows - true_rows), (0, 0))), rhs) for lhs, rhs in pairs]
    steps = rows // block
    dma = pltpu.SemaphoreType.DMA
    depth = sum(p[0].shape[1] for p in pairs)
    return pl.pallas_call(
        functools.partial(line_kernel, len(pairs), block, group, lag, lag2, turned),
        out_shape=jax.ShapeDtypeStruct((rows, width), LOW),
        in_specs=[pl.BlockSpec(memory_space=pltpu.VMEM)] * (2 * len(pairs)),
        out_specs=pl.BlockSpec(memory_space=pltpu.VMEM),
        scratch_shapes=[
            pltpu.VMEM((rows, width), LOW),
            pltpu.VMEM((rows, width), WIDE),
            pltpu.VMEM((rows, width), LOW),
            pltpu.VMEM((rows, width), LOW),
        ] + [dma((steps,))] * 8,
        compiler_params=pltpu.CompilerParams(collective_id=ident, has_side_effects=True, vmem_limit_bytes=60 << 20),
        cost_estimate=pl.CostEstimate(flops=2 * rows * width * depth, bytes_accessed=230 * 10**6, transcendentals=0),
        name=f"line_sum_{ident}",
    )(*[p[0] for p in pairs], *[p[1] for p in pairs])[:true_rows].astype(WIDE)

def scatter_rows(mix, dimension):
    return lax.psum_scatter(mix, ("dp", "seq"), scatter_dimension=dimension, tiled=True)


def plane_sum_kernel(seq_count, value_ref, seq_ref, all_ref, slots, send_sem, recv_sem):
    count = slots.shape[0]
    dp = lax.axis_index("dp")
    me = dp * seq_count + lax.axis_index("seq")

    def device(place):
        return {"dp": place // seq_count, "seq": lax.rem(place, seq_count)}

    barrier = pltpu.get_barrier_semaphore()
    for hop in range(1, count):
        pl.semaphore_signal(
            barrier, inc=1, device_id=device(lax.rem(me + hop, count)),
            device_id_type=pl.DeviceIdType.MESH)
    pl.semaphore_wait(barrier, count - 1)

    def copy(slot, hop, place):
        return pltpu.make_async_remote_copy(
            src_ref=value_ref, dst_ref=slots.at[slot], send_sem=send_sem.at[hop - 1],
            recv_sem=recv_sem.at[hop - 1], device_id=device(place),
            device_id_type=pl.DeviceIdType.MESH)

    for hop in range(1, count):
        copy(me, hop, lax.rem(me + hop, count)).start()
    slots[pl.ds(me, 1)] = value_ref[...][None]
    for hop in range(1, count):
        origin = lax.rem(me + count - hop, count)
        copy(origin, hop, origin).wait_recv()
    for hop in range(1, count):
        copy(me, hop, lax.rem(me + hop, count)).wait_send()

    def span(start):
        total = slots[start].astype(WIDE)
        for slot in range(1, seq_count):
            total = total + slots[start + slot].astype(WIDE)
        return total

    seq_ref[...] = span(dp * seq_count)
    total = span(0)
    for part in range(1, count // seq_count):
        total = total + span(part * seq_count)
    all_ref[...] = total


def plane_sum(first, values, ident):
    seq_count = lax.axis_size("seq")
    count = lax.axis_size("dp") * seq_count
    flat = jnp.concatenate([value.reshape(-1).astype(LOW) for value in [first] + values])
    size = flat.shape[0]
    lines = -(-size // 2048) * 16
    packed = jnp.pad(flat, (0, lines * 128 - size)).reshape(lines, 128)
    vmem = pl.BlockSpec(memory_space=pltpu.VMEM)
    seq_total, all_total = pl.pallas_call(
        functools.partial(plane_sum_kernel, seq_count),
        out_shape=(jax.ShapeDtypeStruct((lines, 128), WIDE),) * 2,
        in_specs=[vmem],
        out_specs=(vmem, vmem),
        scratch_shapes=[
            pltpu.VMEM((count, lines, 128), LOW),
            pltpu.SemaphoreType.DMA((count - 1,)),
            pltpu.SemaphoreType.DMA((count - 1,)),
        ],
        compiler_params=pltpu.CompilerParams(collective_id=ident, has_side_effects=True),
        name="plane_sum",
    )(packed)
    all_total = all_total.reshape(-1)
    first_pair = (
        seq_total.reshape(-1)[: first.size].reshape(first.shape),
        all_total[: first.size].reshape(first.shape),
    )
    outs = []
    start = first.size
    for value in values:
        outs.append(all_total[start : start + value.size].reshape(value.shape))
        start += value.size
    return first_pair, outs


def small_kernel(value_ref, out_ref, slots, send_sem, recv_sem):
    count = slots.shape[0]
    me = lax.axis_index("tensor")
    barrier = pltpu.get_barrier_semaphore()
    for hop in range(1, count):
        pl.semaphore_signal(
            barrier, inc=1, device_id={"tensor": lax.rem(me + hop, count)},
            device_id_type=pl.DeviceIdType.MESH)
    pl.semaphore_wait(barrier, count - 1)
    copies = []
    for hop in range(1, count):
        copy = pltpu.make_async_remote_copy(
            src_ref=value_ref, dst_ref=slots.at[me], send_sem=send_sem.at[hop - 1],
            recv_sem=recv_sem.at[hop - 1], device_id={"tensor": lax.rem(me + hop, count)},
            device_id_type=pl.DeviceIdType.MESH)
        copy.start()
        copies.append(copy)
    slots[pl.ds(me, 1)] = value_ref[...][None]
    for hop in range(1, count):
        origin = lax.rem(me + count - hop, count)
        pltpu.make_async_remote_copy(
            src_ref=value_ref, dst_ref=slots.at[origin], send_sem=send_sem.at[hop - 1],
            recv_sem=recv_sem.at[hop - 1], device_id={"tensor": origin},
            device_id_type=pl.DeviceIdType.MESH).wait_recv()
    for copy in copies:
        copy.wait_send()
    total = slots[0]
    for slot in range(1, count):
        total = total + slots[slot]
    out_ref[...] = total


def small_sum(values, ident):
    count = lax.axis_size("tensor")
    flat = jnp.concatenate([value.reshape(-1) for value in values])
    size = flat.shape[0]
    lines = -(-size // 1024) * 8
    packed = jnp.pad(flat, (0, lines * 128 - size)).reshape(lines, 128)
    summed = pl.pallas_call(
        small_kernel,
        out_shape=jax.ShapeDtypeStruct((lines, 128), WIDE),
        in_specs=[pl.BlockSpec(memory_space=pltpu.VMEM)],
        out_specs=pl.BlockSpec(memory_space=pltpu.VMEM),
        scratch_shapes=[
            pltpu.VMEM((count, lines, 128), WIDE),
            pltpu.SemaphoreType.DMA((count - 1,)),
            pltpu.SemaphoreType.DMA((count - 1,)),
        ],
        compiler_params=pltpu.CompilerParams(collective_id=ident, has_side_effects=True),
        name=f"small_sum_{ident}",
    )(packed).reshape(-1)
    outs = []
    start = 0
    for value in values:
        outs.append(summed[start : start + value.size].reshape(value.shape))
        start += value.size
    return outs


LOG2E = 1.4426950408889634
HIDDEN_SCORE = -1e30


def plane_places():
    me = lax.axis_index("seq")
    column = lax.rem(me, 2)
    line = me // 2
    return (me, me + 1 - 2 * column, me + 2 - 4 * line, 3 - me)


def plane_barrier(places):
    barrier = pltpu.get_barrier_semaphore()
    for place in places[1:]:
        pl.semaphore_signal(
            barrier, inc=1, device_id={"seq": place}, device_id_type=pl.DeviceIdType.MESH
        )
    pl.semaphore_wait(barrier, 3)


def plane_copy(src, dst, send, recv, place):
    return pltpu.make_async_remote_copy(
        src_ref=src,
        dst_ref=dst,
        send_sem=send,
        recv_sem=recv,
        device_id={"seq": place},
        device_id_type=pl.DeviceIdType.MESH,
    )


def head_lanes(head):
    return pl.ds(pl.multiple_of(head * HEAD_DIM, 128), HEAD_DIM)


def block_valid(key_rows, owner, true_rows, length):
    row = lax.broadcasted_iota(jnp.int32, (key_rows, 1), 0)
    return (row < true_rows) & (owner * true_rows + row < length)


def over_last(lhs, rhs):
    return lax.dot_general(lhs, rhs, (((1,), (1,)), ((), ())), preferred_element_type=WIDE)


def attend_kernel(
    true_rows, length_ref, query_ref, kv_ref, out_ref, turned_ref, total_ref, got_ref, peak, summed, send, recv
):
    places = plane_places()
    plane_barrier(places)
    heads = query_ref.shape[1] // HEAD_DIM
    key_rows = kv_ref.shape[1]
    length = length_ref[0]
    factor = LOG2E / math.sqrt(HEAD_DIM)

    def own_copy(relation, part):
        index = 2 * relation + part
        return plane_copy(
            kv_ref.at[part], got_ref.at[relation, part], send.at[index], recv.at[index], places[relation + 1]
        )

    key_pass = plane_copy(got_ref.at[0, 0], got_ref.at[2, 0], send.at[4], recv.at[4], places[2])
    value_pass = plane_copy(got_ref.at[1, 1], got_ref.at[2, 1], send.at[5], recv.at[5], places[1])
    for part in range(2):
        for relation in range(2):
            own_copy(relation, part).start()

    peak[...] = jnp.full(peak.shape, HIDDEN_SCORE, WIDE)
    summed[...] = jnp.zeros(summed.shape, WIDE)
    turned_ref[...] = jnp.zeros(turned_ref.shape, WIDE)

    def block(source, owner):
        def step(head, carry):
            lanes = head_lanes(head)
            scores = over_last(source(0, lanes), query_ref[:, lanes]) * factor
            scores = jnp.where(block_valid(key_rows, owner, true_rows, length), scores, HIDDEN_SCORE)
            before = peak[head]
            after = jnp.maximum(before, jnp.max(scores, axis=0, keepdims=True))
            shrink = jnp.exp2(before - after)
            terms = jnp.exp2(scores - after)
            peak[head] = after
            summed[head] = summed[head] * shrink + jnp.sum(terms, axis=0, keepdims=True)
            turned_ref[head] = turned_ref[head] * shrink + lax.dot_general(
                source(1, lanes),
                terms.astype(LOW),
                (((0,), (0,)), ((), ())),
                preferred_element_type=WIDE,
            )

            return carry

        lax.fori_loop(0, heads, step, 0)

    block(lambda part, lanes: kv_ref[part, :, lanes], places[0])
    own_copy(0, 0).wait_recv()
    key_pass.start()
    own_copy(0, 1).wait_recv()
    own_copy(1, 1).wait_recv()
    value_pass.start()
    own_copy(1, 0).wait_recv()
    for relation in range(3):
        if relation == 2:
            key_pass.wait_recv()
            value_pass.wait_recv()
        block(
            lambda part, lanes, relation=relation: got_ref[relation, part, :, lanes],
            places[relation + 1],
        )

    for head in range(heads):
        lanes = slice(head * HEAD_DIM, (head + 1) * HEAD_DIM)
        attended = turned_ref[head] / summed[head]
        turned_ref[head] = attended
        out_ref[:, lanes] = jnp.transpose(attended).astype(LOW)
        total_ref[head] = peak[head] + jnp.log2(summed[head])
    for part in range(2):
        for relation in range(2):
            own_copy(relation, part).wait_send()
    key_pass.wait_send()
    value_pass.wait_send()


def attend(query_low, kv_low, length, true_rows, ident):
    rows, width = query_low.shape
    heads = width // HEAD_DIM
    key_rows = kv_low.shape[1]
    dma = pltpu.SemaphoreType.DMA
    vmem = pl.BlockSpec(memory_space=pltpu.VMEM)
    return pl.pallas_call(
        functools.partial(attend_kernel, true_rows),
        out_shape=(
            jax.ShapeDtypeStruct((rows, width), LOW),
            jax.ShapeDtypeStruct((heads, HEAD_DIM, rows), WIDE),
            jax.ShapeDtypeStruct((heads, 1, rows), WIDE),
            jax.ShapeDtypeStruct((3, 2, key_rows, width), LOW),
        ),
        in_specs=[pl.BlockSpec(memory_space=pltpu.SMEM), vmem, vmem],
        out_specs=(vmem,) * 4,
        scratch_shapes=[
            pltpu.VMEM((heads, 1, rows), WIDE),
            pltpu.VMEM((heads, 1, rows), WIDE),
            dma((6,)),
            dma((6,)),
        ],
        compiler_params=pltpu.CompilerParams(
            collective_id=ident, has_side_effects=True, vmem_limit_bytes=56 << 20
        ),
        cost_estimate=pl.CostEstimate(flops=10**9, bytes_accessed=150 * 10**6, transcendentals=0),
        name="attend",
    )(length, query_low, kv_low)


def attend_back_kernel(
    true_rows, length_ref, query_ref, kv_ref, got_ref, turned_ref, total_ref, grad_ref,
    query_grad_ref, kv_grad_ref, centre, query_turned, leaving, landing, send, recv,
):
    places = plane_places()
    plane_barrier(places)
    heads = query_ref.shape[1] // HEAD_DIM
    key_rows = kv_ref.shape[1]
    length = length_ref[0]
    scale = 1.0 / math.sqrt(HEAD_DIM)
    for head in range(heads):
        lanes = slice(head * HEAD_DIM, (head + 1) * HEAD_DIM)
        grads = jnp.transpose(grad_ref[:, lanes].astype(WIDE))
        centre[head] = jnp.sum(grads * turned_ref[head], axis=0, keepdims=True)
    query_turned[...] = jnp.zeros(query_turned.shape, WIDE)

    def block(source, sink, owner):
        def step(head, carry):
            lanes = head_lanes(head)
            keys = source(0, lanes)
            query = query_ref[:, lanes]
            grads = grad_ref[:, lanes]
            probs = jnp.exp2(over_last(keys, query) * (scale * LOG2E) - total_ref[head])
            probs = jnp.where(block_valid(key_rows, owner, true_rows, length), probs, 0.0)
            grad_probs = over_last(source(1, lanes), grads)
            grad_scores = (probs * (grad_probs - centre[head])).astype(LOW)
            sink(0, lanes, jnp.dot(grad_scores, query, preferred_element_type=WIDE) * scale)
            sink(1, lanes, jnp.dot(probs.astype(LOW), grads, preferred_element_type=WIDE))
            query_turned[head] = query_turned[head] + lax.dot_general(
                keys, grad_scores, (((0,), (0,)), ((), ())), preferred_element_type=WIDE
            )

            return carry

        lax.fori_loop(0, heads, step, 0)

    def grad_copy(relation, part):
        return plane_copy(
            leaving.at[relation, part],
            landing.at[relation, part],
            send.at[relation, part],
            recv.at[relation, part],
            places[relation + 1],
        )

    for relation in (2, 1, 0):

        def sink(part, lanes, value, relation=relation):
            leaving[relation, part, :, lanes] = value.astype(LOW)

        block(
            lambda part, lanes, relation=relation: got_ref[relation, part, :, lanes],
            sink,
            places[relation + 1],
        )
        for part in range(2):
            grad_copy(relation, part).start()

    def own_sink(part, lanes, value):
        kv_grad_ref[part, :, lanes] = value

    block(lambda part, lanes: kv_ref[part, :, lanes], own_sink, places[0])
    for head in range(heads):
        lanes = slice(head * HEAD_DIM, (head + 1) * HEAD_DIM)
        query_grad_ref[:, lanes] = jnp.transpose(query_turned[head]) * scale
    for relation in (2, 1, 0):
        for part in range(2):
            grad_copy(relation, part).wait_recv()

    def gather(tile, carry):
        rows = pl.ds(pl.multiple_of(tile * 16, 16), 16)
        for part in range(2):
            total = kv_grad_ref[part, rows]
            for relation in range(3):
                total = total + landing[relation, part, rows].astype(WIDE)
            kv_grad_ref[part, rows] = total
        return carry

    lax.fori_loop(0, key_rows // 16, gather, 0)
    for relation in range(3):
        for part in range(2):
            grad_copy(relation, part).wait_send()


def attend_back(query_low, kv_low, got, turned, total, grad_low, length, true_rows, ident):
    rows, width = query_low.shape
    heads = width // HEAD_DIM
    key_rows = kv_low.shape[1]
    dma = pltpu.SemaphoreType.DMA
    vmem = pl.BlockSpec(memory_space=pltpu.VMEM)
    return pl.pallas_call(
        functools.partial(attend_back_kernel, true_rows),
        out_shape=(
            jax.ShapeDtypeStruct((rows, width), WIDE),
            jax.ShapeDtypeStruct((2, key_rows, width), WIDE),
        ),
        in_specs=[pl.BlockSpec(memory_space=pltpu.SMEM)] + [vmem] * 6,
        out_specs=(vmem,) * 2,
        scratch_shapes=[
            pltpu.VMEM((heads, 1, rows), WIDE),
            pltpu.VMEM((heads, HEAD_DIM, rows), WIDE),
            pltpu.VMEM((3, 2, key_rows, width), LOW),
            pltpu.VMEM((3, 2, key_rows, width), LOW),
            dma((3, 2)),
            dma((3, 2)),
        ],
        compiler_params=pltpu.CompilerParams(
            collective_id=ident, has_side_effects=True, vmem_limit_bytes=56 << 20
        ),
        cost_estimate=pl.CostEstimate(flops=10**9, bytes_accessed=200 * 10**6, transcendentals=0),
        name="attend_back",
    )(length, query_low, kv_low, got, turned, total, grad_low)


def head_forward(query, keys, values, key_ok, score_scale):
    scores = (
        jnp.einsum("csh,clh->csl", query, keys, preferred_element_type=jnp.float32) * score_scale
    )
    scores = jnp.where(key_ok[:, None, :], scores, -jnp.inf)
    row_peak = jnp.max(scores, axis=-1, keepdims=True)
    exp_terms = jnp.exp(scores - row_peak)
    summed = jnp.sum(exp_terms, axis=-1, keepdims=True)
    probs_low = (exp_terms / summed).astype(jnp.bfloat16)
    attended = jnp.einsum("csl,clh->csh", probs_low, values, preferred_element_type=jnp.float32)
    return (attended, row_peak[..., 0] + jnp.log(summed[..., 0]))


def head_backward(query, keys, values, key_ok, log_total, grad_att, score_scale):
    scores = (
        jnp.einsum("csh,clh->csl", query, keys, preferred_element_type=jnp.float32) * score_scale
    )
    probs = jnp.where(key_ok[:, None, :], jnp.exp(scores - log_total[..., None]), 0.0)
    grad_probs = jnp.einsum("csh,clh->csl", grad_att, values, preferred_element_type=jnp.float32)
    centre = jnp.sum(probs * grad_probs, axis=-1)
    grad_scores = (probs * (grad_probs - centre[..., None])).astype(jnp.bfloat16)
    grad_query = (
        jnp.einsum("csl,clh->csh", grad_scores, keys, preferred_element_type=jnp.float32)
        * score_scale
    )
    grad_keys = (
        jnp.einsum("csl,csh->clh", grad_scores, query, preferred_element_type=jnp.float32)
        * score_scale
    )
    grad_values = jnp.einsum(
        "csl,csh->clh", probs.astype(jnp.bfloat16), grad_att, preferred_element_type=jnp.float32
    )
    return (grad_query, centre, grad_keys, grad_values)


def shards(
    hidden,
    teacher,
    text,
    time_embed,
    lengths,
    positions,
    modulation,
    self_in,
    self_bias,
    self_out,
    norm_gains,
    cross_gain,
    cross_shift,
    cross_q,
    cross_kv,
    cross_bias,
    cross_out,
    ffn_in,
    ffn_in_bias,
    ffn_out,
    out_bias,
):
    low_type = jnp.bfloat16
    wide_type = jnp.float32
    clip_count, seq_rows, model_width = hidden.shape
    local_width = self_in.shape[2]
    local_heads = local_width // HEAD_DIM
    text_local = text.shape[1]
    seq_count = lax.axis_size("seq")
    slot_count = seq_rows * seq_count
    text_count = text_local * seq_count
    flat_rows = clip_count * seq_rows
    score_scale = 1.0 / math.sqrt(HEAD_DIM)
    seq_place = lax.axis_index("seq")
    clip_first = lax.axis_index("dp") * clip_count
    clip_lengths = lax.dynamic_slice_in_dim(lengths, clip_first, clip_count)
    key_valid = jnp.arange(slot_count, dtype=jnp.int32)[None, :] < clip_lengths[:, None]
    row_ids = seq_place * seq_rows + jnp.arange(seq_rows, dtype=jnp.int32)
    row_valid = row_ids[None, :] < clip_lengths[:, None]
    text_valid = jnp.ones((clip_count, text_count), dtype=jnp.bool_)
    valid_total = jnp.sum(lengths).astype(wide_type)
    modulated = modulation[None] + time_embed
    cosine_rep, sine_rep = rope_tables(positions, HEAD_DIM)
    rotate_now = functools.partial(
        rotate, cosine_rep=cosine_rep, sine_rep=sine_rep, swap_matrix=swap_table(HEAD_DIM)
    )
    head_shape = (clip_count, seq_rows, local_heads, HEAD_DIM)
    clip_ids = jnp.arange(flat_rows, dtype=jnp.int32) // seq_rows
    clip_table = (clip_ids[:, None] == jnp.arange(clip_count, dtype=jnp.int32)[None, :]).astype(
        wide_type
    )
    valid_rows = row_valid.reshape(flat_rows)
    hidden_rows = hidden.reshape(flat_rows, model_width)
    teacher_rows = teacher.reshape(flat_rows, model_width)

    def per_row(index_no):
        return jnp.dot(clip_table, modulated[:, index_no], precision=lax.Precision.HIGHEST)

    def per_clip(values):
        return jnp.dot(clip_table.T, values, precision=lax.Precision.HIGHEST)

    scale_one = per_row(1)
    gate_one = per_row(2)
    scale_two = per_row(4)
    gate_two = per_row(5)
    normed_one = layer_norm(hidden_rows)
    attn_in = (normed_one * (1.0 + scale_one) + per_row(0)).astype(low_type)
    projected = (
        jnp.einsum("rd,kde->kre", attn_in, self_in, preferred_element_type=wide_type)
        + self_bias[:, None, :]
    )
    query_pre = projected[0]
    key_pre = projected[1]
    value_pre = projected[2]
    query_sq, key_sq = small_sum(
        [jnp.sum(query_pre * query_pre, axis=-1), jnp.sum(key_pre * key_pre, axis=-1)], 6
    )
    query_rate = lax.rsqrt(query_sq / model_width + eps_norm)[:, None]
    key_rate = lax.rsqrt(key_sq / model_width + eps_norm)[:, None]
    query_norm = (query_pre * query_rate * norm_gains[0]).reshape(head_shape)
    key_norm = (key_pre * key_rate * norm_gains[1]).reshape(head_shape)
    query_low = rotate_now(query_norm).astype(low_type)
    key_low = rotate_now(key_norm).astype(low_type)
    value_low = value_pre.astype(low_type).reshape(head_shape)
    plane = seq_count == 4 and clip_count == 1
    if plane:
        query_pad = -flat_rows % 128
        key_pad = -flat_rows % 16
        query_flat = query_low.reshape(flat_rows, local_width)
        query_flat = jnp.pad(query_flat, ((0, query_pad), (0, 0)))
        own_kv = jnp.pad(
            jnp.stack(
                [key_low.reshape(flat_rows, local_width), value_low.reshape(flat_rows, local_width)]
            ),
            ((0, 0), (0, key_pad), (0, 0)),
        )
        attn_low, attn_turned, self_totals, got_kv = attend(
            query_flat, own_kv, clip_lengths, flat_rows, 10
        )
        attn_low = attn_low[:flat_rows]
    else:
        local_kv = jnp.stack(
            [
                key_low.reshape(clip_count, seq_rows, local_width),
                value_low.reshape(clip_count, seq_rows, local_width),
            ]
        )
        whole_kv = lax.all_gather(local_kv, "seq", axis=2, tiled=True)
        keys_all = whole_kv[0].reshape(clip_count, slot_count, local_heads, HEAD_DIM)
        values_all = whole_kv[1].reshape(clip_count, slot_count, local_heads, HEAD_DIM)
        att_heads = []
        total_heads = []
        for head_no in range(local_heads):
            attended, log_total = head_forward(
                query_low[:, :, head_no],
                keys_all[:, :, head_no],
                values_all[:, :, head_no],
                key_valid,
                score_scale,
            )
            att_heads.append(attended)
            total_heads.append(log_total)
        attn_low = jnp.stack(att_heads, axis=2).astype(low_type).reshape(flat_rows, local_width)
        self_totals = jnp.stack(total_heads)
    branch_one = (
        line_sum([(attn_low, self_out)], False, 0) + out_bias[0]
    )
    after_one = hidden_rows + branch_one * gate_one
    normed_three = layer_norm(after_one)
    cross_in = (normed_three * cross_gain + cross_shift).astype(low_type)
    cross_query_pre = jnp.dot(cross_in, cross_q, preferred_element_type=wide_type) + cross_bias[0]
    text_low = text.astype(low_type)
    text_start = seq_place * text_local
    text_all = lax.all_gather(text_low, "seq", axis=1, tiled=True)
    text_proj = (
        jnp.einsum("ctd,kde->kcte", text_all, cross_kv, preferred_element_type=wide_type)
        + cross_bias[1:, None, None, :]
    )
    cross_sq, text_sq = small_sum(
        [
            jnp.sum(cross_query_pre * cross_query_pre, axis=-1),
            jnp.sum(text_proj[0] * text_proj[0], axis=-1),
        ],
        7,
    )
    text_rate_all = lax.rsqrt(text_sq / model_width + eps_norm)[..., None]
    text_key_low = (text_proj[0] * text_rate_all * norm_gains[3]).astype(low_type)
    text_value_low = text_proj[1].astype(low_type)
    text_key_pre = lax.dynamic_slice_in_dim(text_proj[0], text_start, text_local, 1)
    text_key_rate = lax.dynamic_slice_in_dim(text_rate_all, text_start, text_local, 1)
    cross_rate = lax.rsqrt(cross_sq / model_width + eps_norm)[:, None]
    cross_query_low = (
        (cross_query_pre * cross_rate * norm_gains[2]).astype(low_type).reshape(head_shape)
    )
    text_key_heads = text_key_low.reshape(clip_count, text_count, local_heads, HEAD_DIM)
    text_value_heads = text_value_low.reshape(clip_count, text_count, local_heads, HEAD_DIM)
    cross_heads = []
    cross_total_heads = []
    for head_no in range(local_heads):
        attended, log_total = head_forward(
            cross_query_low[:, :, head_no],
            text_key_heads[:, :, head_no],
            text_value_heads[:, :, head_no],
            text_valid,
            score_scale,
        )
        cross_heads.append(attended)
        cross_total_heads.append(log_total)
    cross_att_low = jnp.stack(cross_heads, axis=2).astype(low_type).reshape(flat_rows, local_width)
    cross_totals = jnp.stack(cross_total_heads)
    branch_two = (
        line_sum([(cross_att_low, cross_out)], False, 1)
        + out_bias[1]
    )
    after_two = after_one + branch_two
    normed_two = layer_norm(after_two)
    ffn_input = (normed_two * (1.0 + scale_two) + per_row(3)).astype(low_type)
    pre_act = jnp.dot(ffn_input, ffn_in, preferred_element_type=wide_type) + ffn_in_bias
    act_low = gelu_tanh(pre_act).astype(low_type)
    branch_three = (
        line_sum([(act_low, ffn_out)], False, 2) + out_bias[2]
    )
    result = after_two + branch_three * gate_two
    residue = jnp.where(valid_rows[:, None], result - teacher_rows, 0.0)
    grad_three = residue * gate_two
    grad_three_low = grad_three.astype(low_type)
    ffn_out_mix = jnp.dot(act_low.T, grad_three_low, preferred_element_type=wide_type)
    grad_act = jnp.dot(grad_three_low, ffn_out.T, preferred_element_type=wide_type)
    grad_pre = jax.vjp(gelu_tanh, pre_act)[1](grad_act)[0]
    grad_pre_low = grad_pre.astype(low_type)
    grad_pre_low, ffn_out_mix = lax.optimization_barrier(
        (grad_pre_low, ffn_out_mix.astype(low_type))
    )
    part_ffn_out = scatter_rows(ffn_out_mix, 1)
    ffn_in_mix = jnp.dot(ffn_input.T, grad_pre_low, preferred_element_type=wide_type)
    grad_ffn_bias = jnp.sum(grad_pre, axis=0)
    grad_ffn_input = line_sum([(grad_pre_low, ffn_in)], True, 3)
    grad_after_two = (
        residue + jax.vjp(layer_norm, after_two)[1](grad_ffn_input * (1.0 + scale_two))[0]
    )
    grad_two_low = grad_after_two.astype(low_type)
    cross_out_mix = jnp.dot(grad_two_low.T, cross_att_low, preferred_element_type=wide_type)
    grad_cross_att = (
        jnp.dot(grad_two_low, cross_out.T, preferred_element_type=wide_type)
        .astype(low_type)
        .reshape(head_shape)
    )
    cross_query_grads = []
    text_key_grads = []
    text_value_grads = []
    for head_no in range(local_heads):
        head_grads = head_backward(
            cross_query_low[:, :, head_no],
            text_key_heads[:, :, head_no],
            text_value_heads[:, :, head_no],
            text_valid,
            cross_totals[head_no],
            grad_cross_att[:, :, head_no],
            score_scale,
        )
        cross_query_grads.append(head_grads[0])
        text_key_grads.append(head_grads[2])
        text_value_grads.append(head_grads[3])
    grad_cross_query = jnp.stack(cross_query_grads, axis=2).reshape(flat_rows, local_width)
    text_grads_all = jnp.stack(
        [
            jnp.stack(text_key_grads, axis=2).reshape(clip_count, text_count, local_width),
            jnp.stack(text_value_grads, axis=2).reshape(clip_count, text_count, local_width),
        ]
    )
    text_grads = lax.psum_scatter(
        text_grads_all.astype(jnp.bfloat16), "seq", scatter_dimension=2, tiled=True
    ).astype(jnp.float32)
    (query_term,) = small_sum(
        [jnp.sum(grad_cross_query * norm_gains[2] * cross_query_pre, axis=-1)], 8
    )
    grad_cross_query_pre = (
        grad_cross_query * norm_gains[2] * cross_rate
        - cross_query_pre * cross_rate**3 * query_term[:, None] / model_width
    )
    gain_cross_query = jnp.sum(grad_cross_query * cross_query_pre * cross_rate, axis=0)
    grad_cross_query_low = grad_cross_query_pre.astype(low_type)
    grad_cross_query_low, ffn_in_mix, part_ffn_out = lax.optimization_barrier(
        (grad_cross_query_low, ffn_in_mix.astype(low_type), part_ffn_out)
    )
    part_ffn_in = scatter_rows(ffn_in_mix, 0)
    cross_q_mix = jnp.dot(cross_in.T, grad_cross_query_low, preferred_element_type=wide_type)
    grad_cross_in = line_sum([(grad_cross_query_low, cross_q)], True, 4)
    text_grads, grad_cross_in = lax.optimization_barrier((text_grads, grad_cross_in))
    (key_term,) = small_sum(
        [jnp.sum(text_grads[0] * norm_gains[3] * text_key_pre, axis=-1)], 12
    )
    grad_text_key_pre = (
        text_grads[0] * norm_gains[3] * text_key_rate
        - text_key_pre * text_key_rate**3 * key_term[..., None] / model_width
    )
    gain_text_key = jnp.sum(text_grads[0] * text_key_pre * text_key_rate, axis=(0, 1))
    grad_cross_bias = jnp.stack(
        [
            jnp.sum(grad_cross_query_pre, axis=0),
            jnp.sum(grad_text_key_pre, axis=(0, 1)),
            jnp.sum(text_grads[1], axis=(0, 1)),
        ]
    )
    text_grad_low = jnp.stack([grad_text_key_pre, text_grads[1]]).astype(low_type)
    cross_kv_mix = jnp.einsum(
        "ctd,kcte->kde", text_low, text_grad_low, preferred_element_type=wide_type
    )
    grad_text = lax.psum(
        jnp.einsum(
            "kcte,kde->ctd", text_grad_low, cross_kv, preferred_element_type=wide_type
        ).astype(jnp.bfloat16),
        "tensor",
    ).astype(jnp.float32)
    grad_cross_gain = jnp.sum(grad_cross_in * normed_three, axis=0)
    grad_cross_shift = jnp.sum(grad_cross_in, axis=0)
    grad_after_one = (
        grad_after_two + jax.vjp(layer_norm, after_one)[1](grad_cross_in * cross_gain)[0]
    )
    grad_one = grad_after_one * gate_one
    grad_one_low = grad_one.astype(low_type)
    self_out_mix = jnp.dot(grad_one_low.T, attn_low, preferred_element_type=wide_type)
    grad_attn = (
        jnp.dot(grad_one_low, self_out.T, preferred_element_type=wide_type)
        .astype(low_type)
        .reshape(head_shape)
    )
    group_mix = jnp.concatenate(
        [cross_out_mix, cross_q_mix, self_out_mix, cross_kv_mix[0], cross_kv_mix[1]], axis=-1
    ).astype(low_type)
    grad_attn, group_mix = lax.optimization_barrier((grad_attn, group_mix))
    part_group = scatter_rows(group_mix, 0)
    if plane:
        query_grads, kv_grads = attend_back(
            query_flat,
            own_kv,
            got_kv,
            attn_turned,
            self_totals,
            jnp.pad(grad_attn.reshape(flat_rows, local_width), ((0, query_pad), (0, 0))),
            clip_lengths,
            flat_rows,
            11,
        )
        query_grads = query_grads[:flat_rows].reshape(head_shape)
        kv_grads = kv_grads[:, :flat_rows]
    else:
        query_grads = []
        key_grads = []
        value_grads = []
        for head_no in range(local_heads):
            head_grads = head_backward(
                query_low[:, :, head_no],
                keys_all[:, :, head_no],
                values_all[:, :, head_no],
                key_valid,
                self_totals[head_no],
                grad_attn[:, :, head_no],
                score_scale,
            )
            query_grads.append(head_grads[0])
            key_grads.append(head_grads[2])
            value_grads.append(head_grads[3])
        owner_grads = [
            jnp.stack(parts, axis=2)
            .astype(jnp.bfloat16)
            .reshape(clip_count, seq_count, seq_rows, local_width)
            for parts in (key_grads, value_grads)
        ]
        owner_grads = jnp.concatenate(
            [
                jnp.swapaxes(part, 0, 1).reshape(seq_count, flat_rows, local_width)
                for part in owner_grads
            ],
            axis=-1,
        )
        pad_rows = -flat_rows % 16
        owner_grads = jnp.pad(owner_grads, ((0, 0), (0, pad_rows), (0, 0)))
        kv_rows = lax.psum_scatter(
            owner_grads.reshape(seq_count * (flat_rows + pad_rows), 2 * local_width),
            "seq",
            scatter_dimension=0,
            tiled=True,
        )[:flat_rows].astype(jnp.float32)
        kv_grads = (kv_rows[:, :local_width], kv_rows[:, local_width:])
        query_grads = jnp.stack(query_grads, axis=2)
    query_grads, part_ffn_in = lax.optimization_barrier((query_grads, part_ffn_in))
    rotate_back = jax.vjp(rotate_now, query_norm)[1]
    grad_query_norm = rotate_back(query_grads)[0].reshape(flat_rows, local_width)
    grad_key_norm = rotate_back(kv_grads[0].reshape(head_shape))[0].reshape(flat_rows, local_width)
    query_back, key_back = small_sum(
        [
            jnp.sum(grad_query_norm * norm_gains[0] * query_pre, axis=-1),
            jnp.sum(grad_key_norm * norm_gains[1] * key_pre, axis=-1),
        ],
        9,
    )
    grad_query_pre = (
        grad_query_norm * norm_gains[0] * query_rate
        - query_pre * query_rate**3 * query_back[:, None] / model_width
    )
    grad_key_pre = (
        grad_key_norm * norm_gains[1] * key_rate
        - key_pre * key_rate**3 * key_back[:, None] / model_width
    )
    gain_query = jnp.sum(grad_query_norm * query_pre * query_rate, axis=0)
    gain_key = jnp.sum(grad_key_norm * key_pre * key_rate, axis=0)
    grad_proj = jnp.stack(
        [grad_query_pre, grad_key_pre, kv_grads[1].reshape(flat_rows, local_width)]
    )
    grad_self_bias = jnp.sum(grad_proj, axis=1)
    grad_proj_low = grad_proj.astype(low_type)
    self_in_mix = jnp.concatenate(
        [
            jnp.dot(attn_in.T, grad_proj_low[j], preferred_element_type=wide_type).astype(low_type)
            for j in range(3)
        ],
        axis=-1,
    )
    grad_proj_low, self_in_mix, part_group = lax.optimization_barrier(
        (grad_proj_low, self_in_mix, part_group)
    )
    part_self_in = scatter_rows(self_in_mix, 0)
    grad_attn_in = line_sum([(grad_proj_low[j], self_in[j]) for j in range(3)], True, 5)
    grad_hidden = (
        grad_after_one + jax.vjp(layer_norm, hidden_rows)[1](grad_attn_in * (1.0 + scale_one))[0]
    )
    grad_time_local = jnp.stack(
        [
            per_clip(grad_attn_in),
            per_clip(grad_attn_in * normed_one),
            per_clip(grad_after_one * branch_one),
            per_clip(grad_ffn_input),
            per_clip(grad_ffn_input * normed_two),
            per_clip(residue * branch_three),
        ],
        axis=1,
    )
    grad_out_bias = jnp.stack(
        [jnp.sum(grad_one, axis=0), jnp.sum(grad_after_two, axis=0), jnp.sum(grad_three, axis=0)]
    )
    stream_values = (
        grad_time_local,
        grad_cross_gain,
        grad_cross_shift,
        grad_out_bias,
        jnp.sum(residue * residue),
    )
    grad_time_local, grad_cross_gain, grad_cross_shift, grad_out_bias, square_local = stream_values
    grad_norm_gains = jnp.stack([gain_query, gain_key, gain_cross_query, gain_text_key])
    time_pair, sums = plane_sum(
        grad_time_local,
        [
            grad_self_bias,
            grad_norm_gains,
            grad_cross_gain,
            grad_cross_shift,
            grad_cross_bias,
            grad_ffn_bias,
            grad_out_bias,
            square_local,
        ],
        13,
    )
    grad_time, time_all = time_pair
    sum_modulation = jnp.sum(time_all, axis=0)
    (
        sum_self_bias,
        sum_gains,
        sum_cross_gain,
        sum_cross_shift,
        sum_cross_bias,
        sum_ffn_bias,
        sum_out_bias,
        square_sum,
    ) = sums
    loss = square_sum / (valid_total * model_width)
    part_ffn_in = part_ffn_in.astype(wide_type)
    part_ffn_out = part_ffn_out.astype(wide_type)
    pieces = [
        part_group[:, j * local_width : (j + 1) * local_width].astype(wide_type) for j in range(5)
    ]
    part_cross_out = pieces[0].T
    part_cross_q = pieces[1]
    part_self_out = pieces[2].T
    part_cross_kv = jnp.stack([pieces[3], pieces[4]])
    part_self_in = jnp.stack(
        [part_self_in[:, j * local_width : (j + 1) * local_width] for j in range(3)]
    ).astype(wide_type)
    result_out = result.reshape(clip_count, seq_rows, model_width)
    grad_hidden_out = grad_hidden.reshape(clip_count, seq_rows, model_width)
    return (
        result_out,
        loss,
        grad_hidden_out,
        grad_text,
        grad_time,
        sum_modulation,
        part_self_in,
        sum_self_bias,
        part_self_out,
        sum_gains,
        sum_cross_gain,
        sum_cross_shift,
        part_cross_q,
        part_cross_kv,
        sum_cross_bias,
        part_cross_out,
        part_ffn_in,
        sum_ffn_bias,
        part_ffn_out,
        sum_out_bias,
    )


def solution(mesh):
    placed = (
        P("dp", "seq", None),
        P("dp", "seq", None),
        P("dp", "seq", None),
        P("dp", None, None),
        P(),
        P(None, "dp", "seq"),
        P(),
        P(None, None, "tensor"),
        P(None, "tensor"),
        P("tensor", None),
        P(None, "tensor"),
        P(),
        P(),
        P(None, "tensor"),
        P(None, None, "tensor"),
        P(None, "tensor"),
        P("tensor", None),
        P(None, "tensor"),
        P("tensor"),
        P("tensor", None),
        P(),
    )
    return jax.shard_map(
        shards,
        mesh=mesh,
        in_specs=placed,
        out_specs=(
            P("dp", "seq", None),
            P(),
            P("dp", "seq", None),
            P("dp", "seq", None),
            P("dp", None, None),
            P(),
            P(None, ("dp", "seq"), "tensor"),
            P(None, "tensor"),
            P("tensor", ("dp", "seq")),
            P(None, "tensor"),
            P(),
            P(),
            P(("dp", "seq"), "tensor"),
            P(None, ("dp", "seq"), "tensor"),
            P(None, "tensor"),
            P("tensor", ("dp", "seq")),
            P(("dp", "seq"), "tensor"),
            P("tensor"),
            P("tensor", ("dp", "seq")),
            P(),
        ),
        check_vma=False,
    )
```

```python
import functools
import math

import jax
import jax.numpy as jnp
from jax import lax
from jax.experimental import pallas as pl
from jax.experimental.pallas import tpu as pltpu
from jax.sharding import PartitionSpec as P

HEAD_DIM = 128
LOW = jnp.bfloat16
WIDE = jnp.float32


eps_norm = 1e-06


def layer_norm(values):
    centred = values - jnp.mean(values, axis=-1, keepdims=True)
    return centred * lax.rsqrt(jnp.mean(centred * centred, axis=-1, keepdims=True) + eps_norm)


def gelu_tanh(values):
    return (
        0.5
        * values
        * (1.0 + jnp.tanh(0.7978845608028654 * (values + 0.044715 * values * values * values)))
    )


def rope_tables(positions, head_size):
    sixth_part = head_size // 6
    part_spans = (head_size - 4 * sixth_part, 2 * sixth_part, 2 * sixth_part)
    pieces = []
    for axis_no in range(3):
        span_now = part_spans[axis_no]
        inverse = 1.0 / 10000.0 ** (jnp.arange(0, span_now, 2).astype(jnp.float32) / span_now)
        pieces.append(positions[axis_no].astype(jnp.float32)[..., None] * inverse)
    angles = jnp.concatenate(pieces, axis=-1)
    cosine_rep = jnp.repeat(jnp.cos(angles), 2, axis=-1)[..., None, :]
    sine_rep = jnp.repeat(jnp.sin(angles), 2, axis=-1)[..., None, :]
    return (cosine_rep, sine_rep)


def swap_table(head_size):
    row_no = jnp.arange(head_size)[:, None]
    col_no = jnp.arange(head_size)[None, :]
    upward = jnp.where((row_no % 2 == 0) & (col_no == row_no + 1), 1.0, 0.0)
    downward = jnp.where((row_no % 2 == 1) & (col_no == row_no - 1), -1.0, 0.0)
    return (upward + downward).astype(jnp.float32)


def rotate(values, cosine_rep, sine_rep, swap_matrix):
    swapped = jnp.matmul(values, swap_matrix, precision=lax.Precision.HIGHEST)
    return values * cosine_rep + swapped * sine_rep


def line_kernel(count, block, group, lag, lag2, turned, *refs):
    lhs_refs = refs[:count]
    rhs_refs = refs[count:2 * count]
    out_ref, raw, part, stage, cross, raw_s, raw_r, mid_s, mid_r, far_s, far_r, near_s, near_r = refs[2 * count:]
    steps = out_ref.shape[0] // block
    me = lax.axis_index("tensor")
    inner = (me == 1) | (me == 2)
    outer = jnp.logical_not(inner)
    leaf = jnp.where(me < 2, 0, 3)
    hub = jnp.where(me < 2, 1, 2)
    mate = 3 - me
    side = jnp.where(me < 2, 0, 1)

    def signal(where):
        pl.semaphore_signal(
            pltpu.get_barrier_semaphore(), inc=1, device_id={"tensor": where},
            device_id_type=pl.DeviceIdType.MESH)

    @pl.when(outer)
    def _():
        signal(hub)
        pl.semaphore_wait(pltpu.get_barrier_semaphore(), 1)

    @pl.when(inner)
    def _():
        signal(leaf)
        signal(mate)
        pl.semaphore_wait(pltpu.get_barrier_semaphore(), 2)

    def rows_of(step):
        return pl.ds(pl.multiple_of(step * block, 16), block)

    def remote(src, dst, send, recv, step, where):
        at = rows_of(step)
        return pltpu.make_async_remote_copy(
            src_ref=src.at[at], dst_ref=dst.at[at], send_sem=send.at[step], recv_sem=recv.at[step],
            device_id={"tensor": where}, device_id_type=pl.DeviceIdType.MESH)

    def raw_copy(step):
        return remote(raw, raw, raw_s, raw_r, step, hub)

    def mid_copy(step):
        return remote(stage, cross, mid_s, mid_r, step, mate)

    def far_copy(step):
        return remote(out_ref, out_ref, far_s, far_r, step, mate)

    def near_copy(step):
        return remote(out_ref, out_ref, near_s, near_r, step, leaf)

    def body(step, carry):
        @pl.when((step < steps) & (lax.rem(step, group) == 0))
        def _():
            at = pl.ds(pl.multiple_of(step * block, 16), block * group)
            total = None
            for lhs, rhs in zip(lhs_refs, rhs_refs):
                term = lax.dot_general(lhs[at], rhs[...], (((1,), (1 if turned else 0,)), ((), ())),
                    preferred_element_type=WIDE)
                total = term if total is None else total + term
            part[at] = total

        @pl.when(outer & (step < steps))
        def _():
            at = rows_of(step)
            raw[at] = part[at].astype(LOW)
            raw_copy(step).start()

        late = step - lag2
        @pl.when(inner & (late >= 0) & (late < steps) & (lax.rem(late + 2 * lag2, 2) != side))
        def _():
            far_copy(late).wait_recv()
            near_copy(late).start()

        near = step - lag
        @pl.when(inner & (near >= 0) & (near < steps) & (lax.rem(near + 2 * lag2, 2) == side))
        def _():
            at = rows_of(near)
            mid_copy(near).wait_recv()
            out_ref[at] = (part[at] + cross[at].astype(WIDE)).astype(LOW)
            far_copy(near).start()
            near_copy(near).start()

        @pl.when(inner & (step < steps))
        def _():
            at = rows_of(step)
            raw_copy(step).wait_recv()

            @pl.when(lax.rem(step, 2) == side)
            def _():
                part[at] = part[at] + raw[at].astype(WIDE)

            @pl.when(lax.rem(step, 2) != side)
            def _():
                stage[at] = (part[at] + raw[at].astype(WIDE)).astype(LOW)
                mid_copy(step).start()

        return carry

    lax.fori_loop(0, steps + lag2, body, 0)

    def drain(step, carry):
        @pl.when(outer)
        def _():
            near_copy(step).wait_recv()
            raw_copy(step).wait_send()

        @pl.when(inner)
        def _():
            near_copy(step).wait_send()

            @pl.when(lax.rem(step, 2) == side)
            def _():
                far_copy(step).wait_send()

            @pl.when(lax.rem(step, 2) != side)
            def _():
                mid_copy(step).wait_send()

        return carry

    lax.fori_loop(0, steps, drain, 0)

def line_sum(pairs, turned, ident, true_rows, block=16, group=7, lag=4, lag2=8):
    width = pairs[0][1].shape[0 if turned else 1]
    unit = block * group
    rows = -(-true_rows // unit) * unit
    pairs = [
        (jnp.pad(lhs, ((0, max(rows - lhs.shape[0], 0)), (0, 0))), rhs) for lhs, rhs in pairs
    ]
    steps = rows // block
    dma = pltpu.SemaphoreType.DMA
    depth = sum(p[0].shape[1] for p in pairs)
    return pl.pallas_call(
        functools.partial(line_kernel, len(pairs), block, group, lag, lag2, turned),
        out_shape=jax.ShapeDtypeStruct((rows, width), LOW),
        in_specs=[pl.BlockSpec(memory_space=pltpu.VMEM)] * (2 * len(pairs)),
        out_specs=pl.BlockSpec(memory_space=pltpu.VMEM),
        scratch_shapes=[
            pltpu.VMEM((rows, width), LOW),
            pltpu.VMEM((rows, width), WIDE),
            pltpu.VMEM((rows, width), LOW),
            pltpu.VMEM((rows, width), LOW),
        ] + [dma((steps,))] * 8,
        compiler_params=pltpu.CompilerParams(collective_id=ident, has_side_effects=True, vmem_limit_bytes=60 << 20),
        cost_estimate=pl.CostEstimate(flops=2 * rows * width * depth, bytes_accessed=230 * 10**6, transcendentals=0),
        name=f"line_sum_{ident}",
    )(*[p[0] for p in pairs], *[p[1] for p in pairs])[:true_rows].astype(WIDE)

def scatter_rows(mix, dimension):
    return lax.psum_scatter(mix, ("dp", "seq"), scatter_dimension=dimension, tiled=True)


def plane_sum_kernel(seq_count, value_ref, seq_ref, all_ref, slots, send_sem, recv_sem):
    count = slots.shape[0]
    dp = lax.axis_index("dp")
    me = dp * seq_count + lax.axis_index("seq")

    def device(place):
        return {"dp": place // seq_count, "seq": lax.rem(place, seq_count)}

    barrier = pltpu.get_barrier_semaphore()
    for hop in range(1, count):
        pl.semaphore_signal(
            barrier, inc=1, device_id=device(lax.rem(me + hop, count)),
            device_id_type=pl.DeviceIdType.MESH)
    pl.semaphore_wait(barrier, count - 1)

    def copy(slot, hop, place):
        return pltpu.make_async_remote_copy(
            src_ref=value_ref, dst_ref=slots.at[slot], send_sem=send_sem.at[hop - 1],
            recv_sem=recv_sem.at[hop - 1], device_id=device(place),
            device_id_type=pl.DeviceIdType.MESH)

    for hop in range(1, count):
        copy(me, hop, lax.rem(me + hop, count)).start()
    slots[pl.ds(me, 1)] = value_ref[...][None]
    for hop in range(1, count):
        origin = lax.rem(me + count - hop, count)
        copy(origin, hop, origin).wait_recv()
    for hop in range(1, count):
        copy(me, hop, lax.rem(me + hop, count)).wait_send()

    def span(start):
        total = slots[start].astype(WIDE)
        for slot in range(1, seq_count):
            total = total + slots[start + slot].astype(WIDE)
        return total

    seq_ref[...] = span(dp * seq_count)
    total = span(0)
    for part in range(1, count // seq_count):
        total = total + span(part * seq_count)
    all_ref[...] = total


def plane_sum(first, values, ident):
    seq_count = lax.axis_size("seq")
    count = lax.axis_size("dp") * seq_count
    flat = jnp.concatenate([value.reshape(-1).astype(LOW) for value in [first] + values])
    size = flat.shape[0]
    lines = -(-size // 2048) * 16
    packed = jnp.pad(flat, (0, lines * 128 - size)).reshape(lines, 128)
    vmem = pl.BlockSpec(memory_space=pltpu.VMEM)
    seq_total, all_total = pl.pallas_call(
        functools.partial(plane_sum_kernel, seq_count),
        out_shape=(jax.ShapeDtypeStruct((lines, 128), WIDE),) * 2,
        in_specs=[vmem],
        out_specs=(vmem, vmem),
        scratch_shapes=[
            pltpu.VMEM((count, lines, 128), LOW),
            pltpu.SemaphoreType.DMA((count - 1,)),
            pltpu.SemaphoreType.DMA((count - 1,)),
        ],
        compiler_params=pltpu.CompilerParams(collective_id=ident, has_side_effects=True),
        name="plane_sum",
    )(packed)
    all_total = all_total.reshape(-1)
    first_pair = (
        seq_total.reshape(-1)[: first.size].reshape(first.shape),
        all_total[: first.size].reshape(first.shape),
    )
    outs = []
    start = first.size
    for value in values:
        outs.append(all_total[start : start + value.size].reshape(value.shape))
        start += value.size
    return first_pair, outs


def small_kernel(value_ref, out_ref, slots, send_sem, recv_sem):
    count = slots.shape[0]
    me = lax.axis_index("tensor")
    barrier = pltpu.get_barrier_semaphore()
    for hop in range(1, count):
        pl.semaphore_signal(
            barrier, inc=1, device_id={"tensor": lax.rem(me + hop, count)},
            device_id_type=pl.DeviceIdType.MESH)
    pl.semaphore_wait(barrier, count - 1)
    copies = []
    for hop in range(1, count):
        copy = pltpu.make_async_remote_copy(
            src_ref=value_ref, dst_ref=slots.at[me], send_sem=send_sem.at[hop - 1],
            recv_sem=recv_sem.at[hop - 1], device_id={"tensor": lax.rem(me + hop, count)},
            device_id_type=pl.DeviceIdType.MESH)
        copy.start()
        copies.append(copy)
    slots[pl.ds(me, 1)] = value_ref[...][None]
    for hop in range(1, count):
        origin = lax.rem(me + count - hop, count)
        pltpu.make_async_remote_copy(
            src_ref=value_ref, dst_ref=slots.at[origin], send_sem=send_sem.at[hop - 1],
            recv_sem=recv_sem.at[hop - 1], device_id={"tensor": origin},
            device_id_type=pl.DeviceIdType.MESH).wait_recv()
    for copy in copies:
        copy.wait_send()
    total = slots[0]
    for slot in range(1, count):
        total = total + slots[slot]
    out_ref[...] = total


def small_sum(values, ident):
    count = lax.axis_size("tensor")
    flat = jnp.concatenate([value.reshape(-1) for value in values])
    size = flat.shape[0]
    lines = -(-size // 1024) * 8
    packed = jnp.pad(flat, (0, lines * 128 - size)).reshape(lines, 128)
    summed = pl.pallas_call(
        small_kernel,
        out_shape=jax.ShapeDtypeStruct((lines, 128), WIDE),
        in_specs=[pl.BlockSpec(memory_space=pltpu.VMEM)],
        out_specs=pl.BlockSpec(memory_space=pltpu.VMEM),
        scratch_shapes=[
            pltpu.VMEM((count, lines, 128), WIDE),
            pltpu.SemaphoreType.DMA((count - 1,)),
            pltpu.SemaphoreType.DMA((count - 1,)),
        ],
        compiler_params=pltpu.CompilerParams(collective_id=ident, has_side_effects=True),
        name=f"small_sum_{ident}",
    )(packed).reshape(-1)
    outs = []
    start = 0
    for value in values:
        outs.append(summed[start : start + value.size].reshape(value.shape))
        start += value.size
    return outs


LOG2E = 1.4426950408889634
HIDDEN_SCORE = -1e30


def plane_places():
    me = lax.axis_index("seq")
    column = lax.rem(me, 2)
    line = me // 2
    return (me, me + 1 - 2 * column, me + 2 - 4 * line, 3 - me)


def plane_barrier(places):
    barrier = pltpu.get_barrier_semaphore()
    for place in places[1:]:
        pl.semaphore_signal(
            barrier, inc=1, device_id={"seq": place}, device_id_type=pl.DeviceIdType.MESH
        )
    pl.semaphore_wait(barrier, 3)


def plane_copy(src, dst, send, recv, place):
    return pltpu.make_async_remote_copy(
        src_ref=src,
        dst_ref=dst,
        send_sem=send,
        recv_sem=recv,
        device_id={"seq": place},
        device_id_type=pl.DeviceIdType.MESH,
    )


def head_lanes(head):
    return pl.ds(pl.multiple_of(head * HEAD_DIM, 128), HEAD_DIM)


def block_valid(key_rows, owner, true_rows, length):
    row = lax.broadcasted_iota(jnp.int32, (key_rows, 1), 0)
    return (row < true_rows) & (owner * true_rows + row < length)


def over_last(lhs, rhs):
    return lax.dot_general(lhs, rhs, (((1,), (1,)), ((), ())), preferred_element_type=WIDE)


def attend_kernel(
    true_rows, length_ref, query_ref, kv_ref, out_ref, turned_ref, total_ref, got_ref, peak, summed, send, recv
):
    places = plane_places()
    plane_barrier(places)
    heads = query_ref.shape[1] // HEAD_DIM
    key_rows = kv_ref.shape[1]
    length = length_ref[0]
    factor = LOG2E / math.sqrt(HEAD_DIM)

    def own_copy(relation, part):
        index = 2 * relation + part
        return plane_copy(
            kv_ref.at[part], got_ref.at[relation, part], send.at[index], recv.at[index], places[relation + 1]
        )

    key_pass = plane_copy(got_ref.at[0, 0], got_ref.at[2, 0], send.at[4], recv.at[4], places[2])
    value_pass = plane_copy(got_ref.at[1, 1], got_ref.at[2, 1], send.at[5], recv.at[5], places[1])
    for part in range(2):
        for relation in range(2):
            own_copy(relation, part).start()

    peak[...] = jnp.full(peak.shape, HIDDEN_SCORE, WIDE)
    summed[...] = jnp.zeros(summed.shape, WIDE)
    turned_ref[...] = jnp.zeros(turned_ref.shape, WIDE)

    def block(source, owner):
        def step(head, carry):
            lanes = head_lanes(head)
            scores = over_last(source(0, lanes), query_ref[:, lanes]) * factor
            scores = jnp.where(block_valid(key_rows, owner, true_rows, length), scores, HIDDEN_SCORE)
            before = peak[head]
            after = jnp.maximum(before, jnp.max(scores, axis=0, keepdims=True))
            shrink = jnp.exp2(before - after)
            terms = jnp.exp2(scores - after)
            peak[head] = after
            summed[head] = summed[head] * shrink + jnp.sum(terms, axis=0, keepdims=True)
            turned_ref[head] = turned_ref[head] * shrink + lax.dot_general(
                source(1, lanes),
                terms.astype(LOW),
                (((0,), (0,)), ((), ())),
                preferred_element_type=WIDE,
            )

            return carry

        lax.fori_loop(0, heads, step, 0)

    block(lambda part, lanes: kv_ref[part, :, lanes], places[0])
    own_copy(0, 0).wait_recv()
    key_pass.start()
    own_copy(0, 1).wait_recv()
    own_copy(1, 1).wait_recv()
    value_pass.start()
    own_copy(1, 0).wait_recv()
    for relation in range(3):
        if relation == 2:
            key_pass.wait_recv()
            value_pass.wait_recv()
        block(
            lambda part, lanes, relation=relation: got_ref[relation, part, :, lanes],
            places[relation + 1],
        )

    for head in range(heads):
        lanes = slice(head * HEAD_DIM, (head + 1) * HEAD_DIM)
        attended = turned_ref[head] / summed[head]
        turned_ref[head] = attended
        out_ref[:, lanes] = jnp.transpose(attended).astype(LOW)
        total_ref[head] = peak[head] + jnp.log2(summed[head])
    for part in range(2):
        for relation in range(2):
            own_copy(relation, part).wait_send()
    key_pass.wait_send()
    value_pass.wait_send()


def attend(query_low, kv_low, length, true_rows, ident):
    rows, width = query_low.shape
    heads = width // HEAD_DIM
    key_rows = kv_low.shape[1]
    dma = pltpu.SemaphoreType.DMA
    vmem = pl.BlockSpec(memory_space=pltpu.VMEM)
    return pl.pallas_call(
        functools.partial(attend_kernel, true_rows),
        out_shape=(
            jax.ShapeDtypeStruct((rows, width), LOW),
            jax.ShapeDtypeStruct((heads, HEAD_DIM, rows), WIDE),
            jax.ShapeDtypeStruct((heads, 1, rows), WIDE),
            jax.ShapeDtypeStruct((3, 2, key_rows, width), LOW),
        ),
        in_specs=[pl.BlockSpec(memory_space=pltpu.SMEM), vmem, vmem],
        out_specs=(vmem,) * 4,
        scratch_shapes=[
            pltpu.VMEM((heads, 1, rows), WIDE),
            pltpu.VMEM((heads, 1, rows), WIDE),
            dma((6,)),
            dma((6,)),
        ],
        compiler_params=pltpu.CompilerParams(
            collective_id=ident, has_side_effects=True, vmem_limit_bytes=56 << 20
        ),
        cost_estimate=pl.CostEstimate(flops=10**9, bytes_accessed=150 * 10**6, transcendentals=0),
        name="attend",
    )(length, query_low, kv_low)


def attend_back_kernel(
    true_rows, length_ref, query_ref, kv_ref, got_ref, turned_ref, total_ref, grad_ref,
    query_grad_ref, kv_grad_ref, centre, query_turned, leaving, landing, send, recv,
):
    places = plane_places()
    plane_barrier(places)
    heads = query_ref.shape[1] // HEAD_DIM
    key_rows = kv_ref.shape[1]
    length = length_ref[0]
    scale = 1.0 / math.sqrt(HEAD_DIM)
    for head in range(heads):
        lanes = slice(head * HEAD_DIM, (head + 1) * HEAD_DIM)
        grads = jnp.transpose(grad_ref[:, lanes].astype(WIDE))
        centre[head] = jnp.sum(grads * turned_ref[head], axis=0, keepdims=True)
    query_turned[...] = jnp.zeros(query_turned.shape, WIDE)
    spare = query_ref.shape[0] - key_rows
    kv_grad_ref[:, pl.ds(key_rows, spare), :] = jnp.zeros((2, spare, query_ref.shape[1]), WIDE)

    def block(source, sink, owner):
        def step(head, carry):
            lanes = head_lanes(head)
            keys = source(0, lanes)
            query = query_ref[:, lanes]
            grads = grad_ref[:, lanes]
            probs = jnp.exp2(over_last(keys, query) * (scale * LOG2E) - total_ref[head])
            probs = jnp.where(block_valid(key_rows, owner, true_rows, length), probs, 0.0)
            grad_probs = over_last(source(1, lanes), grads)
            grad_scores = (probs * (grad_probs - centre[head])).astype(LOW)
            sink(0, lanes, jnp.dot(grad_scores, query, preferred_element_type=WIDE) * scale)
            sink(1, lanes, jnp.dot(probs.astype(LOW), grads, preferred_element_type=WIDE))
            query_turned[head] = query_turned[head] + lax.dot_general(
                keys, grad_scores, (((0,), (0,)), ((), ())), preferred_element_type=WIDE
            )

            return carry

        lax.fori_loop(0, heads, step, 0)

    def grad_copy(relation, part):
        return plane_copy(
            leaving.at[relation, part],
            landing.at[relation, part],
            send.at[relation, part],
            recv.at[relation, part],
            places[relation + 1],
        )

    for relation in (2, 1, 0):

        def sink(part, lanes, value, relation=relation):
            leaving[relation, part, :, lanes] = value.astype(LOW)

        block(
            lambda part, lanes, relation=relation: got_ref[relation, part, :, lanes],
            sink,
            places[relation + 1],
        )
        for part in range(2):
            grad_copy(relation, part).start()

    def own_sink(part, lanes, value):
        kv_grad_ref[part, pl.ds(0, key_rows), lanes] = value

    block(lambda part, lanes: kv_ref[part, :, lanes], own_sink, places[0])
    for head in range(heads):
        lanes = slice(head * HEAD_DIM, (head + 1) * HEAD_DIM)
        query_grad_ref[:, lanes] = jnp.transpose(query_turned[head]) * scale
    for relation in (2, 1, 0):
        for part in range(2):
            grad_copy(relation, part).wait_recv()

    def gather(tile, carry):
        rows = pl.ds(pl.multiple_of(tile * 16, 16), 16)
        for part in range(2):
            total = kv_grad_ref[part, rows]
            for relation in range(3):
                total = total + landing[relation, part, rows].astype(WIDE)
            kv_grad_ref[part, rows] = total
        return carry

    lax.fori_loop(0, key_rows // 16, gather, 0)
    for relation in range(3):
        for part in range(2):
            grad_copy(relation, part).wait_send()


def attend_back(query_low, kv_low, got, turned, total, grad_low, length, true_rows, ident):
    rows, width = query_low.shape
    heads = width // HEAD_DIM
    key_rows = kv_low.shape[1]
    dma = pltpu.SemaphoreType.DMA
    vmem = pl.BlockSpec(memory_space=pltpu.VMEM)
    return pl.pallas_call(
        functools.partial(attend_back_kernel, true_rows),
        out_shape=(
            jax.ShapeDtypeStruct((rows, width), WIDE),
            jax.ShapeDtypeStruct((2, rows, width), WIDE),
        ),
        in_specs=[pl.BlockSpec(memory_space=pltpu.SMEM)] + [vmem] * 6,
        out_specs=(vmem,) * 2,
        scratch_shapes=[
            pltpu.VMEM((heads, 1, rows), WIDE),
            pltpu.VMEM((heads, HEAD_DIM, rows), WIDE),
            pltpu.VMEM((3, 2, key_rows, width), LOW),
            pltpu.VMEM((3, 2, key_rows, width), LOW),
            dma((3, 2)),
            dma((3, 2)),
        ],
        compiler_params=pltpu.CompilerParams(
            collective_id=ident, has_side_effects=True, vmem_limit_bytes=56 << 20
        ),
        cost_estimate=pl.CostEstimate(flops=10**9, bytes_accessed=200 * 10**6, transcendentals=0),
        name="attend_back",
    )(length, query_low, kv_low, got, turned, total, grad_low)


def pair_swap(values):
    lane = lax.broadcasted_iota(jnp.int32, values.shape, 1)
    return jnp.where(
        lax.rem(lane, 2) == 0,
        pltpu.roll(values, HEAD_DIM - 1, axis=1),
        pltpu.roll(values, 1, axis=1),
    )


def rows_to_lanes(values):
    return jnp.sum(jnp.transpose(values), axis=0, keepdims=True)


def lanes_to_rows(row):
    return jnp.transpose(jnp.broadcast_to(row, (HEAD_DIM, row.shape[1])))


def tensor_barrier():
    count = lax.axis_size("tensor")
    me = lax.axis_index("tensor")
    barrier = pltpu.get_barrier_semaphore()
    for hop in range(1, count):
        pl.semaphore_signal(
            barrier, inc=1, device_id={"tensor": lax.rem(me + hop, count)},
            device_id_type=pl.DeviceIdType.MESH)
    pl.semaphore_wait(barrier, count - 1)


def tensor_copy(stage, slots, send, recv, slot, hop, place):
    return pltpu.make_async_remote_copy(
        src_ref=stage, dst_ref=slots.at[slot], send_sem=send.at[hop - 1],
        recv_sem=recv.at[hop - 1], device_id={"tensor": place},
        device_id_type=pl.DeviceIdType.MESH)


def tensor_send(stage, slots, send, recv):
    count = slots.shape[0]
    me = lax.axis_index("tensor")
    for hop in range(1, count):
        tensor_copy(stage, slots, send, recv, me, hop, lax.rem(me + hop, count)).start()
    slots[pl.ds(me, 1)] = stage[...][None]


def tensor_collect(stage, slots, send, recv):
    count = slots.shape[0]
    me = lax.axis_index("tensor")
    for hop in range(1, count):
        origin = lax.rem(me + count - hop, count)
        tensor_copy(stage, slots, send, recv, origin, hop, origin).wait_recv()
    for hop in range(1, count):
        tensor_copy(stage, slots, send, recv, me, hop, lax.rem(me + hop, count)).wait_send()
    total = slots[0]
    for slot in range(1, count):
        total = total + slots[slot]
    return total


def project_kernel(
    rows_ref, weight_ref, bias_ref, gain_ref, cosine_ref, sine_ref,
    pre_ref, query_ref, kv_ref, square_ref, stage, slots, send, recv,
):
    heads = query_ref.shape[1] // HEAD_DIM
    key_rows = kv_ref.shape[1]
    width = rows_ref.shape[1]
    tensor_barrier()
    stage[...] = jnp.zeros(stage.shape, WIDE)
    for part in range(2):
        pre_ref[part] = (
            jnp.dot(rows_ref[...], weight_ref[part], preferred_element_type=WIDE)
            + bias_ref[part : part + 1]
        )
        squares = None
        for head in range(heads):
            piece = pre_ref[part, :, head * HEAD_DIM : (head + 1) * HEAD_DIM]
            squares = piece * piece if squares is None else squares + piece * piece
        stage[part : part + 1] = rows_to_lanes(squares)
    tensor_send(stage, slots, send, recv)
    values = jnp.dot(rows_ref[...], weight_ref[2], preferred_element_type=WIDE) + bias_ref[2:3]
    kv_ref[1] = values[:key_rows].astype(LOW)
    total = tensor_collect(stage, slots, send, recv)
    square_ref[...] = total
    for part in range(2):
        rate = lanes_to_rows(lax.rsqrt(total[part : part + 1] / width + eps_norm))
        for head in range(heads):
            lanes = slice(head * HEAD_DIM, (head + 1) * HEAD_DIM)
            normed = pre_ref[part, :, lanes] * rate * gain_ref[part : part + 1, lanes]
            turned = normed * cosine_ref[...] + pair_swap(normed) * sine_ref[...]
            if part == 0:
                query_ref[:, lanes] = turned.astype(LOW)
            else:
                kv_ref[0, :, lanes] = turned[:key_rows].astype(LOW)


def project(rows_low, weights, bias, gains, cosine, sine, key_rows, ident):
    rows = rows_low.shape[0]
    width = weights.shape[2]
    count = lax.axis_size("tensor")
    vmem = pl.BlockSpec(memory_space=pltpu.VMEM)
    dma = pltpu.SemaphoreType.DMA
    return pl.pallas_call(
        project_kernel,
        out_shape=(
            jax.ShapeDtypeStruct((2, rows, width), WIDE),
            jax.ShapeDtypeStruct((rows, width), LOW),
            jax.ShapeDtypeStruct((2, key_rows, width), LOW),
            jax.ShapeDtypeStruct((8, rows), WIDE),
        ),
        in_specs=[vmem] * 6,
        out_specs=(vmem,) * 4,
        scratch_shapes=[
            pltpu.VMEM((8, rows), WIDE),
            pltpu.VMEM((count, 8, rows), WIDE),
            dma((count - 1,)),
            dma((count - 1,)),
        ],
        compiler_params=pltpu.CompilerParams(
            collective_id=ident, has_side_effects=True, vmem_limit_bytes=56 << 20
        ),
        name="project",
    )(rows_low, weights, bias, gains, cosine, sine)


def unproject_kernel(
    width, query_grad_ref, kv_grad_ref, pre_ref, square_ref, gain_ref, cosine_ref, sine_ref,
    query_low_ref, key_low_ref, value_low_ref, sums_ref, work, stage, slots, send, recv,
):
    heads = query_grad_ref.shape[1] // HEAD_DIM
    tensor_barrier()
    stage[...] = jnp.zeros(stage.shape, WIDE)
    sums_ref[...] = jnp.zeros(sums_ref.shape, WIDE)
    total = square_ref[...]
    for part in range(2):
        terms = None
        rate = lanes_to_rows(lax.rsqrt(total[part : part + 1] / width + eps_norm))
        for head in range(heads):
            lanes = slice(head * HEAD_DIM, (head + 1) * HEAD_DIM)
            grads = query_grad_ref[:, lanes] if part == 0 else kv_grad_ref[0, :, lanes]
            grads = grads * cosine_ref[...] - pair_swap(grads) * sine_ref[...]
            pre = pre_ref[part, :, lanes]
            sums_ref[3 + part : 4 + part, lanes] = jnp.sum(
                grads * pre * rate, axis=0, keepdims=True
            )
            grads = grads * gain_ref[part : part + 1, lanes]
            work[part, :, lanes] = grads
            terms = grads * pre if terms is None else terms + grads * pre
        stage[part : part + 1] = rows_to_lanes(terms)
    tensor_send(stage, slots, send, recv)
    values = kv_grad_ref[1]
    sums_ref[2:3] = jnp.sum(values, axis=0, keepdims=True)
    value_low_ref[...] = values.astype(LOW)
    back_total = tensor_collect(stage, slots, send, recv)
    for part in range(2):
        rate_row = lax.rsqrt(total[part : part + 1] / width + eps_norm)
        rate = lanes_to_rows(rate_row)
        back = lanes_to_rows(rate_row * rate_row * rate_row * back_total[part : part + 1] / width)
        for head in range(heads):
            lanes = slice(head * HEAD_DIM, (head + 1) * HEAD_DIM)
            grads = work[part, :, lanes] * rate - pre_ref[part, :, lanes] * back
            sums_ref[part : part + 1, lanes] = jnp.sum(grads, axis=0, keepdims=True)
            if part == 0:
                query_low_ref[:, lanes] = grads.astype(LOW)
            else:
                key_low_ref[:, lanes] = grads.astype(LOW)


def unproject(query_grads, kv_grads, pre, squares, gains, cosine, sine, model_width, ident):
    rows, width = query_grads.shape
    count = lax.axis_size("tensor")
    vmem = pl.BlockSpec(memory_space=pltpu.VMEM)
    dma = pltpu.SemaphoreType.DMA
    return pl.pallas_call(
        functools.partial(unproject_kernel, model_width),
        out_shape=(jax.ShapeDtypeStruct((rows, width), LOW),) * 3
        + (jax.ShapeDtypeStruct((8, width), WIDE),),
        in_specs=[vmem] * 7,
        out_specs=(vmem,) * 4,
        scratch_shapes=[
            pltpu.VMEM((2, rows, width), WIDE),
            pltpu.VMEM((8, rows), WIDE),
            pltpu.VMEM((count, 8, rows), WIDE),
            dma((count - 1,)),
            dma((count - 1,)),
        ],
        compiler_params=pltpu.CompilerParams(
            collective_id=ident, has_side_effects=True, vmem_limit_bytes=56 << 20
        ),
        name="unproject",
    )(query_grads, kv_grads, pre, squares, gains, cosine, sine)


def seq_scatter_kernel(blocks_ref, out_ref, slots, send_sem, recv_sem):
    count = slots.shape[0]
    me = lax.axis_index("seq")
    barrier = pltpu.get_barrier_semaphore()
    for hop in range(1, count):
        pl.semaphore_signal(
            barrier, inc=1, device_id={"seq": lax.rem(me + hop, count)},
            device_id_type=pl.DeviceIdType.MESH)
    pl.semaphore_wait(barrier, count - 1)

    def copy(block, slot, hop, place):
        return pltpu.make_async_remote_copy(
            src_ref=blocks_ref.at[block], dst_ref=slots.at[slot], send_sem=send_sem.at[hop - 1],
            recv_sem=recv_sem.at[hop - 1], device_id={"seq": place},
            device_id_type=pl.DeviceIdType.MESH)

    for hop in range(1, count):
        place = lax.rem(me + hop, count)
        copy(place, me, hop, place).start()
    slots[pl.ds(me, 1)] = blocks_ref[pl.ds(me, 1)]
    for hop in range(1, count):
        origin = lax.rem(me + count - hop, count)
        copy(me, origin, hop, origin).wait_recv()
    for hop in range(1, count):
        place = lax.rem(me + hop, count)
        copy(place, me, hop, place).wait_send()
    total = slots[0].astype(WIDE)
    for slot in range(1, count):
        total = total + slots[slot].astype(WIDE)
    out_ref[...] = total


def seq_scatter(blocks, ident):
    count, rows, width = blocks.shape
    vmem = pl.BlockSpec(memory_space=pltpu.VMEM)
    return pl.pallas_call(
        seq_scatter_kernel,
        out_shape=jax.ShapeDtypeStruct((rows, width), WIDE),
        in_specs=[vmem],
        out_specs=vmem,
        scratch_shapes=[
            pltpu.VMEM((count, rows, width), LOW),
            pltpu.SemaphoreType.DMA((count - 1,)),
            pltpu.SemaphoreType.DMA((count - 1,)),
        ],
        compiler_params=pltpu.CompilerParams(collective_id=ident, has_side_effects=True),
        name="seq_scatter",
    )(blocks)


def head_forward(query, keys, values, key_ok, score_scale):
    scores = (
        jnp.einsum("csh,clh->csl", query, keys, preferred_element_type=jnp.float32) * score_scale
    )
    scores = jnp.where(key_ok[:, None, :], scores, -jnp.inf)
    row_peak = jnp.max(scores, axis=-1, keepdims=True)
    exp_terms = jnp.exp(scores - row_peak)
    summed = jnp.sum(exp_terms, axis=-1, keepdims=True)
    probs_low = (exp_terms / summed).astype(jnp.bfloat16)
    attended = jnp.einsum("csl,clh->csh", probs_low, values, preferred_element_type=jnp.float32)
    return (attended, row_peak[..., 0] + jnp.log(summed[..., 0]))


def head_backward(query, keys, values, key_ok, log_total, grad_att, score_scale):
    scores = (
        jnp.einsum("csh,clh->csl", query, keys, preferred_element_type=jnp.float32) * score_scale
    )
    probs = jnp.where(key_ok[:, None, :], jnp.exp(scores - log_total[..., None]), 0.0)
    grad_probs = jnp.einsum("csh,clh->csl", grad_att, values, preferred_element_type=jnp.float32)
    centre = jnp.sum(probs * grad_probs, axis=-1)
    grad_scores = (probs * (grad_probs - centre[..., None])).astype(jnp.bfloat16)
    grad_query = (
        jnp.einsum("csl,clh->csh", grad_scores, keys, preferred_element_type=jnp.float32)
        * score_scale
    )
    grad_keys = (
        jnp.einsum("csl,csh->clh", grad_scores, query, preferred_element_type=jnp.float32)
        * score_scale
    )
    grad_values = jnp.einsum(
        "csl,csh->clh", probs.astype(jnp.bfloat16), grad_att, preferred_element_type=jnp.float32
    )
    return (grad_query, centre, grad_keys, grad_values)


def shards(
    hidden,
    teacher,
    text,
    time_embed,
    lengths,
    positions,
    modulation,
    self_in,
    self_bias,
    self_out,
    norm_gains,
    cross_gain,
    cross_shift,
    cross_q,
    cross_kv,
    cross_bias,
    cross_out,
    ffn_in,
    ffn_in_bias,
    ffn_out,
    out_bias,
):
    low_type = jnp.bfloat16
    wide_type = jnp.float32
    clip_count, seq_rows, model_width = hidden.shape
    local_width = self_in.shape[2]
    local_heads = local_width // HEAD_DIM
    text_local = text.shape[1]
    seq_count = lax.axis_size("seq")
    slot_count = seq_rows * seq_count
    text_count = text_local * seq_count
    flat_rows = clip_count * seq_rows
    score_scale = 1.0 / math.sqrt(HEAD_DIM)
    seq_place = lax.axis_index("seq")
    clip_first = lax.axis_index("dp") * clip_count
    clip_lengths = lax.dynamic_slice_in_dim(lengths, clip_first, clip_count)
    key_valid = jnp.arange(slot_count, dtype=jnp.int32)[None, :] < clip_lengths[:, None]
    row_ids = seq_place * seq_rows + jnp.arange(seq_rows, dtype=jnp.int32)
    row_valid = row_ids[None, :] < clip_lengths[:, None]
    text_valid = jnp.ones((clip_count, text_count), dtype=jnp.bool_)
    valid_total = jnp.sum(lengths).astype(wide_type)
    modulated = modulation[None] + time_embed
    cosine_rep, sine_rep = rope_tables(positions, HEAD_DIM)
    rotate_now = functools.partial(
        rotate, cosine_rep=cosine_rep, sine_rep=sine_rep, swap_matrix=swap_table(HEAD_DIM)
    )
    head_shape = (clip_count, seq_rows, local_heads, HEAD_DIM)
    clip_ids = jnp.arange(flat_rows, dtype=jnp.int32) // seq_rows
    clip_table = (clip_ids[:, None] == jnp.arange(clip_count, dtype=jnp.int32)[None, :]).astype(
        wide_type
    )
    valid_rows = row_valid.reshape(flat_rows)
    hidden_rows = hidden.reshape(flat_rows, model_width)
    teacher_rows = teacher.reshape(flat_rows, model_width)

    def per_row(index_no):
        return jnp.dot(clip_table, modulated[:, index_no], precision=lax.Precision.HIGHEST)

    def per_clip(values):
        return jnp.dot(clip_table.T, values, precision=lax.Precision.HIGHEST)

    scale_one = per_row(1)
    gate_one = per_row(2)
    scale_two = per_row(4)
    gate_two = per_row(5)
    normed_one = layer_norm(hidden_rows)
    query_pad = -flat_rows % 128
    key_pad = -flat_rows % 16

    def pad_queries(values):
        return jnp.pad(values, ((0, query_pad), (0, 0)))

    attn_in = pad_queries((normed_one * (1.0 + scale_one) + per_row(0)).astype(low_type))
    cosine_flat = pad_queries(cosine_rep.reshape(flat_rows, HEAD_DIM))
    sine_flat = pad_queries(sine_rep.reshape(flat_rows, HEAD_DIM)) * jnp.where(
        jnp.arange(HEAD_DIM) % 2 == 0, -1.0, 1.0
    )
    self_gains = norm_gains[:2]
    proj_pre, query_flat, own_kv, proj_squares = project(
        attn_in, self_in, self_bias, self_gains, cosine_flat, sine_flat, flat_rows + key_pad, 6
    )
    plane = seq_count == 4 and clip_count == 1
    if plane:
        attn_low, attn_turned, self_totals, got_kv = attend(
            query_flat, own_kv, clip_lengths, flat_rows, 10
        )
    else:
        query_low = query_flat[:flat_rows].reshape(head_shape)
        key_low = own_kv[0, :flat_rows]
        value_low = own_kv[1, :flat_rows]
        local_kv = jnp.stack(
            [
                key_low.reshape(clip_count, seq_rows, local_width),
                value_low.reshape(clip_count, seq_rows, local_width),
            ]
        )
        whole_kv = lax.all_gather(local_kv, "seq", axis=2, tiled=True)
        keys_all = whole_kv[0].reshape(clip_count, slot_count, local_heads, HEAD_DIM)
        values_all = whole_kv[1].reshape(clip_count, slot_count, local_heads, HEAD_DIM)
        att_heads = []
        total_heads = []
        for head_no in range(local_heads):
            attended, log_total = head_forward(
                query_low[:, :, head_no],
                keys_all[:, :, head_no],
                values_all[:, :, head_no],
                key_valid,
                score_scale,
            )
            att_heads.append(attended)
            total_heads.append(log_total)
        attn_low = jnp.stack(att_heads, axis=2).astype(low_type).reshape(flat_rows, local_width)
        attn_low = pad_queries(attn_low)
        self_totals = jnp.stack(total_heads)
    branch_one = (
        line_sum([(attn_low, self_out)], False, 0, flat_rows) + out_bias[0]
    )
    after_one = hidden_rows + branch_one * gate_one
    normed_three = layer_norm(after_one)
    cross_in = (normed_three * cross_gain + cross_shift).astype(low_type)
    cross_query_pre = jnp.dot(cross_in, cross_q, preferred_element_type=wide_type) + cross_bias[0]
    text_low = text.astype(low_type)
    text_start = seq_place * text_local
    text_all = lax.all_gather(text_low, "seq", axis=1, tiled=True)
    text_proj = (
        jnp.einsum("ctd,kde->kcte", text_all, cross_kv, preferred_element_type=wide_type)
        + cross_bias[1:, None, None, :]
    )
    cross_sq, text_sq = small_sum(
        [
            jnp.sum(cross_query_pre * cross_query_pre, axis=-1),
            jnp.sum(text_proj[0] * text_proj[0], axis=-1),
        ],
        7,
    )
    text_rate_all = lax.rsqrt(text_sq / model_width + eps_norm)[..., None]
    text_key_low = (text_proj[0] * text_rate_all * norm_gains[3]).astype(low_type)
    text_value_low = text_proj[1].astype(low_type)
    text_key_pre = lax.dynamic_slice_in_dim(text_proj[0], text_start, text_local, 1)
    text_key_rate = lax.dynamic_slice_in_dim(text_rate_all, text_start, text_local, 1)
    cross_rate = lax.rsqrt(cross_sq / model_width + eps_norm)[:, None]
    cross_query_low = (
        (cross_query_pre * cross_rate * norm_gains[2]).astype(low_type).reshape(head_shape)
    )
    text_key_heads = text_key_low.reshape(clip_count, text_count, local_heads, HEAD_DIM)
    text_value_heads = text_value_low.reshape(clip_count, text_count, local_heads, HEAD_DIM)
    cross_heads = []
    cross_total_heads = []
    for head_no in range(local_heads):
        attended, log_total = head_forward(
            cross_query_low[:, :, head_no],
            text_key_heads[:, :, head_no],
            text_value_heads[:, :, head_no],
            text_valid,
            score_scale,
        )
        cross_heads.append(attended)
        cross_total_heads.append(log_total)
    cross_att_low = jnp.stack(cross_heads, axis=2).astype(low_type).reshape(flat_rows, local_width)
    cross_totals = jnp.stack(cross_total_heads)
    branch_two = (
        line_sum([(cross_att_low, cross_out)], False, 1, flat_rows)
        + out_bias[1]
    )
    after_two = after_one + branch_two
    normed_two = layer_norm(after_two)
    ffn_input = (normed_two * (1.0 + scale_two) + per_row(3)).astype(low_type)
    pre_act = jnp.dot(ffn_input, ffn_in, preferred_element_type=wide_type) + ffn_in_bias
    act_low = gelu_tanh(pre_act).astype(low_type)
    branch_three = (
        line_sum([(act_low, ffn_out)], False, 2, flat_rows) + out_bias[2]
    )
    result = after_two + branch_three * gate_two
    residue = jnp.where(valid_rows[:, None], result - teacher_rows, 0.0)
    grad_three = residue * gate_two
    grad_three_low = grad_three.astype(low_type)
    ffn_out_mix = jnp.dot(act_low.T, grad_three_low, preferred_element_type=wide_type)
    grad_act = jnp.dot(grad_three_low, ffn_out.T, preferred_element_type=wide_type)
    grad_pre = jax.vjp(gelu_tanh, pre_act)[1](grad_act)[0]
    grad_pre_low = grad_pre.astype(low_type)
    grad_pre_low, ffn_out_mix = lax.optimization_barrier(
        (grad_pre_low, ffn_out_mix.astype(low_type))
    )
    part_ffn_out = scatter_rows(ffn_out_mix, 1)
    ffn_in_mix = jnp.dot(ffn_input.T, grad_pre_low, preferred_element_type=wide_type)
    grad_ffn_bias = jnp.sum(grad_pre, axis=0)
    grad_ffn_input = line_sum([(grad_pre_low, ffn_in)], True, 3, flat_rows)
    grad_after_two = (
        residue + jax.vjp(layer_norm, after_two)[1](grad_ffn_input * (1.0 + scale_two))[0]
    )
    grad_two_low = grad_after_two.astype(low_type)
    cross_out_mix = jnp.dot(grad_two_low.T, cross_att_low, preferred_element_type=wide_type)
    grad_cross_att = (
        jnp.dot(grad_two_low, cross_out.T, preferred_element_type=wide_type)
        .astype(low_type)
        .reshape(head_shape)
    )
    cross_query_grads = []
    text_key_grads = []
    text_value_grads = []
    for head_no in range(local_heads):
        head_grads = head_backward(
            cross_query_low[:, :, head_no],
            text_key_heads[:, :, head_no],
            text_value_heads[:, :, head_no],
            text_valid,
            cross_totals[head_no],
            grad_cross_att[:, :, head_no],
            score_scale,
        )
        cross_query_grads.append(head_grads[0])
        text_key_grads.append(head_grads[2])
        text_value_grads.append(head_grads[3])
    grad_cross_query = jnp.stack(cross_query_grads, axis=2).reshape(flat_rows, local_width)
    text_grads_all = jnp.stack(
        [
            jnp.stack(text_key_grads, axis=2).reshape(clip_count, text_count, local_width),
            jnp.stack(text_value_grads, axis=2).reshape(clip_count, text_count, local_width),
        ]
    )
    text_blocks = text_grads_all.astype(low_type).reshape(
        2, clip_count, seq_count, text_local, local_width
    )
    text_blocks = jnp.transpose(text_blocks, (2, 1, 3, 0, 4)).reshape(
        seq_count, clip_count * text_local, 2 * local_width
    )
    text_rows = seq_scatter(text_blocks, 14)
    text_grads = [
        text_rows[:, j * local_width : (j + 1) * local_width].reshape(
            clip_count, text_local, local_width
        )
        for j in range(2)
    ]
    query_term, key_term = small_sum(
        [
            jnp.sum(grad_cross_query * norm_gains[2] * cross_query_pre, axis=-1),
            jnp.sum(text_grads[0] * norm_gains[3] * text_key_pre, axis=-1),
        ],
        8,
    )
    grad_cross_query_pre = (
        grad_cross_query * norm_gains[2] * cross_rate
        - cross_query_pre * cross_rate**3 * query_term[:, None] / model_width
    )
    gain_cross_query = jnp.sum(grad_cross_query * cross_query_pre * cross_rate, axis=0)
    grad_cross_query_low = grad_cross_query_pre.astype(low_type)
    grad_cross_query_low, ffn_in_mix, part_ffn_out = lax.optimization_barrier(
        (grad_cross_query_low, ffn_in_mix.astype(low_type), part_ffn_out)
    )
    part_ffn_in = scatter_rows(ffn_in_mix, 0)
    cross_q_mix = jnp.dot(cross_in.T, grad_cross_query_low, preferred_element_type=wide_type)
    grad_cross_in = line_sum([(grad_cross_query_low, cross_q)], True, 4, flat_rows)
    grad_text_key_pre = (
        text_grads[0] * norm_gains[3] * text_key_rate
        - text_key_pre * text_key_rate**3 * key_term[..., None] / model_width
    )
    gain_text_key = jnp.sum(text_grads[0] * text_key_pre * text_key_rate, axis=(0, 1))
    grad_cross_bias = jnp.stack(
        [
            jnp.sum(grad_cross_query_pre, axis=0),
            jnp.sum(grad_text_key_pre, axis=(0, 1)),
            jnp.sum(text_grads[1], axis=(0, 1)),
        ]
    )
    text_grad_low = jnp.stack([grad_text_key_pre, text_grads[1]]).astype(low_type)
    cross_kv_mix = jnp.einsum(
        "ctd,kcte->kde", text_low, text_grad_low, preferred_element_type=wide_type
    )
    grad_text = lax.psum(
        jnp.einsum(
            "kcte,kde->ctd", text_grad_low, cross_kv, preferred_element_type=wide_type
        ).astype(jnp.bfloat16),
        "tensor",
    ).astype(jnp.float32)
    grad_cross_gain = jnp.sum(grad_cross_in * normed_three, axis=0)
    grad_cross_shift = jnp.sum(grad_cross_in, axis=0)
    grad_after_one = (
        grad_after_two + jax.vjp(layer_norm, after_one)[1](grad_cross_in * cross_gain)[0]
    )
    grad_one = grad_after_one * gate_one
    grad_one_low = grad_one.astype(low_type)
    self_out_mix = jnp.dot(grad_one_low.T, attn_low[:flat_rows], preferred_element_type=wide_type)
    grad_attn = (
        jnp.dot(grad_one_low, self_out.T, preferred_element_type=wide_type)
        .astype(low_type)
        .reshape(head_shape)
    )
    group_mix = jnp.concatenate(
        [cross_out_mix, cross_q_mix, self_out_mix, cross_kv_mix[0], cross_kv_mix[1]], axis=-1
    ).astype(low_type)
    grad_attn, group_mix = lax.optimization_barrier((grad_attn, group_mix))
    part_group = scatter_rows(group_mix, 0)
    if plane:
        query_grads, kv_grads = attend_back(
            query_flat,
            own_kv,
            got_kv,
            attn_turned,
            self_totals,
            pad_queries(grad_attn.reshape(flat_rows, local_width)),
            clip_lengths,
            flat_rows,
            11,
        )
    else:
        query_grads = []
        key_grads = []
        value_grads = []
        for head_no in range(local_heads):
            head_grads = head_backward(
                query_low[:, :, head_no],
                keys_all[:, :, head_no],
                values_all[:, :, head_no],
                key_valid,
                self_totals[head_no],
                grad_attn[:, :, head_no],
                score_scale,
            )
            query_grads.append(head_grads[0])
            key_grads.append(head_grads[2])
            value_grads.append(head_grads[3])
        owner_grads = [
            jnp.stack(parts, axis=2)
            .astype(jnp.bfloat16)
            .reshape(clip_count, seq_count, seq_rows, local_width)
            for parts in (key_grads, value_grads)
        ]
        owner_grads = jnp.concatenate(
            [
                jnp.swapaxes(part, 0, 1).reshape(seq_count, flat_rows, local_width)
                for part in owner_grads
            ],
            axis=-1,
        )
        pad_rows = -flat_rows % 16
        owner_grads = jnp.pad(owner_grads, ((0, 0), (0, pad_rows), (0, 0)))
        kv_rows = lax.psum_scatter(
            owner_grads.reshape(seq_count * (flat_rows + pad_rows), 2 * local_width),
            "seq",
            scatter_dimension=0,
            tiled=True,
        )[:flat_rows].astype(jnp.float32)
        kv_grads = jnp.stack(
            [pad_queries(kv_rows[:, :local_width]), pad_queries(kv_rows[:, local_width:])]
        )
        query_grads = pad_queries(
            jnp.stack(query_grads, axis=2).reshape(flat_rows, local_width)
        )
    query_grads, part_ffn_in = lax.optimization_barrier((query_grads, part_ffn_in))
    *grad_proj_low, proj_sums = unproject(
        query_grads,
        kv_grads,
        proj_pre,
        proj_squares,
        self_gains,
        cosine_flat,
        sine_flat,
        model_width,
        9,
    )
    grad_self_bias = proj_sums[:3]
    self_in_mix = jnp.concatenate(
        [
            jnp.dot(attn_in.T, grad_proj_low[j], preferred_element_type=wide_type).astype(low_type)
            for j in range(3)
        ],
        axis=-1,
    )
    grad_proj_low, self_in_mix, part_group = lax.optimization_barrier(
        (grad_proj_low, self_in_mix, part_group)
    )
    part_self_in = scatter_rows(self_in_mix, 0)
    grad_attn_in = line_sum([(grad_proj_low[j], self_in[j]) for j in range(3)], True, 5, flat_rows)
    grad_hidden = (
        grad_after_one + jax.vjp(layer_norm, hidden_rows)[1](grad_attn_in * (1.0 + scale_one))[0]
    )
    grad_time_local = jnp.stack(
        [
            per_clip(grad_attn_in),
            per_clip(grad_attn_in * normed_one),
            per_clip(grad_after_one * branch_one),
            per_clip(grad_ffn_input),
            per_clip(grad_ffn_input * normed_two),
            per_clip(residue * branch_three),
        ],
        axis=1,
    )
    grad_out_bias = jnp.stack(
        [jnp.sum(grad_one, axis=0), jnp.sum(grad_after_two, axis=0), jnp.sum(grad_three, axis=0)]
    )
    stream_values = (
        grad_time_local,
        grad_cross_gain,
        grad_cross_shift,
        grad_out_bias,
        jnp.sum(residue * residue),
    )
    grad_time_local, grad_cross_gain, grad_cross_shift, grad_out_bias, square_local = stream_values
    grad_norm_gains = jnp.concatenate(
        [proj_sums[3:5], gain_cross_query[None], gain_text_key[None]]
    )
    time_pair, sums = plane_sum(
        grad_time_local,
        [
            grad_self_bias,
            grad_norm_gains,
            grad_cross_gain,
            grad_cross_shift,
            grad_cross_bias,
            grad_ffn_bias,
            grad_out_bias,
            square_local,
        ],
        13,
    )
    grad_time, time_all = time_pair
    sum_modulation = jnp.sum(time_all, axis=0)
    (
        sum_self_bias,
        sum_gains,
        sum_cross_gain,
        sum_cross_shift,
        sum_cross_bias,
        sum_ffn_bias,
        sum_out_bias,
        square_sum,
    ) = sums
    loss = square_sum / (valid_total * model_width)
    part_ffn_in = part_ffn_in.astype(wide_type)
    part_ffn_out = part_ffn_out.astype(wide_type)
    pieces = [
        part_group[:, j * local_width : (j + 1) * local_width].astype(wide_type) for j in range(5)
    ]
    part_cross_out = pieces[0].T
    part_cross_q = pieces[1]
    part_self_out = pieces[2].T
    part_cross_kv = jnp.stack([pieces[3], pieces[4]])
    part_self_in = jnp.stack(
        [part_self_in[:, j * local_width : (j + 1) * local_width] for j in range(3)]
    ).astype(wide_type)
    result_out = result.reshape(clip_count, seq_rows, model_width)
    grad_hidden_out = grad_hidden.reshape(clip_count, seq_rows, model_width)
    return (
        result_out,
        loss,
        grad_hidden_out,
        grad_text,
        grad_time,
        sum_modulation,
        part_self_in,
        sum_self_bias,
        part_self_out,
        sum_gains,
        sum_cross_gain,
        sum_cross_shift,
        part_cross_q,
        part_cross_kv,
        sum_cross_bias,
        part_cross_out,
        part_ffn_in,
        sum_ffn_bias,
        part_ffn_out,
        sum_out_bias,
    )


def solution(mesh):
    placed = (
        P("dp", "seq", None),
        P("dp", "seq", None),
        P("dp", "seq", None),
        P("dp", None, None),
        P(),
        P(None, "dp", "seq"),
        P(),
        P(None, None, "tensor"),
        P(None, "tensor"),
        P("tensor", None),
        P(None, "tensor"),
        P(),
        P(),
        P(None, "tensor"),
        P(None, None, "tensor"),
        P(None, "tensor"),
        P("tensor", None),
        P(None, "tensor"),
        P("tensor"),
        P("tensor", None),
        P(),
    )
    return jax.shard_map(
        shards,
        mesh=mesh,
        in_specs=placed,
        out_specs=(
            P("dp", "seq", None),
            P(),
            P("dp", "seq", None),
            P("dp", "seq", None),
            P("dp", None, None),
            P(),
            P(None, ("dp", "seq"), "tensor"),
            P(None, "tensor"),
            P("tensor", ("dp", "seq")),
            P(None, "tensor"),
            P(),
            P(),
            P(("dp", "seq"), "tensor"),
            P(None, ("dp", "seq"), "tensor"),
            P(None, "tensor"),
            P("tensor", ("dp", "seq")),
            P(("dp", "seq"), "tensor"),
            P("tensor"),
            P("tensor", ("dp", "seq")),
            P(),
        ),
        check_vma=False,
    )
```

```python
import functools
import math

import jax
import jax.numpy as jnp
from jax import lax
from jax.experimental import pallas as pl
from jax.experimental.pallas import tpu as pltpu
from jax.experimental.layout import Layout, with_layout_constraint
from jax.sharding import PartitionSpec as P

HEAD_DIM = 128
LOW = jnp.bfloat16
WIDE = jnp.float32


eps_norm = 1e-06


def layer_norm(values):
    centred = values - jnp.mean(values, axis=-1, keepdims=True)
    return centred * lax.rsqrt(jnp.mean(centred * centred, axis=-1, keepdims=True) + eps_norm)


def gelu_tanh(values):
    return (
        0.5
        * values
        * (1.0 + jnp.tanh(0.7978845608028654 * (values + 0.044715 * values * values * values)))
    )


def rope_tables(positions, head_size):
    sixth_part = head_size // 6
    part_spans = (head_size - 4 * sixth_part, 2 * sixth_part, 2 * sixth_part)
    pieces = []
    for axis_no in range(3):
        span_now = part_spans[axis_no]
        inverse = 1.0 / 10000.0 ** (jnp.arange(0, span_now, 2).astype(jnp.float32) / span_now)
        pieces.append(positions[axis_no].astype(jnp.float32)[..., None] * inverse)
    angles = jnp.concatenate(pieces, axis=-1)
    cosine_rep = jnp.repeat(jnp.cos(angles), 2, axis=-1)[..., None, :]
    sine_rep = jnp.repeat(jnp.sin(angles), 2, axis=-1)[..., None, :]
    return (cosine_rep, sine_rep)


def swap_table(head_size):
    row_no = jnp.arange(head_size)[:, None]
    col_no = jnp.arange(head_size)[None, :]
    upward = jnp.where((row_no % 2 == 0) & (col_no == row_no + 1), 1.0, 0.0)
    downward = jnp.where((row_no % 2 == 1) & (col_no == row_no - 1), -1.0, 0.0)
    return (upward + downward).astype(jnp.float32)


def rotate(values, cosine_rep, sine_rep, swap_matrix):
    swapped = jnp.matmul(values, swap_matrix, precision=lax.Precision.HIGHEST)
    return values * cosine_rep + swapped * sine_rep


def line_kernel(count, block, group, lag, lag2, turned, *refs):
    lhs_refs = refs[:count]
    rhs_refs = refs[count:2 * count]
    out_ref, raw, part, stage, cross, raw_s, raw_r, mid_s, mid_r, far_s, far_r, near_s, near_r = refs[2 * count:]
    steps = out_ref.shape[0] // block
    me = lax.axis_index("tensor")
    inner = (me == 1) | (me == 2)
    outer = jnp.logical_not(inner)
    leaf = jnp.where(me < 2, 0, 3)
    hub = jnp.where(me < 2, 1, 2)
    mate = 3 - me
    side = jnp.where(me < 2, 0, 1)

    def signal(where):
        pl.semaphore_signal(
            pltpu.get_barrier_semaphore(), inc=1, device_id={"tensor": where},
            device_id_type=pl.DeviceIdType.MESH)

    @pl.when(outer)
    def _():
        signal(hub)
        pl.semaphore_wait(pltpu.get_barrier_semaphore(), 1)

    @pl.when(inner)
    def _():
        signal(leaf)
        signal(mate)
        pl.semaphore_wait(pltpu.get_barrier_semaphore(), 2)

    def rows_of(step):
        return pl.ds(pl.multiple_of(step * block, 16), block)

    def remote(src, dst, send, recv, step, where):
        at = rows_of(step)
        return pltpu.make_async_remote_copy(
            src_ref=src.at[at], dst_ref=dst.at[at], send_sem=send.at[step], recv_sem=recv.at[step],
            device_id={"tensor": where}, device_id_type=pl.DeviceIdType.MESH)

    def raw_copy(step):
        return remote(raw, raw, raw_s, raw_r, step, hub)

    def mid_copy(step):
        return remote(stage, cross, mid_s, mid_r, step, mate)

    def far_copy(step):
        return remote(out_ref, out_ref, far_s, far_r, step, mate)

    def near_copy(step):
        return remote(out_ref, out_ref, near_s, near_r, step, leaf)

    def body(step, carry):
        @pl.when((step < steps) & (lax.rem(step, group) == 0))
        def _():
            at = pl.ds(pl.multiple_of(step * block, 16), block * group)
            total = None
            for lhs, rhs in zip(lhs_refs, rhs_refs):
                term = lax.dot_general(lhs[at], rhs[...], (((1,), (1 if turned else 0,)), ((), ())),
                    preferred_element_type=WIDE)
                total = term if total is None else total + term
            part[at] = total

        @pl.when(outer & (step < steps))
        def _():
            at = rows_of(step)
            raw[at] = part[at].astype(LOW)
            raw_copy(step).start()

        late = step - lag2
        @pl.when(inner & (late >= 0) & (late < steps) & (lax.rem(late + 2 * lag2, 2) != side))
        def _():
            far_copy(late).wait_recv()
            near_copy(late).start()

        near = step - lag
        @pl.when(inner & (near >= 0) & (near < steps) & (lax.rem(near + 2 * lag2, 2) == side))
        def _():
            at = rows_of(near)
            mid_copy(near).wait_recv()
            out_ref[at] = (part[at] + cross[at].astype(WIDE)).astype(LOW)
            far_copy(near).start()
            near_copy(near).start()

        @pl.when(inner & (step < steps))
        def _():
            at = rows_of(step)
            raw_copy(step).wait_recv()

            @pl.when(lax.rem(step, 2) == side)
            def _():
                part[at] = part[at] + raw[at].astype(WIDE)

            @pl.when(lax.rem(step, 2) != side)
            def _():
                stage[at] = (part[at] + raw[at].astype(WIDE)).astype(LOW)
                mid_copy(step).start()

        return carry

    lax.fori_loop(0, steps + lag2, body, 0)

    def drain(step, carry):
        @pl.when(outer)
        def _():
            near_copy(step).wait_recv()
            raw_copy(step).wait_send()

        @pl.when(inner)
        def _():
            near_copy(step).wait_send()

            @pl.when(lax.rem(step, 2) == side)
            def _():
                far_copy(step).wait_send()

            @pl.when(lax.rem(step, 2) != side)
            def _():
                mid_copy(step).wait_send()

        return carry

    lax.fori_loop(0, steps, drain, 0)

def line_sum(pairs, turned, ident, true_rows, block=16, group=7, lag=4, lag2=8):
    width = pairs[0][1].shape[0 if turned else 1]
    unit = block * group
    rows = -(-true_rows // unit) * unit
    pairs = [
        (jnp.pad(lhs, ((0, max(rows - lhs.shape[0], 0)), (0, 0))), rhs) for lhs, rhs in pairs
    ]
    steps = rows // block
    dma = pltpu.SemaphoreType.DMA
    depth = sum(p[0].shape[1] for p in pairs)
    return pl.pallas_call(
        functools.partial(line_kernel, len(pairs), block, group, lag, lag2, turned),
        out_shape=jax.ShapeDtypeStruct((rows, width), LOW),
        in_specs=[pl.BlockSpec(memory_space=pltpu.VMEM)] * (2 * len(pairs)),
        out_specs=pl.BlockSpec(memory_space=pltpu.VMEM),
        scratch_shapes=[
            pltpu.VMEM((rows, width), LOW),
            pltpu.VMEM((rows, width), WIDE),
            pltpu.VMEM((rows, width), LOW),
            pltpu.VMEM((rows, width), LOW),
        ] + [dma((steps,))] * 8,
        compiler_params=pltpu.CompilerParams(collective_id=ident, has_side_effects=True, vmem_limit_bytes=60 << 20),
        cost_estimate=pl.CostEstimate(flops=2 * rows * width * depth, bytes_accessed=230 * 10**6, transcendentals=0),
        name=f"line_sum_{ident}",
    )(*[p[0] for p in pairs], *[p[1] for p in pairs])[:true_rows].astype(WIDE)

def row_major(values):
    return with_layout_constraint(values, Layout((0, 1)))


def scatter_rows(mix, dimension):
    return lax.psum_scatter(mix, ("dp", "seq"), scatter_dimension=dimension, tiled=True)


def plane_sum_kernel(seq_count, value_ref, seq_ref, all_ref, slots, send_sem, recv_sem):
    count = slots.shape[0]
    dp = lax.axis_index("dp")
    me = dp * seq_count + lax.axis_index("seq")

    def device(place):
        return {"dp": place // seq_count, "seq": lax.rem(place, seq_count)}

    barrier = pltpu.get_barrier_semaphore()
    for hop in range(1, count):
        pl.semaphore_signal(
            barrier, inc=1, device_id=device(lax.rem(me + hop, count)),
            device_id_type=pl.DeviceIdType.MESH)
    pl.semaphore_wait(barrier, count - 1)

    def copy(slot, hop, place):
        return pltpu.make_async_remote_copy(
            src_ref=value_ref, dst_ref=slots.at[slot], send_sem=send_sem.at[hop - 1],
            recv_sem=recv_sem.at[hop - 1], device_id=device(place),
            device_id_type=pl.DeviceIdType.MESH)

    for hop in range(1, count):
        copy(me, hop, lax.rem(me + hop, count)).start()
    slots[pl.ds(me, 1)] = value_ref[...][None]
    for hop in range(1, count):
        origin = lax.rem(me + count - hop, count)
        copy(origin, hop, origin).wait_recv()
    for hop in range(1, count):
        copy(me, hop, lax.rem(me + hop, count)).wait_send()

    def span(start):
        total = slots[start].astype(WIDE)
        for slot in range(1, seq_count):
            total = total + slots[start + slot].astype(WIDE)
        return total

    seq_ref[...] = span(dp * seq_count)
    total = span(0)
    for part in range(1, count // seq_count):
        total = total + span(part * seq_count)
    all_ref[...] = total


def plane_sum(first, values, ident):
    seq_count = lax.axis_size("seq")
    count = lax.axis_size("dp") * seq_count
    flat = jnp.concatenate([value.reshape(-1).astype(LOW) for value in [first] + values])
    size = flat.shape[0]
    lines = -(-size // 2048) * 16
    packed = jnp.pad(flat, (0, lines * 128 - size)).reshape(lines, 128)
    vmem = pl.BlockSpec(memory_space=pltpu.VMEM)
    seq_total, all_total = pl.pallas_call(
        functools.partial(plane_sum_kernel, seq_count),
        out_shape=(jax.ShapeDtypeStruct((lines, 128), WIDE),) * 2,
        in_specs=[vmem],
        out_specs=(vmem, vmem),
        scratch_shapes=[
            pltpu.VMEM((count, lines, 128), LOW),
            pltpu.SemaphoreType.DMA((count - 1,)),
            pltpu.SemaphoreType.DMA((count - 1,)),
        ],
        compiler_params=pltpu.CompilerParams(collective_id=ident, has_side_effects=True),
        name="plane_sum",
    )(packed)
    all_total = all_total.reshape(-1)
    first_pair = (
        seq_total.reshape(-1)[: first.size].reshape(first.shape),
        all_total[: first.size].reshape(first.shape),
    )
    outs = []
    start = first.size
    for value in values:
        outs.append(all_total[start : start + value.size].reshape(value.shape))
        start += value.size
    return first_pair, outs


def small_kernel(value_ref, out_ref, slots, send_sem, recv_sem):
    count = slots.shape[0]
    me = lax.axis_index("tensor")
    barrier = pltpu.get_barrier_semaphore()
    for hop in range(1, count):
        pl.semaphore_signal(
            barrier, inc=1, device_id={"tensor": lax.rem(me + hop, count)},
            device_id_type=pl.DeviceIdType.MESH)
    pl.semaphore_wait(barrier, count - 1)
    copies = []
    for hop in range(1, count):
        copy = pltpu.make_async_remote_copy(
            src_ref=value_ref, dst_ref=slots.at[me], send_sem=send_sem.at[hop - 1],
            recv_sem=recv_sem.at[hop - 1], device_id={"tensor": lax.rem(me + hop, count)},
            device_id_type=pl.DeviceIdType.MESH)
        copy.start()
        copies.append(copy)
    slots[pl.ds(me, 1)] = value_ref[...][None]
    for hop in range(1, count):
        origin = lax.rem(me + count - hop, count)
        pltpu.make_async_remote_copy(
            src_ref=value_ref, dst_ref=slots.at[origin], send_sem=send_sem.at[hop - 1],
            recv_sem=recv_sem.at[hop - 1], device_id={"tensor": origin},
            device_id_type=pl.DeviceIdType.MESH).wait_recv()
    for copy in copies:
        copy.wait_send()
    total = slots[0]
    for slot in range(1, count):
        total = total + slots[slot]
    out_ref[...] = total


def small_sum(values, ident):
    count = lax.axis_size("tensor")
    flat = jnp.concatenate([value.reshape(-1) for value in values])
    size = flat.shape[0]
    lines = -(-size // 1024) * 8
    packed = jnp.pad(flat, (0, lines * 128 - size)).reshape(lines, 128)
    summed = pl.pallas_call(
        small_kernel,
        out_shape=jax.ShapeDtypeStruct((lines, 128), WIDE),
        in_specs=[pl.BlockSpec(memory_space=pltpu.VMEM)],
        out_specs=pl.BlockSpec(memory_space=pltpu.VMEM),
        scratch_shapes=[
            pltpu.VMEM((count, lines, 128), WIDE),
            pltpu.SemaphoreType.DMA((count - 1,)),
            pltpu.SemaphoreType.DMA((count - 1,)),
        ],
        compiler_params=pltpu.CompilerParams(collective_id=ident, has_side_effects=True),
        name=f"small_sum_{ident}",
    )(packed).reshape(-1)
    outs = []
    start = 0
    for value in values:
        outs.append(summed[start : start + value.size].reshape(value.shape))
        start += value.size
    return outs


LOG2E = 1.4426950408889634
HIDDEN_SCORE = -1e30


def plane_places():
    me = lax.axis_index("seq")
    column = lax.rem(me, 2)
    line = me // 2
    return (me, me + 1 - 2 * column, me + 2 - 4 * line, 3 - me)


def plane_barrier(places):
    barrier = pltpu.get_barrier_semaphore()
    for place in places[1:]:
        pl.semaphore_signal(
            barrier, inc=1, device_id={"seq": place}, device_id_type=pl.DeviceIdType.MESH
        )
    pl.semaphore_wait(barrier, 3)


def plane_copy(src, dst, send, recv, place):
    return pltpu.make_async_remote_copy(
        src_ref=src,
        dst_ref=dst,
        send_sem=send,
        recv_sem=recv,
        device_id={"seq": place},
        device_id_type=pl.DeviceIdType.MESH,
    )


def head_lanes(head):
    return pl.ds(pl.multiple_of(head * HEAD_DIM, 128), HEAD_DIM)


def block_valid(key_rows, owner, true_rows, length):
    row = lax.broadcasted_iota(jnp.int32, (key_rows, 1), 0)
    return (row < true_rows) & (owner * true_rows + row < length)


def over_last(lhs, rhs):
    return lax.dot_general(lhs, rhs, (((1,), (1,)), ((), ())), preferred_element_type=WIDE)


def attend_kernel(
    true_rows, length_ref, query_ref, kv_ref, out_ref, turned_ref, total_ref, got_ref, peak, summed, send, recv
):
    places = plane_places()
    plane_barrier(places)
    heads = query_ref.shape[1] // HEAD_DIM
    key_rows = kv_ref.shape[1]
    length = length_ref[0]
    factor = LOG2E / math.sqrt(HEAD_DIM)

    def own_copy(relation, part):
        index = 2 * relation + part
        return plane_copy(
            kv_ref.at[part], got_ref.at[relation, part], send.at[index], recv.at[index], places[relation + 1]
        )

    key_pass = plane_copy(got_ref.at[0, 0], got_ref.at[2, 0], send.at[4], recv.at[4], places[2])
    value_pass = plane_copy(got_ref.at[1, 1], got_ref.at[2, 1], send.at[5], recv.at[5], places[1])
    for part in range(2):
        for relation in range(2):
            own_copy(relation, part).start()

    peak[...] = jnp.full(peak.shape, HIDDEN_SCORE, WIDE)
    summed[...] = jnp.zeros(summed.shape, WIDE)
    turned_ref[...] = jnp.zeros(turned_ref.shape, WIDE)

    def block(source, owner):
        def step(head, carry):
            lanes = head_lanes(head)
            scores = over_last(source(0, lanes), query_ref[:, lanes]) * factor
            scores = jnp.where(block_valid(key_rows, owner, true_rows, length), scores, HIDDEN_SCORE)
            before = peak[head]
            after = jnp.maximum(before, jnp.max(scores, axis=0, keepdims=True))
            shrink = jnp.exp2(before - after)
            terms = jnp.exp2(scores - after)
            peak[head] = after
            summed[head] = summed[head] * shrink + jnp.sum(terms, axis=0, keepdims=True)
            turned_ref[head] = turned_ref[head] * shrink + lax.dot_general(
                source(1, lanes),
                terms.astype(LOW),
                (((0,), (0,)), ((), ())),
                preferred_element_type=WIDE,
            )

            return carry

        lax.fori_loop(0, heads, step, 0)

    block(lambda part, lanes: kv_ref[part, :, lanes], places[0])
    own_copy(0, 0).wait_recv()
    key_pass.start()
    own_copy(0, 1).wait_recv()
    own_copy(1, 1).wait_recv()
    value_pass.start()
    own_copy(1, 0).wait_recv()
    for relation in range(3):
        if relation == 2:
            key_pass.wait_recv()
            value_pass.wait_recv()
        block(
            lambda part, lanes, relation=relation: got_ref[relation, part, :, lanes],
            places[relation + 1],
        )

    for head in range(heads):
        lanes = slice(head * HEAD_DIM, (head + 1) * HEAD_DIM)
        attended = turned_ref[head] / summed[head]
        turned_ref[head] = attended
        out_ref[:, lanes] = jnp.transpose(attended).astype(LOW)
        total_ref[head] = peak[head] + jnp.log2(summed[head])
    for part in range(2):
        for relation in range(2):
            own_copy(relation, part).wait_send()
    key_pass.wait_send()
    value_pass.wait_send()


def attend(query_low, kv_low, length, true_rows, ident):
    rows, width = query_low.shape
    heads = width // HEAD_DIM
    key_rows = kv_low.shape[1]
    dma = pltpu.SemaphoreType.DMA
    vmem = pl.BlockSpec(memory_space=pltpu.VMEM)
    return pl.pallas_call(
        functools.partial(attend_kernel, true_rows),
        out_shape=(
            jax.ShapeDtypeStruct((rows, width), LOW),
            jax.ShapeDtypeStruct((heads, HEAD_DIM, rows), WIDE),
            jax.ShapeDtypeStruct((heads, 1, rows), WIDE),
            jax.ShapeDtypeStruct((3, 2, key_rows, width), LOW),
        ),
        in_specs=[pl.BlockSpec(memory_space=pltpu.SMEM), vmem, vmem],
        out_specs=(vmem,) * 4,
        scratch_shapes=[
            pltpu.VMEM((heads, 1, rows), WIDE),
            pltpu.VMEM((heads, 1, rows), WIDE),
            dma((6,)),
            dma((6,)),
        ],
        compiler_params=pltpu.CompilerParams(
            collective_id=ident, has_side_effects=True, vmem_limit_bytes=56 << 20
        ),
        cost_estimate=pl.CostEstimate(flops=10**9, bytes_accessed=150 * 10**6, transcendentals=0),
        name="attend",
    )(length, query_low, kv_low)


def attend_back_kernel(
    true_rows, length_ref, query_ref, kv_ref, got_ref, turned_ref, total_ref, grad_ref,
    query_grad_ref, kv_grad_ref, centre, query_turned, leaving, landing, send, recv,
):
    places = plane_places()
    plane_barrier(places)
    heads = query_ref.shape[1] // HEAD_DIM
    key_rows = kv_ref.shape[1]
    length = length_ref[0]
    scale = 1.0 / math.sqrt(HEAD_DIM)
    for head in range(heads):
        lanes = slice(head * HEAD_DIM, (head + 1) * HEAD_DIM)
        grads = jnp.transpose(grad_ref[:, lanes].astype(WIDE))
        centre[head] = jnp.sum(grads * turned_ref[head], axis=0, keepdims=True)
    query_turned[...] = jnp.zeros(query_turned.shape, WIDE)
    spare = query_ref.shape[0] - key_rows
    kv_grad_ref[:, pl.ds(key_rows, spare), :] = jnp.zeros((2, spare, query_ref.shape[1]), WIDE)

    def block(source, sink, owner):
        def step(head, carry):
            lanes = head_lanes(head)
            keys = source(0, lanes)
            query = query_ref[:, lanes]
            grads = grad_ref[:, lanes]
            probs = jnp.exp2(over_last(keys, query) * (scale * LOG2E) - total_ref[head])
            probs = jnp.where(block_valid(key_rows, owner, true_rows, length), probs, 0.0)
            grad_probs = over_last(source(1, lanes), grads)
            grad_scores = (probs * (grad_probs - centre[head])).astype(LOW)
            sink(0, lanes, jnp.dot(grad_scores, query, preferred_element_type=WIDE) * scale)
            sink(1, lanes, jnp.dot(probs.astype(LOW), grads, preferred_element_type=WIDE))
            query_turned[head] = query_turned[head] + lax.dot_general(
                keys, grad_scores, (((0,), (0,)), ((), ())), preferred_element_type=WIDE
            )

            return carry

        lax.fori_loop(0, heads, step, 0)

    def grad_copy(relation, part):
        return plane_copy(
            leaving.at[relation, part],
            landing.at[relation, part],
            send.at[relation, part],
            recv.at[relation, part],
            places[relation + 1],
        )

    for relation in (2, 1, 0):

        def sink(part, lanes, value, relation=relation):
            leaving[relation, part, :, lanes] = value.astype(LOW)

        block(
            lambda part, lanes, relation=relation: got_ref[relation, part, :, lanes],
            sink,
            places[relation + 1],
        )
        for part in range(2):
            grad_copy(relation, part).start()

    def own_sink(part, lanes, value):
        kv_grad_ref[part, pl.ds(0, key_rows), lanes] = value

    block(lambda part, lanes: kv_ref[part, :, lanes], own_sink, places[0])
    for head in range(heads):
        lanes = slice(head * HEAD_DIM, (head + 1) * HEAD_DIM)
        query_grad_ref[:, lanes] = jnp.transpose(query_turned[head]) * scale
    for relation in (2, 1, 0):
        for part in range(2):
            grad_copy(relation, part).wait_recv()

    def gather(tile, carry):
        rows = pl.ds(pl.multiple_of(tile * 16, 16), 16)
        for part in range(2):
            total = kv_grad_ref[part, rows]
            for relation in range(3):
                total = total + landing[relation, part, rows].astype(WIDE)
            kv_grad_ref[part, rows] = total
        return carry

    lax.fori_loop(0, key_rows // 16, gather, 0)
    for relation in range(3):
        for part in range(2):
            grad_copy(relation, part).wait_send()


def attend_back(query_low, kv_low, got, turned, total, grad_low, length, true_rows, ident):
    rows, width = query_low.shape
    heads = width // HEAD_DIM
    key_rows = kv_low.shape[1]
    dma = pltpu.SemaphoreType.DMA
    vmem = pl.BlockSpec(memory_space=pltpu.VMEM)
    return pl.pallas_call(
        functools.partial(attend_back_kernel, true_rows),
        out_shape=(
            jax.ShapeDtypeStruct((rows, width), WIDE),
            jax.ShapeDtypeStruct((2, rows, width), WIDE),
        ),
        in_specs=[pl.BlockSpec(memory_space=pltpu.SMEM)] + [vmem] * 6,
        out_specs=(vmem,) * 2,
        scratch_shapes=[
            pltpu.VMEM((heads, 1, rows), WIDE),
            pltpu.VMEM((heads, HEAD_DIM, rows), WIDE),
            pltpu.VMEM((3, 2, key_rows, width), LOW),
            pltpu.VMEM((3, 2, key_rows, width), LOW),
            dma((3, 2)),
            dma((3, 2)),
        ],
        compiler_params=pltpu.CompilerParams(
            collective_id=ident, has_side_effects=True, vmem_limit_bytes=56 << 20
        ),
        cost_estimate=pl.CostEstimate(flops=10**9, bytes_accessed=200 * 10**6, transcendentals=0),
        name="attend_back",
    )(length, query_low, kv_low, got, turned, total, grad_low)


def pair_swap(values):
    lane = lax.broadcasted_iota(jnp.int32, values.shape, 1)
    return jnp.where(
        lax.rem(lane, 2) == 0,
        pltpu.roll(values, HEAD_DIM - 1, axis=1),
        pltpu.roll(values, 1, axis=1),
    )


def rows_to_lanes(values):
    return jnp.sum(jnp.transpose(values), axis=0, keepdims=True)


def lanes_to_rows(row):
    return jnp.transpose(jnp.broadcast_to(row, (HEAD_DIM, row.shape[1])))


def tensor_barrier():
    count = lax.axis_size("tensor")
    me = lax.axis_index("tensor")
    barrier = pltpu.get_barrier_semaphore()
    for hop in range(1, count):
        pl.semaphore_signal(
            barrier, inc=1, device_id={"tensor": lax.rem(me + hop, count)},
            device_id_type=pl.DeviceIdType.MESH)
    pl.semaphore_wait(barrier, count - 1)


def tensor_copy(stage, slots, send, recv, slot, hop, place):
    return pltpu.make_async_remote_copy(
        src_ref=stage, dst_ref=slots.at[slot], send_sem=send.at[hop - 1],
        recv_sem=recv.at[hop - 1], device_id={"tensor": place},
        device_id_type=pl.DeviceIdType.MESH)


def tensor_send(stage, slots, send, recv):
    count = slots.shape[0]
    me = lax.axis_index("tensor")
    for hop in range(1, count):
        tensor_copy(stage, slots, send, recv, me, hop, lax.rem(me + hop, count)).start()
    slots[pl.ds(me, 1)] = stage[...][None]


def tensor_collect(stage, slots, send, recv):
    count = slots.shape[0]
    me = lax.axis_index("tensor")
    for hop in range(1, count):
        origin = lax.rem(me + count - hop, count)
        tensor_copy(stage, slots, send, recv, origin, hop, origin).wait_recv()
    for hop in range(1, count):
        tensor_copy(stage, slots, send, recv, me, hop, lax.rem(me + hop, count)).wait_send()
    total = slots[0]
    for slot in range(1, count):
        total = total + slots[slot]
    return total


def project_kernel(
    rows_ref, weight_ref, bias_ref, gain_ref, cosine_ref, sine_ref,
    pre_ref, query_ref, kv_ref, square_ref, stage, slots, send, recv,
):
    heads = query_ref.shape[1] // HEAD_DIM
    key_rows = kv_ref.shape[1]
    width = rows_ref.shape[1]
    tensor_barrier()
    stage[...] = jnp.zeros(stage.shape, WIDE)
    for part in range(2):
        pre_ref[part] = (
            jnp.dot(rows_ref[...], weight_ref[part], preferred_element_type=WIDE)
            + bias_ref[part : part + 1]
        )
        squares = None
        for head in range(heads):
            piece = pre_ref[part, :, head * HEAD_DIM : (head + 1) * HEAD_DIM]
            squares = piece * piece if squares is None else squares + piece * piece
        stage[part : part + 1] = rows_to_lanes(squares)
    tensor_send(stage, slots, send, recv)
    values = jnp.dot(rows_ref[...], weight_ref[2], preferred_element_type=WIDE) + bias_ref[2:3]
    kv_ref[1] = values[:key_rows].astype(LOW)
    total = tensor_collect(stage, slots, send, recv)
    square_ref[...] = total
    for part in range(2):
        rate = lanes_to_rows(lax.rsqrt(total[part : part + 1] / width + eps_norm))
        for head in range(heads):
            lanes = slice(head * HEAD_DIM, (head + 1) * HEAD_DIM)
            normed = pre_ref[part, :, lanes] * rate * gain_ref[part : part + 1, lanes]
            turned = normed * cosine_ref[...] + pair_swap(normed) * sine_ref[...]
            if part == 0:
                query_ref[:, lanes] = turned.astype(LOW)
            else:
                kv_ref[0, :, lanes] = turned[:key_rows].astype(LOW)


def project(rows_low, weights, bias, gains, cosine, sine, key_rows, ident):
    rows = rows_low.shape[0]
    width = weights.shape[2]
    count = lax.axis_size("tensor")
    vmem = pl.BlockSpec(memory_space=pltpu.VMEM)
    dma = pltpu.SemaphoreType.DMA
    return pl.pallas_call(
        project_kernel,
        out_shape=(
            jax.ShapeDtypeStruct((2, rows, width), WIDE),
            jax.ShapeDtypeStruct((rows, width), LOW),
            jax.ShapeDtypeStruct((2, key_rows, width), LOW),
            jax.ShapeDtypeStruct((8, rows), WIDE),
        ),
        in_specs=[vmem] * 6,
        out_specs=(vmem,) * 4,
        scratch_shapes=[
            pltpu.VMEM((8, rows), WIDE),
            pltpu.VMEM((count, 8, rows), WIDE),
            dma((count - 1,)),
            dma((count - 1,)),
        ],
        compiler_params=pltpu.CompilerParams(
            collective_id=ident, has_side_effects=True, vmem_limit_bytes=56 << 20
        ),
        name="project",
    )(rows_low, weights, bias, gains, cosine, sine)


def unproject_kernel(
    width, query_grad_ref, kv_grad_ref, pre_ref, square_ref, gain_ref, cosine_ref, sine_ref,
    query_low_ref, key_low_ref, value_low_ref, sums_ref, work, stage, slots, send, recv,
):
    heads = query_grad_ref.shape[1] // HEAD_DIM
    tensor_barrier()
    stage[...] = jnp.zeros(stage.shape, WIDE)
    sums_ref[...] = jnp.zeros(sums_ref.shape, WIDE)
    total = square_ref[...]
    for part in range(2):
        terms = None
        rate = lanes_to_rows(lax.rsqrt(total[part : part + 1] / width + eps_norm))
        for head in range(heads):
            lanes = slice(head * HEAD_DIM, (head + 1) * HEAD_DIM)
            grads = query_grad_ref[:, lanes] if part == 0 else kv_grad_ref[0, :, lanes]
            grads = grads * cosine_ref[...] - pair_swap(grads) * sine_ref[...]
            pre = pre_ref[part, :, lanes]
            sums_ref[3 + part : 4 + part, lanes] = jnp.sum(
                grads * pre * rate, axis=0, keepdims=True
            )
            grads = grads * gain_ref[part : part + 1, lanes]
            work[part, :, lanes] = grads
            terms = grads * pre if terms is None else terms + grads * pre
        stage[part : part + 1] = rows_to_lanes(terms)
    tensor_send(stage, slots, send, recv)
    values = kv_grad_ref[1]
    sums_ref[2:3] = jnp.sum(values, axis=0, keepdims=True)
    value_low_ref[...] = values.astype(LOW)
    back_total = tensor_collect(stage, slots, send, recv)
    for part in range(2):
        rate_row = lax.rsqrt(total[part : part + 1] / width + eps_norm)
        rate = lanes_to_rows(rate_row)
        back = lanes_to_rows(rate_row * rate_row * rate_row * back_total[part : part + 1] / width)
        for head in range(heads):
            lanes = slice(head * HEAD_DIM, (head + 1) * HEAD_DIM)
            grads = work[part, :, lanes] * rate - pre_ref[part, :, lanes] * back
            sums_ref[part : part + 1, lanes] = jnp.sum(grads, axis=0, keepdims=True)
            if part == 0:
                query_low_ref[:, lanes] = grads.astype(LOW)
            else:
                key_low_ref[:, lanes] = grads.astype(LOW)


def unproject(query_grads, kv_grads, pre, squares, gains, cosine, sine, model_width, ident):
    rows, width = query_grads.shape
    count = lax.axis_size("tensor")
    vmem = pl.BlockSpec(memory_space=pltpu.VMEM)
    dma = pltpu.SemaphoreType.DMA
    return pl.pallas_call(
        functools.partial(unproject_kernel, model_width),
        out_shape=(jax.ShapeDtypeStruct((rows, width), LOW),) * 3
        + (jax.ShapeDtypeStruct((8, width), WIDE),),
        in_specs=[vmem] * 7,
        out_specs=(vmem,) * 4,
        scratch_shapes=[
            pltpu.VMEM((2, rows, width), WIDE),
            pltpu.VMEM((8, rows), WIDE),
            pltpu.VMEM((count, 8, rows), WIDE),
            dma((count - 1,)),
            dma((count - 1,)),
        ],
        compiler_params=pltpu.CompilerParams(
            collective_id=ident, has_side_effects=True, vmem_limit_bytes=56 << 20
        ),
        name="unproject",
    )(query_grads, kv_grads, pre, squares, gains, cosine, sine)


def seq_scatter_kernel(blocks_ref, out_ref, slots, send_sem, recv_sem):
    count = slots.shape[0]
    me = lax.axis_index("seq")
    barrier = pltpu.get_barrier_semaphore()
    for hop in range(1, count):
        pl.semaphore_signal(
            barrier, inc=1, device_id={"seq": lax.rem(me + hop, count)},
            device_id_type=pl.DeviceIdType.MESH)
    pl.semaphore_wait(barrier, count - 1)

    def copy(block, slot, hop, place):
        return pltpu.make_async_remote_copy(
            src_ref=blocks_ref.at[block], dst_ref=slots.at[slot], send_sem=send_sem.at[hop - 1],
            recv_sem=recv_sem.at[hop - 1], device_id={"seq": place},
            device_id_type=pl.DeviceIdType.MESH)

    for hop in range(1, count):
        place = lax.rem(me + hop, count)
        copy(place, me, hop, place).start()
    slots[pl.ds(me, 1)] = blocks_ref[pl.ds(me, 1)]
    for hop in range(1, count):
        origin = lax.rem(me + count - hop, count)
        copy(me, origin, hop, origin).wait_recv()
    for hop in range(1, count):
        place = lax.rem(me + hop, count)
        copy(place, me, hop, place).wait_send()
    total = slots[0].astype(WIDE)
    for slot in range(1, count):
        total = total + slots[slot].astype(WIDE)
    out_ref[...] = total


def seq_scatter(blocks, ident):
    count, rows, width = blocks.shape
    vmem = pl.BlockSpec(memory_space=pltpu.VMEM)
    return pl.pallas_call(
        seq_scatter_kernel,
        out_shape=jax.ShapeDtypeStruct((rows, width), WIDE),
        in_specs=[vmem],
        out_specs=vmem,
        scratch_shapes=[
            pltpu.VMEM((count, rows, width), LOW),
            pltpu.SemaphoreType.DMA((count - 1,)),
            pltpu.SemaphoreType.DMA((count - 1,)),
        ],
        compiler_params=pltpu.CompilerParams(collective_id=ident, has_side_effects=True),
        name="seq_scatter",
    )(blocks)


def head_sum(term):
    def add(heads):
        total = None
        for head in range(heads):
            piece = term(head, slice(head * HEAD_DIM, (head + 1) * HEAD_DIM))
            total = piece if total is None else total + piece
        return total

    return add


def cross_attend_kernel(
    rows_ref, text_ref, query_weight_ref, text_weight_ref, bias_ref, gain_ref,
    query_pre_ref, key_pre_ref, query_ref, kv_ref, square_ref, out_ref, turned_ref, total_ref,
    stage, slots, send, recv,
):
    heads = query_ref.shape[1] // HEAD_DIM
    width = rows_ref.shape[1]
    factor = LOG2E / math.sqrt(HEAD_DIM)
    tensor_barrier()
    stage[...] = jnp.zeros(stage.shape, WIDE)
    query_pre_ref[...] = (
        jnp.dot(rows_ref[...], query_weight_ref[...], preferred_element_type=WIDE)
        + bias_ref[0:1]
    )
    key_pre_ref[...] = (
        jnp.dot(text_ref[...], text_weight_ref[0], preferred_element_type=WIDE) + bias_ref[1:2]
    )
    for part, pre_ref in enumerate((query_pre_ref, key_pre_ref)):
        squares = head_sum(lambda head, lanes: pre_ref[:, lanes] * pre_ref[:, lanes])(heads)
        stage[part : part + 1, : pre_ref.shape[0]] = rows_to_lanes(squares)
    tensor_send(stage, slots, send, recv)
    values = jnp.dot(text_ref[...], text_weight_ref[1], preferred_element_type=WIDE)
    kv_ref[1] = (values + bias_ref[2:3]).astype(LOW)
    total = tensor_collect(stage, slots, send, recv)
    square_ref[...] = total
    for part, pre_ref in enumerate((query_pre_ref, key_pre_ref)):
        square = total[part : part + 1, : pre_ref.shape[0]]
        rate = lanes_to_rows(lax.rsqrt(square / width + eps_norm))
        for head in range(heads):
            lanes = slice(head * HEAD_DIM, (head + 1) * HEAD_DIM)
            normed = (pre_ref[:, lanes] * rate * gain_ref[part : part + 1, lanes]).astype(LOW)
            if part == 0:
                query_ref[:, lanes] = normed
            else:
                kv_ref[0, :, lanes] = normed

    def step(head, carry):
        lanes = head_lanes(head)
        scores = over_last(kv_ref[0, :, lanes], query_ref[:, lanes]) * factor
        peak = jnp.max(scores, axis=0, keepdims=True)
        terms = jnp.exp2(scores - peak)
        summed = jnp.sum(terms, axis=0, keepdims=True)
        attended = (
            lax.dot_general(
                kv_ref[1, :, lanes],
                terms.astype(LOW),
                (((0,), (0,)), ((), ())),
                preferred_element_type=WIDE,
            )
            / summed
        )
        turned_ref[head] = attended
        out_ref[:, lanes] = jnp.transpose(attended).astype(LOW)
        total_ref[head] = peak + jnp.log2(summed)
        return carry

    lax.fori_loop(0, heads, step, 0)


def cross_attend(rows_low, text_all, query_weight, text_weights, bias, gains, ident):
    rows = rows_low.shape[0]
    tokens = text_all.shape[0]
    width = query_weight.shape[1]
    heads = width // HEAD_DIM
    count = lax.axis_size("tensor")
    vmem = pl.BlockSpec(memory_space=pltpu.VMEM)
    dma = pltpu.SemaphoreType.DMA
    return pl.pallas_call(
        cross_attend_kernel,
        out_shape=(
            jax.ShapeDtypeStruct((rows, width), WIDE),
            jax.ShapeDtypeStruct((tokens, width), WIDE),
            jax.ShapeDtypeStruct((rows, width), LOW),
            jax.ShapeDtypeStruct((2, tokens, width), LOW),
            jax.ShapeDtypeStruct((8, rows), WIDE),
            jax.ShapeDtypeStruct((rows, width), LOW),
            jax.ShapeDtypeStruct((heads, HEAD_DIM, rows), WIDE),
            jax.ShapeDtypeStruct((heads, 1, rows), WIDE),
        ),
        in_specs=[vmem] * 6,
        out_specs=(vmem,) * 8,
        scratch_shapes=[
            pltpu.VMEM((8, rows), WIDE),
            pltpu.VMEM((count, 8, rows), WIDE),
            dma((count - 1,)),
            dma((count - 1,)),
        ],
        compiler_params=pltpu.CompilerParams(
            collective_id=ident, has_side_effects=True, vmem_limit_bytes=56 << 20
        ),
        name="cross_attend",
    )(rows_low, text_all, query_weight, text_weights, bias, gains)


def cross_back_kernel(
    width, query_ref, kv_ref, turned_ref, total_ref, grad_ref, query_pre_ref, key_pre_ref,
    square_ref, text_square_ref, gain_ref, query_low_ref, text_low_ref, sums_ref,
    centre, query_turned, work, text_work, leaving, landing, stage, slots, text_send, text_recv,
    send, recv,
):
    heads = query_ref.shape[1] // HEAD_DIM
    tokens = key_pre_ref.shape[0]
    scale = 1.0 / math.sqrt(HEAD_DIM)
    places = plane_places()
    count = slots.shape[0]
    mine = lax.axis_index("tensor")
    barrier = pltpu.get_barrier_semaphore()
    for place in places[1:]:
        pl.semaphore_signal(
            barrier, inc=1, device_id={"seq": place}, device_id_type=pl.DeviceIdType.MESH
        )
    for hop in range(1, count):
        pl.semaphore_signal(
            barrier, inc=1, device_id={"tensor": lax.rem(mine + hop, count)},
            device_id_type=pl.DeviceIdType.MESH)
    pl.semaphore_wait(barrier, 3 + count - 1)

    for head in range(heads):
        lanes = slice(head * HEAD_DIM, (head + 1) * HEAD_DIM)
        grads = jnp.transpose(grad_ref[:, lanes].astype(WIDE))
        centre[head] = jnp.sum(grads * turned_ref[head], axis=0, keepdims=True)
    stage[...] = jnp.zeros(stage.shape, WIDE)
    sums_ref[...] = jnp.zeros(sums_ref.shape, WIDE)

    def step(head, carry):
        lanes = head_lanes(head)
        keys = kv_ref[0, :, lanes]
        query = query_ref[:, lanes]
        grads = grad_ref[:, lanes]
        probs = jnp.exp2(over_last(keys, query) * (scale * LOG2E) - total_ref[head])
        grad_probs = over_last(kv_ref[1, :, lanes], grads)
        grad_scores = (probs * (grad_probs - centre[head])).astype(LOW)
        key_grads = jnp.dot(grad_scores, query, preferred_element_type=WIDE) * scale
        leaving[0, :, lanes] = key_grads.astype(LOW)
        value_grads = jnp.dot(probs.astype(LOW), grads, preferred_element_type=WIDE)
        leaving[1, :, lanes] = value_grads.astype(LOW)
        query_turned[head] = lax.dot_general(
            keys, grad_scores, (((0,), (0,)), ((), ())), preferred_element_type=WIDE
        )
        return carry

    lax.fori_loop(0, heads, step, 0)

    def owned(place):
        return pl.ds(pl.multiple_of(place * tokens, 16), tokens)

    def text_copy(relation, part):
        place = places[relation + 1]
        return plane_copy(
            leaving.at[part, owned(place)],
            landing.at[relation, part],
            text_send.at[relation, part],
            text_recv.at[relation, part],
            place,
        )

    for relation in (2, 1, 0):
        for part in range(2):
            text_copy(relation, part).start()

    rate_row = lax.rsqrt(square_ref[0:1] / width + eps_norm)
    rate = lanes_to_rows(rate_row)
    terms = None
    for head in range(heads):
        lanes = slice(head * HEAD_DIM, (head + 1) * HEAD_DIM)
        grads = jnp.transpose(query_turned[head]) * scale
        pre = query_pre_ref[:, lanes]
        sums_ref[3:4, lanes] = jnp.sum(grads * pre * rate, axis=0, keepdims=True)
        grads = grads * gain_ref[0:1, lanes]
        work[:, lanes] = grads
        terms = grads * pre if terms is None else terms + grads * pre
    stage[0:1] = rows_to_lanes(terms)

    for relation in range(3):
        for part in range(2):
            text_copy(relation, part).wait_recv()
    for part in range(2):
        total = leaving[part, owned(places[0])].astype(WIDE)
        for relation in range(3):
            total = total + landing[relation, part].astype(WIDE)
        text_work[part] = total
    text_row = lax.rsqrt(text_square_ref[0:1] / width + eps_norm)
    text_rate = lanes_to_rows(text_row)
    terms = None
    for head in range(heads):
        lanes = slice(head * HEAD_DIM, (head + 1) * HEAD_DIM)
        grads = text_work[0, :, lanes]
        pre = key_pre_ref[:, lanes]
        sums_ref[4:5, lanes] = jnp.sum(grads * pre * text_rate, axis=0, keepdims=True)
        grads = grads * gain_ref[1:2, lanes]
        text_work[0, :, lanes] = grads
        terms = grads * pre if terms is None else terms + grads * pre
    stage[1:2, :tokens] = rows_to_lanes(terms)

    tensor_send(stage, slots, send, recv)
    sums_ref[2:3] = jnp.sum(text_work[1], axis=0, keepdims=True)
    text_low_ref[1] = text_work[1].astype(LOW)
    back_total = tensor_collect(stage, slots, send, recv)
    back = lanes_to_rows(rate_row * rate_row * rate_row * back_total[0:1] / width)
    text_back = lanes_to_rows(text_row * text_row * text_row * back_total[1:2, :tokens] / width)
    for head in range(heads):
        lanes = slice(head * HEAD_DIM, (head + 1) * HEAD_DIM)
        grads = work[:, lanes] * rate - query_pre_ref[:, lanes] * back
        sums_ref[0:1, lanes] = jnp.sum(grads, axis=0, keepdims=True)
        query_low_ref[:, lanes] = grads.astype(LOW)
        grads = text_work[0, :, lanes] * text_rate - key_pre_ref[:, lanes] * text_back
        sums_ref[1:2, lanes] = jnp.sum(grads, axis=0, keepdims=True)
        text_low_ref[0, :, lanes] = grads.astype(LOW)
    for relation in range(3):
        for part in range(2):
            text_copy(relation, part).wait_send()


def cross_back(saved, grad_low, key_pre_own, text_squares, gains, model_width, ident):
    query_pre, _, query_low, kv_low, squares, _, turned, total = saved
    rows, width = query_low.shape
    heads = width // HEAD_DIM
    tokens = key_pre_own.shape[0]
    count = lax.axis_size("tensor")
    vmem = pl.BlockSpec(memory_space=pltpu.VMEM)
    dma = pltpu.SemaphoreType.DMA
    return pl.pallas_call(
        functools.partial(cross_back_kernel, model_width),
        out_shape=(
            jax.ShapeDtypeStruct((rows, width), LOW),
            jax.ShapeDtypeStruct((2, tokens, width), LOW),
            jax.ShapeDtypeStruct((8, width), WIDE),
        ),
        in_specs=[vmem] * 10,
        out_specs=(vmem,) * 3,
        scratch_shapes=[
            pltpu.VMEM((heads, 1, rows), WIDE),
            pltpu.VMEM((heads, HEAD_DIM, rows), WIDE),
            pltpu.VMEM((rows, width), WIDE),
            pltpu.VMEM((2, tokens, width), WIDE),
            pltpu.VMEM(kv_low.shape, LOW),
            pltpu.VMEM((3, 2, tokens, width), LOW),
            pltpu.VMEM((8, rows), WIDE),
            pltpu.VMEM((count, 8, rows), WIDE),
            dma((3, 2)),
            dma((3, 2)),
            dma((count - 1,)),
            dma((count - 1,)),
        ],
        compiler_params=pltpu.CompilerParams(
            collective_id=ident, has_side_effects=True, vmem_limit_bytes=56 << 20
        ),
        name="cross_back",
    )(
        query_low, kv_low, turned, total, grad_low, query_pre, key_pre_own, squares, text_squares,
        gains,
    )


def head_forward(query, keys, values, key_ok, score_scale):
    scores = (
        jnp.einsum("csh,clh->csl", query, keys, preferred_element_type=jnp.float32) * score_scale
    )
    scores = jnp.where(key_ok[:, None, :], scores, -jnp.inf)
    row_peak = jnp.max(scores, axis=-1, keepdims=True)
    exp_terms = jnp.exp(scores - row_peak)
    summed = jnp.sum(exp_terms, axis=-1, keepdims=True)
    probs_low = (exp_terms / summed).astype(jnp.bfloat16)
    attended = jnp.einsum("csl,clh->csh", probs_low, values, preferred_element_type=jnp.float32)
    return (attended, row_peak[..., 0] + jnp.log(summed[..., 0]))


def head_backward(query, keys, values, key_ok, log_total, grad_att, score_scale):
    scores = (
        jnp.einsum("csh,clh->csl", query, keys, preferred_element_type=jnp.float32) * score_scale
    )
    probs = jnp.where(key_ok[:, None, :], jnp.exp(scores - log_total[..., None]), 0.0)
    grad_probs = jnp.einsum("csh,clh->csl", grad_att, values, preferred_element_type=jnp.float32)
    centre = jnp.sum(probs * grad_probs, axis=-1)
    grad_scores = (probs * (grad_probs - centre[..., None])).astype(jnp.bfloat16)
    grad_query = (
        jnp.einsum("csl,clh->csh", grad_scores, keys, preferred_element_type=jnp.float32)
        * score_scale
    )
    grad_keys = (
        jnp.einsum("csl,csh->clh", grad_scores, query, preferred_element_type=jnp.float32)
        * score_scale
    )
    grad_values = jnp.einsum(
        "csl,csh->clh", probs.astype(jnp.bfloat16), grad_att, preferred_element_type=jnp.float32
    )
    return (grad_query, centre, grad_keys, grad_values)


def shards(
    hidden,
    teacher,
    text,
    time_embed,
    lengths,
    positions,
    modulation,
    self_in,
    self_bias,
    self_out,
    norm_gains,
    cross_gain,
    cross_shift,
    cross_q,
    cross_kv,
    cross_bias,
    cross_out,
    ffn_in,
    ffn_in_bias,
    ffn_out,
    out_bias,
):
    low_type = jnp.bfloat16
    wide_type = jnp.float32
    clip_count, seq_rows, model_width = hidden.shape
    local_width = self_in.shape[2]
    local_heads = local_width // HEAD_DIM
    text_local = text.shape[1]
    seq_count = lax.axis_size("seq")
    slot_count = seq_rows * seq_count
    text_count = text_local * seq_count
    flat_rows = clip_count * seq_rows
    score_scale = 1.0 / math.sqrt(HEAD_DIM)
    seq_place = lax.axis_index("seq")
    clip_first = lax.axis_index("dp") * clip_count
    clip_lengths = lax.dynamic_slice_in_dim(lengths, clip_first, clip_count)
    key_valid = jnp.arange(slot_count, dtype=jnp.int32)[None, :] < clip_lengths[:, None]
    row_ids = seq_place * seq_rows + jnp.arange(seq_rows, dtype=jnp.int32)
    row_valid = row_ids[None, :] < clip_lengths[:, None]
    text_valid = jnp.ones((clip_count, text_count), dtype=jnp.bool_)
    valid_total = jnp.sum(lengths).astype(wide_type)
    modulated = modulation[None] + time_embed
    cosine_rep, sine_rep = rope_tables(positions, HEAD_DIM)
    rotate_now = functools.partial(
        rotate, cosine_rep=cosine_rep, sine_rep=sine_rep, swap_matrix=swap_table(HEAD_DIM)
    )
    head_shape = (clip_count, seq_rows, local_heads, HEAD_DIM)
    clip_ids = jnp.arange(flat_rows, dtype=jnp.int32) // seq_rows
    clip_table = (clip_ids[:, None] == jnp.arange(clip_count, dtype=jnp.int32)[None, :]).astype(
        wide_type
    )
    valid_rows = row_valid.reshape(flat_rows)
    hidden_rows = hidden.reshape(flat_rows, model_width)
    teacher_rows = teacher.reshape(flat_rows, model_width)

    def per_row(index_no):
        return jnp.dot(clip_table, modulated[:, index_no], precision=lax.Precision.HIGHEST)

    def per_clip(values):
        return jnp.dot(clip_table.T, values, precision=lax.Precision.HIGHEST)

    scale_one = per_row(1)
    gate_one = per_row(2)
    scale_two = per_row(4)
    gate_two = per_row(5)
    normed_one = layer_norm(hidden_rows)
    query_pad = -flat_rows % 128
    key_pad = -flat_rows % 16

    def pad_queries(values):
        return jnp.pad(values, ((0, query_pad), (0, 0)))

    attn_in = pad_queries((normed_one * (1.0 + scale_one) + per_row(0)).astype(low_type))
    cosine_flat = pad_queries(cosine_rep.reshape(flat_rows, HEAD_DIM))
    sine_flat = pad_queries(sine_rep.reshape(flat_rows, HEAD_DIM)) * jnp.where(
        jnp.arange(HEAD_DIM) % 2 == 0, -1.0, 1.0
    )
    self_gains = norm_gains[:2]
    proj_pre, query_flat, own_kv, proj_squares = project(
        attn_in, self_in, self_bias, self_gains, cosine_flat, sine_flat, flat_rows + key_pad, 6
    )
    plane = seq_count == 4 and clip_count == 1
    if plane:
        attn_low, attn_turned, self_totals, got_kv = attend(
            query_flat, own_kv, clip_lengths, flat_rows, 10
        )
    else:
        query_low = query_flat[:flat_rows].reshape(head_shape)
        key_low = own_kv[0, :flat_rows]
        value_low = own_kv[1, :flat_rows]
        local_kv = jnp.stack(
            [
                key_low.reshape(clip_count, seq_rows, local_width),
                value_low.reshape(clip_count, seq_rows, local_width),
            ]
        )
        whole_kv = lax.all_gather(local_kv, "seq", axis=2, tiled=True)
        keys_all = whole_kv[0].reshape(clip_count, slot_count, local_heads, HEAD_DIM)
        values_all = whole_kv[1].reshape(clip_count, slot_count, local_heads, HEAD_DIM)
        att_heads = []
        total_heads = []
        for head_no in range(local_heads):
            attended, log_total = head_forward(
                query_low[:, :, head_no],
                keys_all[:, :, head_no],
                values_all[:, :, head_no],
                key_valid,
                score_scale,
            )
            att_heads.append(attended)
            total_heads.append(log_total)
        attn_low = jnp.stack(att_heads, axis=2).astype(low_type).reshape(flat_rows, local_width)
        attn_low = pad_queries(attn_low)
        self_totals = jnp.stack(total_heads)
    branch_one = (
        line_sum([(attn_low, self_out)], False, 0, flat_rows) + out_bias[0]
    )
    after_one = hidden_rows + branch_one * gate_one
    normed_three = layer_norm(after_one)
    cross_in = (normed_three * cross_gain + cross_shift).astype(low_type)
    text_low = text.astype(low_type)
    text_start = seq_place * text_local
    text_all = lax.all_gather(text_low, "seq", axis=1, tiled=True)
    cross_plane = plane and text_local % 128 == 0 and text_count <= flat_rows
    if cross_plane:
        cross_in = pad_queries(cross_in)
        cross_saved = cross_attend(
            cross_in, text_all[0], cross_q, cross_kv, cross_bias, norm_gains[2:], 7
        )
        cross_att_low = cross_saved[5]
    else:
        cross_query_pre = jnp.dot(cross_in, cross_q, preferred_element_type=wide_type) + cross_bias[0]
        text_proj = (
            jnp.einsum("ctd,kde->kcte", text_all, cross_kv, preferred_element_type=wide_type)
            + cross_bias[1:, None, None, :]
        )
        cross_sq, text_sq = small_sum(
            [
                jnp.sum(cross_query_pre * cross_query_pre, axis=-1),
                jnp.sum(text_proj[0] * text_proj[0], axis=-1),
            ],
            7,
        )
        text_rate_all = lax.rsqrt(text_sq / model_width + eps_norm)[..., None]
        text_key_low = (text_proj[0] * text_rate_all * norm_gains[3]).astype(low_type)
        text_value_low = text_proj[1].astype(low_type)
        text_key_pre = lax.dynamic_slice_in_dim(text_proj[0], text_start, text_local, 1)
        text_key_rate = lax.dynamic_slice_in_dim(text_rate_all, text_start, text_local, 1)
        cross_rate = lax.rsqrt(cross_sq / model_width + eps_norm)[:, None]
        cross_query_low = (
            (cross_query_pre * cross_rate * norm_gains[2]).astype(low_type).reshape(head_shape)
        )
        text_key_heads = text_key_low.reshape(clip_count, text_count, local_heads, HEAD_DIM)
        text_value_heads = text_value_low.reshape(clip_count, text_count, local_heads, HEAD_DIM)
        cross_heads = []
        cross_total_heads = []
        for head_no in range(local_heads):
            attended, log_total = head_forward(
                cross_query_low[:, :, head_no],
                text_key_heads[:, :, head_no],
                text_value_heads[:, :, head_no],
                text_valid,
                score_scale,
            )
            cross_heads.append(attended)
            cross_total_heads.append(log_total)
        cross_att_low = jnp.stack(cross_heads, axis=2).astype(low_type).reshape(flat_rows, local_width)
        cross_totals = jnp.stack(cross_total_heads)
    branch_two = (
        line_sum([(cross_att_low, cross_out)], False, 1, flat_rows)
        + out_bias[1]
    )
    after_two = after_one + branch_two
    normed_two = layer_norm(after_two)
    ffn_input = (normed_two * (1.0 + scale_two) + per_row(3)).astype(low_type)
    pre_act = jnp.dot(ffn_input, ffn_in, preferred_element_type=wide_type) + ffn_in_bias
    act_low = gelu_tanh(pre_act).astype(low_type)
    branch_three = (
        line_sum([(act_low, ffn_out)], False, 2, flat_rows) + out_bias[2]
    )
    result = after_two + branch_three * gate_two
    residue = jnp.where(valid_rows[:, None], result - teacher_rows, 0.0)
    grad_three = residue * gate_two
    grad_three_low = grad_three.astype(low_type)
    ffn_out_mix = jnp.dot(grad_three_low.T, act_low, preferred_element_type=wide_type)
    grad_act = jnp.dot(grad_three_low, ffn_out.T, preferred_element_type=wide_type)
    grad_pre = jax.vjp(gelu_tanh, pre_act)[1](grad_act)[0]
    grad_pre_low = grad_pre.astype(low_type)
    grad_pre_low, ffn_out_mix = lax.optimization_barrier(
        (grad_pre_low, row_major(ffn_out_mix.astype(low_type)))
    )
    part_ffn_out = scatter_rows(ffn_out_mix, 0)
    ffn_in_mix = jnp.dot(ffn_input.T, grad_pre_low, preferred_element_type=wide_type)
    grad_ffn_bias = jnp.sum(grad_pre, axis=0)
    grad_ffn_input = line_sum([(grad_pre_low, ffn_in)], True, 3, flat_rows)
    grad_after_two = (
        residue + jax.vjp(layer_norm, after_two)[1](grad_ffn_input * (1.0 + scale_two))[0]
    )
    grad_two_low = grad_after_two.astype(low_type)
    cross_out_mix = jnp.dot(grad_two_low.T, cross_att_low[:flat_rows], preferred_element_type=wide_type)
    grad_cross_att = (
        jnp.dot(grad_two_low, cross_out.T, preferred_element_type=wide_type).astype(low_type)
    )
    if cross_plane:
        grad_cross_query_low, text_grad_low, cross_sums = cross_back(
            cross_saved,
            pad_queries(grad_cross_att),
            lax.dynamic_slice_in_dim(cross_saved[1], text_start, text_local, 0),
            lax.dynamic_slice_in_dim(
                jnp.broadcast_to(cross_saved[4][1:2, :text_count], (8, text_count)),
                text_start,
                text_local,
                1,
            ),
            norm_gains[2:],
            model_width,
            8,
        )
        text_grad_low = text_grad_low[:, None]
        grad_cross_bias = cross_sums[:3]
        gain_cross_query = cross_sums[3]
        gain_text_key = cross_sums[4]
    else:
        grad_cross_att = grad_cross_att.reshape(head_shape)
        cross_query_grads = []
        text_key_grads = []
        text_value_grads = []
        for head_no in range(local_heads):
            head_grads = head_backward(
                cross_query_low[:, :, head_no],
                text_key_heads[:, :, head_no],
                text_value_heads[:, :, head_no],
                text_valid,
                cross_totals[head_no],
                grad_cross_att[:, :, head_no],
                score_scale,
            )
            cross_query_grads.append(head_grads[0])
            text_key_grads.append(head_grads[2])
            text_value_grads.append(head_grads[3])
        grad_cross_query = jnp.stack(cross_query_grads, axis=2).reshape(flat_rows, local_width)
        text_grads_all = jnp.stack(
            [
                jnp.stack(text_key_grads, axis=2).reshape(clip_count, text_count, local_width),
                jnp.stack(text_value_grads, axis=2).reshape(clip_count, text_count, local_width),
            ]
        )
        text_blocks = text_grads_all.astype(low_type).reshape(
            2, clip_count, seq_count, text_local, local_width
        )
        text_blocks = jnp.transpose(text_blocks, (2, 1, 3, 0, 4)).reshape(
            seq_count, clip_count * text_local, 2 * local_width
        )
        text_rows = seq_scatter(text_blocks, 14)
        text_grads = [
            text_rows[:, j * local_width : (j + 1) * local_width].reshape(
                clip_count, text_local, local_width
            )
            for j in range(2)
        ]
        query_term, key_term = small_sum(
            [
                jnp.sum(grad_cross_query * norm_gains[2] * cross_query_pre, axis=-1),
                jnp.sum(text_grads[0] * norm_gains[3] * text_key_pre, axis=-1),
            ],
            8,
        )
        grad_cross_query_pre = (
            grad_cross_query * norm_gains[2] * cross_rate
            - cross_query_pre * cross_rate**3 * query_term[:, None] / model_width
        )
        gain_cross_query = jnp.sum(grad_cross_query * cross_query_pre * cross_rate, axis=0)
        grad_cross_query_low = grad_cross_query_pre.astype(low_type)
        grad_text_key_pre = (
            text_grads[0] * norm_gains[3] * text_key_rate
            - text_key_pre * text_key_rate**3 * key_term[..., None] / model_width
        )
        gain_text_key = jnp.sum(text_grads[0] * text_key_pre * text_key_rate, axis=(0, 1))
        grad_cross_bias = jnp.stack(
            [
                jnp.sum(grad_cross_query_pre, axis=0),
                jnp.sum(grad_text_key_pre, axis=(0, 1)),
                jnp.sum(text_grads[1], axis=(0, 1)),
            ]
        )
        text_grad_low = jnp.stack([grad_text_key_pre, text_grads[1]]).astype(low_type)
    grad_cross_query_low, ffn_in_mix, part_ffn_out = lax.optimization_barrier(
        (grad_cross_query_low, row_major(ffn_in_mix.astype(low_type)), part_ffn_out)
    )
    part_ffn_in = scatter_rows(ffn_in_mix, 0)
    cross_q_mix = jnp.dot(cross_in.T, grad_cross_query_low, preferred_element_type=wide_type)
    grad_cross_in = line_sum([(grad_cross_query_low, cross_q)], True, 4, flat_rows)
    cross_kv_mix = jnp.einsum(
        "ctd,kcte->kde", text_low, text_grad_low, preferred_element_type=wide_type
    )
    grad_text = lax.psum(
        jnp.einsum(
            "kcte,kde->ctd", text_grad_low, cross_kv, preferred_element_type=wide_type
        ).astype(jnp.bfloat16),
        "tensor",
    ).astype(jnp.float32)
    grad_cross_gain = jnp.sum(grad_cross_in * normed_three, axis=0)
    grad_cross_shift = jnp.sum(grad_cross_in, axis=0)
    grad_after_one = (
        grad_after_two + jax.vjp(layer_norm, after_one)[1](grad_cross_in * cross_gain)[0]
    )
    grad_one = grad_after_one * gate_one
    grad_one_low = grad_one.astype(low_type)
    self_out_mix = jnp.dot(grad_one_low.T, attn_low[:flat_rows], preferred_element_type=wide_type)
    grad_attn = (
        jnp.dot(grad_one_low, self_out.T, preferred_element_type=wide_type)
        .astype(low_type)
        .reshape(head_shape)
    )
    group_mix = jnp.concatenate(
        [cross_out_mix, cross_q_mix, self_out_mix, cross_kv_mix[0], cross_kv_mix[1]], axis=-1
    ).astype(low_type)
    grad_attn, group_mix = lax.optimization_barrier((grad_attn, row_major(group_mix)))
    part_group = scatter_rows(group_mix, 0)
    if plane:
        query_grads, kv_grads = attend_back(
            query_flat,
            own_kv,
            got_kv,
            attn_turned,
            self_totals,
            pad_queries(grad_attn.reshape(flat_rows, local_width)),
            clip_lengths,
            flat_rows,
            11,
        )
    else:
        query_grads = []
        key_grads = []
        value_grads = []
        for head_no in range(local_heads):
            head_grads = head_backward(
                query_low[:, :, head_no],
                keys_all[:, :, head_no],
                values_all[:, :, head_no],
                key_valid,
                self_totals[head_no],
                grad_attn[:, :, head_no],
                score_scale,
            )
            query_grads.append(head_grads[0])
            key_grads.append(head_grads[2])
            value_grads.append(head_grads[3])
        owner_grads = [
            jnp.stack(parts, axis=2)
            .astype(jnp.bfloat16)
            .reshape(clip_count, seq_count, seq_rows, local_width)
            for parts in (key_grads, value_grads)
        ]
        owner_grads = jnp.concatenate(
            [
                jnp.swapaxes(part, 0, 1).reshape(seq_count, flat_rows, local_width)
                for part in owner_grads
            ],
            axis=-1,
        )
        pad_rows = -flat_rows % 16
        owner_grads = jnp.pad(owner_grads, ((0, 0), (0, pad_rows), (0, 0)))
        kv_rows = lax.psum_scatter(
            owner_grads.reshape(seq_count * (flat_rows + pad_rows), 2 * local_width),
            "seq",
            scatter_dimension=0,
            tiled=True,
        )[:flat_rows].astype(jnp.float32)
        kv_grads = jnp.stack(
            [pad_queries(kv_rows[:, :local_width]), pad_queries(kv_rows[:, local_width:])]
        )
        query_grads = pad_queries(
            jnp.stack(query_grads, axis=2).reshape(flat_rows, local_width)
        )
    query_grads, part_ffn_in = lax.optimization_barrier((query_grads, part_ffn_in))
    *grad_proj_low, proj_sums = unproject(
        query_grads,
        kv_grads,
        proj_pre,
        proj_squares,
        self_gains,
        cosine_flat,
        sine_flat,
        model_width,
        9,
    )
    grad_self_bias = proj_sums[:3]
    self_in_mix = jnp.concatenate(
        [
            jnp.dot(attn_in.T, grad_proj_low[j], preferred_element_type=wide_type).astype(low_type)
            for j in range(3)
        ],
        axis=-1,
    )
    grad_proj_low, self_in_mix, part_group = lax.optimization_barrier(
        (grad_proj_low, row_major(self_in_mix), part_group)
    )
    part_self_in = scatter_rows(self_in_mix, 0)
    grad_attn_in = line_sum([(grad_proj_low[j], self_in[j]) for j in range(3)], True, 5, flat_rows)
    grad_hidden = (
        grad_after_one + jax.vjp(layer_norm, hidden_rows)[1](grad_attn_in * (1.0 + scale_one))[0]
    )
    grad_time_local = jnp.stack(
        [
            per_clip(grad_attn_in),
            per_clip(grad_attn_in * normed_one),
            per_clip(grad_after_one * branch_one),
            per_clip(grad_ffn_input),
            per_clip(grad_ffn_input * normed_two),
            per_clip(residue * branch_three),
        ],
        axis=1,
    )
    grad_out_bias = jnp.stack(
        [jnp.sum(grad_one, axis=0), jnp.sum(grad_after_two, axis=0), jnp.sum(grad_three, axis=0)]
    )
    stream_values = (
        grad_time_local,
        grad_cross_gain,
        grad_cross_shift,
        grad_out_bias,
        jnp.sum(residue * residue),
    )
    grad_time_local, grad_cross_gain, grad_cross_shift, grad_out_bias, square_local = stream_values
    grad_norm_gains = jnp.concatenate(
        [proj_sums[3:5], gain_cross_query[None], gain_text_key[None]]
    )
    time_pair, sums = plane_sum(
        grad_time_local,
        [
            grad_self_bias,
            grad_norm_gains,
            grad_cross_gain,
            grad_cross_shift,
            grad_cross_bias,
            grad_ffn_bias,
            grad_out_bias,
            square_local,
        ],
        13,
    )
    grad_time, time_all = time_pair
    sum_modulation = jnp.sum(time_all, axis=0)
    (
        sum_self_bias,
        sum_gains,
        sum_cross_gain,
        sum_cross_shift,
        sum_cross_bias,
        sum_ffn_bias,
        sum_out_bias,
        square_sum,
    ) = sums
    loss = square_sum / (valid_total * model_width)
    part_ffn_in = part_ffn_in.astype(wide_type)
    part_ffn_out = part_ffn_out.T.astype(wide_type)
    pieces = [
        part_group[:, j * local_width : (j + 1) * local_width].astype(wide_type) for j in range(5)
    ]
    part_cross_out = pieces[0].T
    part_cross_q = pieces[1]
    part_self_out = pieces[2].T
    part_cross_kv = jnp.stack([pieces[3], pieces[4]])
    part_self_in = jnp.stack(
        [part_self_in[:, j * local_width : (j + 1) * local_width] for j in range(3)]
    ).astype(wide_type)
    result_out = result.reshape(clip_count, seq_rows, model_width)
    grad_hidden_out = grad_hidden.reshape(clip_count, seq_rows, model_width)
    return (
        result_out,
        loss,
        grad_hidden_out,
        grad_text,
        grad_time,
        sum_modulation,
        part_self_in,
        sum_self_bias,
        part_self_out,
        sum_gains,
        sum_cross_gain,
        sum_cross_shift,
        part_cross_q,
        part_cross_kv,
        sum_cross_bias,
        part_cross_out,
        part_ffn_in,
        sum_ffn_bias,
        part_ffn_out,
        sum_out_bias,
    )


def solution(mesh):
    placed = (
        P("dp", "seq", None),
        P("dp", "seq", None),
        P("dp", "seq", None),
        P("dp", None, None),
        P(),
        P(None, "dp", "seq"),
        P(),
        P(None, None, "tensor"),
        P(None, "tensor"),
        P("tensor", None),
        P(None, "tensor"),
        P(),
        P(),
        P(None, "tensor"),
        P(None, None, "tensor"),
        P(None, "tensor"),
        P("tensor", None),
        P(None, "tensor"),
        P("tensor"),
        P("tensor", None),
        P(),
    )
    return jax.shard_map(
        shards,
        mesh=mesh,
        in_specs=placed,
        out_specs=(
            P("dp", "seq", None),
            P(),
            P("dp", "seq", None),
            P("dp", "seq", None),
            P("dp", None, None),
            P(),
            P(None, ("dp", "seq"), "tensor"),
            P(None, "tensor"),
            P("tensor", ("dp", "seq")),
            P(None, "tensor"),
            P(),
            P(),
            P(("dp", "seq"), "tensor"),
            P(None, ("dp", "seq"), "tensor"),
            P(None, "tensor"),
            P("tensor", ("dp", "seq")),
            P(("dp", "seq"), "tensor"),
            P("tensor"),
            P("tensor", ("dp", "seq")),
            P(),
        ),
        check_vma=False,
    )
```

```python
import functools
import math

import jax
import jax.numpy as jnp
from jax import lax
from jax.experimental import pallas as pl
from jax.experimental.pallas import tpu as pltpu
from jax.experimental.layout import Layout, with_layout_constraint
from jax.sharding import PartitionSpec as P

HEAD_DIM = 128
LOW = jnp.bfloat16
WIDE = jnp.float32


eps_norm = 1e-06


def layer_norm(values):
    centred = values - jnp.mean(values, axis=-1, keepdims=True)
    return centred * lax.rsqrt(jnp.mean(centred * centred, axis=-1, keepdims=True) + eps_norm)


def gelu_tanh(values):
    return (
        0.5
        * values
        * (1.0 + jnp.tanh(0.7978845608028654 * (values + 0.044715 * values * values * values)))
    )


def rope_tables(positions, head_size):
    sixth_part = head_size // 6
    part_spans = (head_size - 4 * sixth_part, 2 * sixth_part, 2 * sixth_part)
    pieces = []
    for axis_no in range(3):
        span_now = part_spans[axis_no]
        inverse = 1.0 / 10000.0 ** (jnp.arange(0, span_now, 2).astype(jnp.float32) / span_now)
        pieces.append(positions[axis_no].astype(jnp.float32)[..., None] * inverse)
    angles = jnp.concatenate(pieces, axis=-1)
    cosine_rep = jnp.repeat(jnp.cos(angles), 2, axis=-1)[..., None, :]
    sine_rep = jnp.repeat(jnp.sin(angles), 2, axis=-1)[..., None, :]
    return (cosine_rep, sine_rep)


def swap_table(head_size):
    row_no = jnp.arange(head_size)[:, None]
    col_no = jnp.arange(head_size)[None, :]
    upward = jnp.where((row_no % 2 == 0) & (col_no == row_no + 1), 1.0, 0.0)
    downward = jnp.where((row_no % 2 == 1) & (col_no == row_no - 1), -1.0, 0.0)
    return (upward + downward).astype(jnp.float32)


def rotate(values, cosine_rep, sine_rep, swap_matrix):
    swapped = jnp.matmul(values, swap_matrix, precision=lax.Precision.HIGHEST)
    return values * cosine_rep + swapped * sine_rep


def line_kernel(count, block, group, lag, lag2, turned, *refs):
    lhs_refs = refs[:count]
    stacked = len(refs[count].shape) == 3
    rhs_count = 1 if stacked else count
    rhs_refs = [refs[count].at[j] for j in range(count)] if stacked else refs[count : 2 * count]
    out_ref, raw, part, stage, cross, raw_s, raw_r, mid_s, mid_r, far_s, far_r, near_s, near_r = refs[count + rhs_count :]
    steps = out_ref.shape[0] // block
    me = lax.axis_index("tensor")
    inner = (me == 1) | (me == 2)
    outer = jnp.logical_not(inner)
    leaf = jnp.where(me < 2, 0, 3)
    hub = jnp.where(me < 2, 1, 2)
    mate = 3 - me
    side = jnp.where(me < 2, 0, 1)

    def signal(where):
        pl.semaphore_signal(
            pltpu.get_barrier_semaphore(), inc=1, device_id={"tensor": where},
            device_id_type=pl.DeviceIdType.MESH)

    @pl.when(outer)
    def _():
        signal(hub)
        pl.semaphore_wait(pltpu.get_barrier_semaphore(), 1)

    @pl.when(inner)
    def _():
        signal(leaf)
        signal(mate)
        pl.semaphore_wait(pltpu.get_barrier_semaphore(), 2)

    def rows_of(step):
        return pl.ds(pl.multiple_of(step * block, 16), block)

    def remote(src, dst, send, recv, step, where):
        at = rows_of(step)
        return pltpu.make_async_remote_copy(
            src_ref=src.at[at], dst_ref=dst.at[at], send_sem=send.at[step], recv_sem=recv.at[step],
            device_id={"tensor": where}, device_id_type=pl.DeviceIdType.MESH)

    def raw_copy(step):
        return remote(raw, raw, raw_s, raw_r, step, hub)

    def mid_copy(step):
        return remote(stage, cross, mid_s, mid_r, step, mate)

    def far_copy(step):
        return remote(out_ref, out_ref, far_s, far_r, step, mate)

    def near_copy(step):
        return remote(out_ref, out_ref, near_s, near_r, step, leaf)

    def body(step, carry):
        @pl.when((step < steps) & (lax.rem(step, group) == 0))
        def _():
            at = pl.ds(pl.multiple_of(step * block, 16), block * group)
            total = None
            for lhs, rhs in zip(lhs_refs, rhs_refs):
                term = lax.dot_general(lhs[at], rhs[...], (((1,), (1 if turned else 0,)), ((), ())),
                    preferred_element_type=WIDE)
                total = term if total is None else total + term
            part[at] = total

        @pl.when(outer & (step < steps))
        def _():
            at = rows_of(step)
            raw[at] = part[at].astype(LOW)
            raw_copy(step).start()

        late = step - lag2
        @pl.when(inner & (late >= 0) & (late < steps) & (lax.rem(late + 2 * lag2, 2) != side))
        def _():
            far_copy(late).wait_recv()
            near_copy(late).start()

        near = step - lag
        @pl.when(inner & (near >= 0) & (near < steps) & (lax.rem(near + 2 * lag2, 2) == side))
        def _():
            at = rows_of(near)
            mid_copy(near).wait_recv()
            out_ref[at] = (part[at] + cross[at].astype(WIDE)).astype(LOW)
            far_copy(near).start()
            near_copy(near).start()

        @pl.when(inner & (step < steps))
        def _():
            at = rows_of(step)
            raw_copy(step).wait_recv()

            @pl.when(lax.rem(step, 2) == side)
            def _():
                part[at] = part[at] + raw[at].astype(WIDE)

            @pl.when(lax.rem(step, 2) != side)
            def _():
                stage[at] = (part[at] + raw[at].astype(WIDE)).astype(LOW)
                mid_copy(step).start()

        return carry

    lax.fori_loop(0, steps + lag2, body, 0)

    def drain(step, carry):
        @pl.when(outer)
        def _():
            near_copy(step).wait_recv()
            raw_copy(step).wait_send()

        @pl.when(inner)
        def _():
            near_copy(step).wait_send()

            @pl.when(lax.rem(step, 2) == side)
            def _():
                far_copy(step).wait_send()

            @pl.when(lax.rem(step, 2) != side)
            def _():
                mid_copy(step).wait_send()

        return carry

    lax.fori_loop(0, steps, drain, 0)

def line_sum(sources, weights, turned, ident, true_rows, block=16, group=7, lag=4, lag2=8):
    width = weights[0].shape[-2 if turned else -1]
    unit = block * group
    rows = -(-true_rows // unit) * unit
    sources = [jnp.pad(lhs, ((0, max(rows - lhs.shape[0], 0)), (0, 0))) for lhs in sources]
    steps = rows // block
    dma = pltpu.SemaphoreType.DMA
    depth = sum(lhs.shape[1] for lhs in sources)
    return pl.pallas_call(
        functools.partial(line_kernel, len(sources), block, group, lag, lag2, turned),
        out_shape=jax.ShapeDtypeStruct((rows, width), LOW),
        in_specs=[pl.BlockSpec(memory_space=pltpu.VMEM)] * (len(sources) + len(weights)),
        out_specs=pl.BlockSpec(memory_space=pltpu.VMEM),
        scratch_shapes=[
            pltpu.VMEM((rows, width), LOW),
            pltpu.VMEM((rows, width), WIDE),
            pltpu.VMEM((rows, width), LOW),
            pltpu.VMEM((rows, width), LOW),
        ] + [dma((steps,))] * 8,
        compiler_params=pltpu.CompilerParams(collective_id=ident, has_side_effects=True, vmem_limit_bytes=60 << 20),
        cost_estimate=pl.CostEstimate(flops=2 * rows * width * depth, bytes_accessed=230 * 10**6, transcendentals=0),
        name=f"line_sum_{ident}",
    )(*sources, *weights)[:true_rows].astype(WIDE)

def row_major(values):
    return with_layout_constraint(values, Layout((0, 1)))


def scatter_rows(mix, dimension):
    return lax.psum_scatter(mix, ("dp", "seq"), scatter_dimension=dimension, tiled=True)


def plane_sum_kernel(seq_count, value_ref, seq_ref, all_ref, slots, send_sem, recv_sem):
    count = slots.shape[0]
    dp = lax.axis_index("dp")
    me = dp * seq_count + lax.axis_index("seq")

    def device(place):
        return {"dp": place // seq_count, "seq": lax.rem(place, seq_count)}

    barrier = pltpu.get_barrier_semaphore()
    for hop in range(1, count):
        pl.semaphore_signal(
            barrier, inc=1, device_id=device(lax.rem(me + hop, count)),
            device_id_type=pl.DeviceIdType.MESH)
    pl.semaphore_wait(barrier, count - 1)

    def copy(slot, hop, place):
        return pltpu.make_async_remote_copy(
            src_ref=value_ref, dst_ref=slots.at[slot], send_sem=send_sem.at[hop - 1],
            recv_sem=recv_sem.at[hop - 1], device_id=device(place),
            device_id_type=pl.DeviceIdType.MESH)

    for hop in range(1, count):
        copy(me, hop, lax.rem(me + hop, count)).start()
    slots[pl.ds(me, 1)] = value_ref[...][None]
    for hop in range(1, count):
        origin = lax.rem(me + count - hop, count)
        copy(origin, hop, origin).wait_recv()
    for hop in range(1, count):
        copy(me, hop, lax.rem(me + hop, count)).wait_send()

    def span(start):
        total = slots[start].astype(WIDE)
        for slot in range(1, seq_count):
            total = total + slots[start + slot].astype(WIDE)
        return total

    seq_ref[...] = span(dp * seq_count)
    total = span(0)
    for part in range(1, count // seq_count):
        total = total + span(part * seq_count)
    all_ref[...] = total


def plane_sum(first, values, ident):
    seq_count = lax.axis_size("seq")
    count = lax.axis_size("dp") * seq_count
    flat = jnp.concatenate([value.reshape(-1).astype(LOW) for value in [first] + values])
    size = flat.shape[0]
    lines = -(-size // 2048) * 16
    packed = jnp.pad(flat, (0, lines * 128 - size)).reshape(lines, 128)
    vmem = pl.BlockSpec(memory_space=pltpu.VMEM)
    seq_total, all_total = pl.pallas_call(
        functools.partial(plane_sum_kernel, seq_count),
        out_shape=(jax.ShapeDtypeStruct((lines, 128), WIDE),) * 2,
        in_specs=[vmem],
        out_specs=(vmem, vmem),
        scratch_shapes=[
            pltpu.VMEM((count, lines, 128), LOW),
            pltpu.SemaphoreType.DMA((count - 1,)),
            pltpu.SemaphoreType.DMA((count - 1,)),
        ],
        compiler_params=pltpu.CompilerParams(collective_id=ident, has_side_effects=True),
        name="plane_sum",
    )(packed)
    all_total = all_total.reshape(-1)
    first_pair = (
        seq_total.reshape(-1)[: first.size].reshape(first.shape),
        all_total[: first.size].reshape(first.shape),
    )
    outs = []
    start = first.size
    for value in values:
        outs.append(all_total[start : start + value.size].reshape(value.shape))
        start += value.size
    return first_pair, outs


def small_kernel(value_ref, out_ref, slots, send_sem, recv_sem):
    count = slots.shape[0]
    me = lax.axis_index("tensor")
    barrier = pltpu.get_barrier_semaphore()
    for hop in range(1, count):
        pl.semaphore_signal(
            barrier, inc=1, device_id={"tensor": lax.rem(me + hop, count)},
            device_id_type=pl.DeviceIdType.MESH)
    pl.semaphore_wait(barrier, count - 1)
    copies = []
    for hop in range(1, count):
        copy = pltpu.make_async_remote_copy(
            src_ref=value_ref, dst_ref=slots.at[me], send_sem=send_sem.at[hop - 1],
            recv_sem=recv_sem.at[hop - 1], device_id={"tensor": lax.rem(me + hop, count)},
            device_id_type=pl.DeviceIdType.MESH)
        copy.start()
        copies.append(copy)
    slots[pl.ds(me, 1)] = value_ref[...][None]
    for hop in range(1, count):
        origin = lax.rem(me + count - hop, count)
        pltpu.make_async_remote_copy(
            src_ref=value_ref, dst_ref=slots.at[origin], send_sem=send_sem.at[hop - 1],
            recv_sem=recv_sem.at[hop - 1], device_id={"tensor": origin},
            device_id_type=pl.DeviceIdType.MESH).wait_recv()
    for copy in copies:
        copy.wait_send()
    total = slots[0]
    for slot in range(1, count):
        total = total + slots[slot]
    out_ref[...] = total


def small_sum(values, ident):
    count = lax.axis_size("tensor")
    flat = jnp.concatenate([value.reshape(-1) for value in values])
    size = flat.shape[0]
    lines = -(-size // 1024) * 8
    packed = jnp.pad(flat, (0, lines * 128 - size)).reshape(lines, 128)
    summed = pl.pallas_call(
        small_kernel,
        out_shape=jax.ShapeDtypeStruct((lines, 128), WIDE),
        in_specs=[pl.BlockSpec(memory_space=pltpu.VMEM)],
        out_specs=pl.BlockSpec(memory_space=pltpu.VMEM),
        scratch_shapes=[
            pltpu.VMEM((count, lines, 128), WIDE),
            pltpu.SemaphoreType.DMA((count - 1,)),
            pltpu.SemaphoreType.DMA((count - 1,)),
        ],
        compiler_params=pltpu.CompilerParams(collective_id=ident, has_side_effects=True),
        name=f"small_sum_{ident}",
    )(packed).reshape(-1)
    outs = []
    start = 0
    for value in values:
        outs.append(summed[start : start + value.size].reshape(value.shape))
        start += value.size
    return outs


LOG2E = 1.4426950408889634
HIDDEN_SCORE = -1e30


def plane_places():
    me = lax.axis_index("seq")
    column = lax.rem(me, 2)
    line = me // 2
    return (me, me + 1 - 2 * column, me + 2 - 4 * line, 3 - me)


def plane_barrier(places):
    barrier = pltpu.get_barrier_semaphore()
    for place in places[1:]:
        pl.semaphore_signal(
            barrier, inc=1, device_id={"seq": place}, device_id_type=pl.DeviceIdType.MESH
        )
    pl.semaphore_wait(barrier, 3)


def plane_copy(src, dst, send, recv, place):
    return pltpu.make_async_remote_copy(
        src_ref=src,
        dst_ref=dst,
        send_sem=send,
        recv_sem=recv,
        device_id={"seq": place},
        device_id_type=pl.DeviceIdType.MESH,
    )


def head_lanes(head):
    return pl.ds(pl.multiple_of(head * HEAD_DIM, 128), HEAD_DIM)


def block_valid(key_rows, owner, true_rows, length):
    row = lax.broadcasted_iota(jnp.int32, (key_rows, 1), 0)
    return (row < true_rows) & (owner * true_rows + row < length)


def over_last(lhs, rhs):
    return lax.dot_general(lhs, rhs, (((1,), (1,)), ((), ())), preferred_element_type=WIDE)


def attend_kernel(
    true_rows, length_ref, query_ref, kv_ref, out_ref, turned_ref, total_ref, got_ref, peak, summed, send, recv
):
    places = plane_places()
    plane_barrier(places)
    heads = query_ref.shape[1] // HEAD_DIM
    key_rows = kv_ref.shape[1]
    length = length_ref[0]
    factor = LOG2E / math.sqrt(HEAD_DIM)

    def own_copy(relation, part):
        index = 2 * relation + part
        return plane_copy(
            kv_ref.at[part], got_ref.at[relation, part], send.at[index], recv.at[index], places[relation + 1]
        )

    key_pass = plane_copy(got_ref.at[0, 0], got_ref.at[2, 0], send.at[4], recv.at[4], places[2])
    value_pass = plane_copy(got_ref.at[1, 1], got_ref.at[2, 1], send.at[5], recv.at[5], places[1])
    for part in range(2):
        for relation in range(2):
            own_copy(relation, part).start()

    peak[...] = jnp.full(peak.shape, HIDDEN_SCORE, WIDE)
    summed[...] = jnp.zeros(summed.shape, WIDE)
    turned_ref[...] = jnp.zeros(turned_ref.shape, WIDE)

    def block(source, owner):
        def step(head, carry):
            lanes = head_lanes(head)
            scores = over_last(source(0, lanes), query_ref[:, lanes]) * factor
            scores = jnp.where(block_valid(key_rows, owner, true_rows, length), scores, HIDDEN_SCORE)
            before = peak[head]
            after = jnp.maximum(before, jnp.max(scores, axis=0, keepdims=True))
            shrink = jnp.exp2(before - after)
            terms = jnp.exp2(scores - after)
            peak[head] = after
            summed[head] = summed[head] * shrink + jnp.sum(terms, axis=0, keepdims=True)
            turned_ref[head] = turned_ref[head] * shrink + lax.dot_general(
                source(1, lanes),
                terms.astype(LOW),
                (((0,), (0,)), ((), ())),
                preferred_element_type=WIDE,
            )

            return carry

        lax.fori_loop(0, heads, step, 0)

    block(lambda part, lanes: kv_ref[part, :, lanes], places[0])
    own_copy(0, 0).wait_recv()
    key_pass.start()
    own_copy(0, 1).wait_recv()
    own_copy(1, 1).wait_recv()
    value_pass.start()
    own_copy(1, 0).wait_recv()
    for relation in range(3):
        if relation == 2:
            key_pass.wait_recv()
            value_pass.wait_recv()
        block(
            lambda part, lanes, relation=relation: got_ref[relation, part, :, lanes],
            places[relation + 1],
        )

    for head in range(heads):
        lanes = slice(head * HEAD_DIM, (head + 1) * HEAD_DIM)
        attended = turned_ref[head] / summed[head]
        turned_ref[head] = attended
        out_ref[:, lanes] = jnp.transpose(attended).astype(LOW)
        total_ref[head] = peak[head] + jnp.log2(summed[head])
    for part in range(2):
        for relation in range(2):
            own_copy(relation, part).wait_send()
    key_pass.wait_send()
    value_pass.wait_send()


def attend(query_low, kv_low, length, true_rows, ident):
    rows, width = query_low.shape
    heads = width // HEAD_DIM
    key_rows = kv_low.shape[1]
    dma = pltpu.SemaphoreType.DMA
    vmem = pl.BlockSpec(memory_space=pltpu.VMEM)
    return pl.pallas_call(
        functools.partial(attend_kernel, true_rows),
        out_shape=(
            jax.ShapeDtypeStruct((rows, width), LOW),
            jax.ShapeDtypeStruct((heads, HEAD_DIM, rows), WIDE),
            jax.ShapeDtypeStruct((heads, 1, rows), WIDE),
            jax.ShapeDtypeStruct((3, 2, key_rows, width), LOW),
        ),
        in_specs=[pl.BlockSpec(memory_space=pltpu.SMEM), vmem, vmem],
        out_specs=(vmem,) * 4,
        scratch_shapes=[
            pltpu.VMEM((heads, 1, rows), WIDE),
            pltpu.VMEM((heads, 1, rows), WIDE),
            dma((6,)),
            dma((6,)),
        ],
        compiler_params=pltpu.CompilerParams(
            collective_id=ident, has_side_effects=True, vmem_limit_bytes=56 << 20
        ),
        cost_estimate=pl.CostEstimate(flops=10**9, bytes_accessed=150 * 10**6, transcendentals=0),
        name="attend",
    )(length, query_low, kv_low)


def attend_back_kernel(
    true_rows, length_ref, query_ref, kv_ref, got_ref, turned_ref, total_ref, grad_ref,
    query_grad_ref, kv_grad_ref, centre, query_turned, leaving, landing, send, recv,
):
    places = plane_places()
    plane_barrier(places)
    heads = query_ref.shape[1] // HEAD_DIM
    key_rows = kv_ref.shape[1]
    length = length_ref[0]
    scale = 1.0 / math.sqrt(HEAD_DIM)
    for head in range(heads):
        lanes = slice(head * HEAD_DIM, (head + 1) * HEAD_DIM)
        grads = jnp.transpose(grad_ref[:, lanes].astype(WIDE))
        centre[head] = jnp.sum(grads * turned_ref[head], axis=0, keepdims=True)
    query_turned[...] = jnp.zeros(query_turned.shape, WIDE)
    spare = query_ref.shape[0] - key_rows
    kv_grad_ref[:, pl.ds(key_rows, spare), :] = jnp.zeros((2, spare, query_ref.shape[1]), WIDE)

    def block(source, sink, owner):
        def step(head, carry):
            lanes = head_lanes(head)
            keys = source(0, lanes)
            query = query_ref[:, lanes]
            grads = grad_ref[:, lanes]
            probs = jnp.exp2(over_last(keys, query) * (scale * LOG2E) - total_ref[head])
            probs = jnp.where(block_valid(key_rows, owner, true_rows, length), probs, 0.0)
            grad_probs = over_last(source(1, lanes), grads)
            grad_scores = (probs * (grad_probs - centre[head])).astype(LOW)
            sink(0, lanes, jnp.dot(grad_scores, query, preferred_element_type=WIDE) * scale)
            sink(1, lanes, jnp.dot(probs.astype(LOW), grads, preferred_element_type=WIDE))
            query_turned[head] = query_turned[head] + lax.dot_general(
                keys, grad_scores, (((0,), (0,)), ((), ())), preferred_element_type=WIDE
            )

            return carry

        lax.fori_loop(0, heads, step, 0)

    def grad_copy(relation, part):
        return plane_copy(
            leaving.at[relation, part],
            landing.at[relation, part],
            send.at[relation, part],
            recv.at[relation, part],
            places[relation + 1],
        )

    for relation in (2, 1, 0):

        def sink(part, lanes, value, relation=relation):
            leaving[relation, part, :, lanes] = value.astype(LOW)

        block(
            lambda part, lanes, relation=relation: got_ref[relation, part, :, lanes],
            sink,
            places[relation + 1],
        )
        for part in range(2):
            grad_copy(relation, part).start()

    def own_sink(part, lanes, value):
        kv_grad_ref[part, pl.ds(0, key_rows), lanes] = value

    block(lambda part, lanes: kv_ref[part, :, lanes], own_sink, places[0])
    for head in range(heads):
        lanes = slice(head * HEAD_DIM, (head + 1) * HEAD_DIM)
        query_grad_ref[:, lanes] = jnp.transpose(query_turned[head]) * scale
    for relation in (2, 1, 0):
        for part in range(2):
            grad_copy(relation, part).wait_recv()

    def gather(tile, carry):
        rows = pl.ds(pl.multiple_of(tile * 16, 16), 16)
        for part in range(2):
            total = kv_grad_ref[part, rows]
            for relation in range(3):
                total = total + landing[relation, part, rows].astype(WIDE)
            kv_grad_ref[part, rows] = total
        return carry

    lax.fori_loop(0, key_rows // 16, gather, 0)
    for relation in range(3):
        for part in range(2):
            grad_copy(relation, part).wait_send()


def attend_back(query_low, kv_low, got, turned, total, grad_low, length, true_rows, ident):
    rows, width = query_low.shape
    heads = width // HEAD_DIM
    key_rows = kv_low.shape[1]
    dma = pltpu.SemaphoreType.DMA
    vmem = pl.BlockSpec(memory_space=pltpu.VMEM)
    return pl.pallas_call(
        functools.partial(attend_back_kernel, true_rows),
        out_shape=(
            jax.ShapeDtypeStruct((rows, width), WIDE),
            jax.ShapeDtypeStruct((2, rows, width), WIDE),
        ),
        in_specs=[pl.BlockSpec(memory_space=pltpu.SMEM)] + [vmem] * 6,
        out_specs=(vmem,) * 2,
        scratch_shapes=[
            pltpu.VMEM((heads, 1, rows), WIDE),
            pltpu.VMEM((heads, HEAD_DIM, rows), WIDE),
            pltpu.VMEM((3, 2, key_rows, width), LOW),
            pltpu.VMEM((3, 2, key_rows, width), LOW),
            dma((3, 2)),
            dma((3, 2)),
        ],
        compiler_params=pltpu.CompilerParams(
            collective_id=ident, has_side_effects=True, vmem_limit_bytes=56 << 20
        ),
        cost_estimate=pl.CostEstimate(flops=10**9, bytes_accessed=200 * 10**6, transcendentals=0),
        name="attend_back",
    )(length, query_low, kv_low, got, turned, total, grad_low)


def pair_swap(values):
    lane = lax.broadcasted_iota(jnp.int32, values.shape, 1)
    return jnp.where(
        lax.rem(lane, 2) == 0,
        pltpu.roll(values, HEAD_DIM - 1, axis=1),
        pltpu.roll(values, 1, axis=1),
    )


def rows_to_lanes(values):
    return jnp.sum(jnp.transpose(values), axis=0, keepdims=True)


def lanes_to_rows(row):
    return jnp.transpose(jnp.broadcast_to(row, (HEAD_DIM, row.shape[1])))


def tensor_barrier():
    count = lax.axis_size("tensor")
    me = lax.axis_index("tensor")
    barrier = pltpu.get_barrier_semaphore()
    for hop in range(1, count):
        pl.semaphore_signal(
            barrier, inc=1, device_id={"tensor": lax.rem(me + hop, count)},
            device_id_type=pl.DeviceIdType.MESH)
    pl.semaphore_wait(barrier, count - 1)


def tensor_copy(stage, slots, send, recv, slot, hop, place):
    return pltpu.make_async_remote_copy(
        src_ref=stage, dst_ref=slots.at[slot], send_sem=send.at[hop - 1],
        recv_sem=recv.at[hop - 1], device_id={"tensor": place},
        device_id_type=pl.DeviceIdType.MESH)


def tensor_send(stage, slots, send, recv):
    count = slots.shape[0]
    me = lax.axis_index("tensor")
    for hop in range(1, count):
        tensor_copy(stage, slots, send, recv, me, hop, lax.rem(me + hop, count)).start()
    slots[pl.ds(me, 1)] = stage[...][None]


def tensor_collect(stage, slots, send, recv):
    count = slots.shape[0]
    me = lax.axis_index("tensor")
    for hop in range(1, count):
        origin = lax.rem(me + count - hop, count)
        tensor_copy(stage, slots, send, recv, origin, hop, origin).wait_recv()
    for hop in range(1, count):
        tensor_copy(stage, slots, send, recv, me, hop, lax.rem(me + hop, count)).wait_send()
    total = slots[0]
    for slot in range(1, count):
        total = total + slots[slot]
    return total


def project_kernel(
    rows_ref, weight_ref, bias_ref, gain_ref, cosine_ref, sine_ref,
    pre_ref, query_ref, kv_ref, square_ref, stage, slots, send, recv,
):
    heads = query_ref.shape[1] // HEAD_DIM
    key_rows = kv_ref.shape[1]
    width = rows_ref.shape[1]
    tensor_barrier()
    stage[...] = jnp.zeros(stage.shape, WIDE)
    for part in range(2):
        pre_ref[part] = (
            jnp.dot(rows_ref[...], weight_ref[part], preferred_element_type=WIDE)
            + bias_ref[part : part + 1]
        )
        squares = None
        for head in range(heads):
            piece = pre_ref[part, :, head * HEAD_DIM : (head + 1) * HEAD_DIM]
            squares = piece * piece if squares is None else squares + piece * piece
        stage[part : part + 1] = rows_to_lanes(squares)
    tensor_send(stage, slots, send, recv)
    values = jnp.dot(rows_ref[...], weight_ref[2], preferred_element_type=WIDE) + bias_ref[2:3]
    kv_ref[1] = values[:key_rows].astype(LOW)
    total = tensor_collect(stage, slots, send, recv)
    square_ref[...] = total
    for part in range(2):
        rate = lanes_to_rows(lax.rsqrt(total[part : part + 1] / width + eps_norm))
        for head in range(heads):
            lanes = slice(head * HEAD_DIM, (head + 1) * HEAD_DIM)
            normed = pre_ref[part, :, lanes] * rate * gain_ref[part : part + 1, lanes]
            turned = normed * cosine_ref[...] + pair_swap(normed) * sine_ref[...]
            if part == 0:
                query_ref[:, lanes] = turned.astype(LOW)
            else:
                kv_ref[0, :, lanes] = turned[:key_rows].astype(LOW)


def project(rows_low, weights, bias, gains, cosine, sine, key_rows, ident):
    rows = rows_low.shape[0]
    width = weights.shape[2]
    count = lax.axis_size("tensor")
    vmem = pl.BlockSpec(memory_space=pltpu.VMEM)
    dma = pltpu.SemaphoreType.DMA
    return pl.pallas_call(
        project_kernel,
        out_shape=(
            jax.ShapeDtypeStruct((2, rows, width), WIDE),
            jax.ShapeDtypeStruct((rows, width), LOW),
            jax.ShapeDtypeStruct((2, key_rows, width), LOW),
            jax.ShapeDtypeStruct((8, rows), WIDE),
        ),
        in_specs=[vmem] * 6,
        out_specs=(vmem,) * 4,
        scratch_shapes=[
            pltpu.VMEM((8, rows), WIDE),
            pltpu.VMEM((count, 8, rows), WIDE),
            dma((count - 1,)),
            dma((count - 1,)),
        ],
        compiler_params=pltpu.CompilerParams(
            collective_id=ident, has_side_effects=True, vmem_limit_bytes=56 << 20
        ),
        name="project",
    )(rows_low, weights, bias, gains, cosine, sine)


def unproject_kernel(
    width, query_grad_ref, kv_grad_ref, pre_ref, square_ref, gain_ref, cosine_ref, sine_ref,
    query_low_ref, key_low_ref, value_low_ref, sums_ref, work, stage, slots, send, recv,
):
    heads = query_grad_ref.shape[1] // HEAD_DIM
    tensor_barrier()
    stage[...] = jnp.zeros(stage.shape, WIDE)
    sums_ref[...] = jnp.zeros(sums_ref.shape, WIDE)
    total = square_ref[...]
    for part in range(2):
        terms = None
        rate = lanes_to_rows(lax.rsqrt(total[part : part + 1] / width + eps_norm))
        for head in range(heads):
            lanes = slice(head * HEAD_DIM, (head + 1) * HEAD_DIM)
            grads = query_grad_ref[:, lanes] if part == 0 else kv_grad_ref[0, :, lanes]
            grads = grads * cosine_ref[...] - pair_swap(grads) * sine_ref[...]
            pre = pre_ref[part, :, lanes]
            sums_ref[3 + part : 4 + part, lanes] = jnp.sum(
                grads * pre * rate, axis=0, keepdims=True
            )
            grads = grads * gain_ref[part : part + 1, lanes]
            work[part, :, lanes] = grads
            terms = grads * pre if terms is None else terms + grads * pre
        stage[part : part + 1] = rows_to_lanes(terms)
    tensor_send(stage, slots, send, recv)
    values = kv_grad_ref[1]
    sums_ref[2:3] = jnp.sum(values, axis=0, keepdims=True)
    value_low_ref[...] = values.astype(LOW)
    back_total = tensor_collect(stage, slots, send, recv)
    for part in range(2):
        rate_row = lax.rsqrt(total[part : part + 1] / width + eps_norm)
        rate = lanes_to_rows(rate_row)
        back = lanes_to_rows(rate_row * rate_row * rate_row * back_total[part : part + 1] / width)
        for head in range(heads):
            lanes = slice(head * HEAD_DIM, (head + 1) * HEAD_DIM)
            grads = work[part, :, lanes] * rate - pre_ref[part, :, lanes] * back
            sums_ref[part : part + 1, lanes] = jnp.sum(grads, axis=0, keepdims=True)
            if part == 0:
                query_low_ref[:, lanes] = grads.astype(LOW)
            else:
                key_low_ref[:, lanes] = grads.astype(LOW)


def unproject(query_grads, kv_grads, pre, squares, gains, cosine, sine, model_width, ident):
    rows, width = query_grads.shape
    count = lax.axis_size("tensor")
    vmem = pl.BlockSpec(memory_space=pltpu.VMEM)
    dma = pltpu.SemaphoreType.DMA
    return pl.pallas_call(
        functools.partial(unproject_kernel, model_width),
        out_shape=(jax.ShapeDtypeStruct((rows, width), LOW),) * 3
        + (jax.ShapeDtypeStruct((8, width), WIDE),),
        in_specs=[vmem] * 7,
        out_specs=(vmem,) * 4,
        scratch_shapes=[
            pltpu.VMEM((2, rows, width), WIDE),
            pltpu.VMEM((8, rows), WIDE),
            pltpu.VMEM((count, 8, rows), WIDE),
            dma((count - 1,)),
            dma((count - 1,)),
        ],
        compiler_params=pltpu.CompilerParams(
            collective_id=ident, has_side_effects=True, vmem_limit_bytes=56 << 20
        ),
        name="unproject",
    )(query_grads, kv_grads, pre, squares, gains, cosine, sine)


def seq_scatter_kernel(blocks_ref, out_ref, slots, send_sem, recv_sem):
    count = slots.shape[0]
    me = lax.axis_index("seq")
    barrier = pltpu.get_barrier_semaphore()
    for hop in range(1, count):
        pl.semaphore_signal(
            barrier, inc=1, device_id={"seq": lax.rem(me + hop, count)},
            device_id_type=pl.DeviceIdType.MESH)
    pl.semaphore_wait(barrier, count - 1)

    def copy(block, slot, hop, place):
        return pltpu.make_async_remote_copy(
            src_ref=blocks_ref.at[block], dst_ref=slots.at[slot], send_sem=send_sem.at[hop - 1],
            recv_sem=recv_sem.at[hop - 1], device_id={"seq": place},
            device_id_type=pl.DeviceIdType.MESH)

    for hop in range(1, count):
        place = lax.rem(me + hop, count)
        copy(place, me, hop, place).start()
    slots[pl.ds(me, 1)] = blocks_ref[pl.ds(me, 1)]
    for hop in range(1, count):
        origin = lax.rem(me + count - hop, count)
        copy(me, origin, hop, origin).wait_recv()
    for hop in range(1, count):
        place = lax.rem(me + hop, count)
        copy(place, me, hop, place).wait_send()
    total = slots[0].astype(WIDE)
    for slot in range(1, count):
        total = total + slots[slot].astype(WIDE)
    out_ref[...] = total


def seq_scatter(blocks, ident):
    count, rows, width = blocks.shape
    vmem = pl.BlockSpec(memory_space=pltpu.VMEM)
    return pl.pallas_call(
        seq_scatter_kernel,
        out_shape=jax.ShapeDtypeStruct((rows, width), WIDE),
        in_specs=[vmem],
        out_specs=vmem,
        scratch_shapes=[
            pltpu.VMEM((count, rows, width), LOW),
            pltpu.SemaphoreType.DMA((count - 1,)),
            pltpu.SemaphoreType.DMA((count - 1,)),
        ],
        compiler_params=pltpu.CompilerParams(collective_id=ident, has_side_effects=True),
        name="seq_scatter",
    )(blocks)


def head_sum(term):
    def add(heads):
        total = None
        for head in range(heads):
            piece = term(head, slice(head * HEAD_DIM, (head + 1) * HEAD_DIM))
            total = piece if total is None else total + piece
        return total

    return add


def cross_attend_kernel(
    rows_ref, text_ref, query_weight_ref, text_weight_ref, bias_ref, gain_ref,
    query_pre_ref, key_pre_ref, query_ref, kv_ref, square_ref, out_ref, turned_ref, total_ref,
    stage, slots, send, recv,
):
    heads = query_ref.shape[1] // HEAD_DIM
    width = rows_ref.shape[1]
    factor = LOG2E / math.sqrt(HEAD_DIM)
    tensor_barrier()
    stage[...] = jnp.zeros(stage.shape, WIDE)
    query_pre_ref[...] = (
        jnp.dot(rows_ref[...], query_weight_ref[...], preferred_element_type=WIDE)
        + bias_ref[0:1]
    )
    key_pre_ref[...] = (
        jnp.dot(text_ref[...], text_weight_ref[0], preferred_element_type=WIDE) + bias_ref[1:2]
    )
    for part, pre_ref in enumerate((query_pre_ref, key_pre_ref)):
        squares = head_sum(lambda head, lanes: pre_ref[:, lanes] * pre_ref[:, lanes])(heads)
        stage[part : part + 1, : pre_ref.shape[0]] = rows_to_lanes(squares)
    tensor_send(stage, slots, send, recv)
    values = jnp.dot(text_ref[...], text_weight_ref[1], preferred_element_type=WIDE)
    kv_ref[1] = (values + bias_ref[2:3]).astype(LOW)
    total = tensor_collect(stage, slots, send, recv)
    square_ref[...] = total
    for part, pre_ref in enumerate((query_pre_ref, key_pre_ref)):
        square = total[part : part + 1, : pre_ref.shape[0]]
        rate = lanes_to_rows(lax.rsqrt(square / width + eps_norm))
        for head in range(heads):
            lanes = slice(head * HEAD_DIM, (head + 1) * HEAD_DIM)
            normed = (pre_ref[:, lanes] * rate * gain_ref[part : part + 1, lanes]).astype(LOW)
            if part == 0:
                query_ref[:, lanes] = normed
            else:
                kv_ref[0, :, lanes] = normed

    def step(head, carry):
        lanes = head_lanes(head)
        scores = over_last(kv_ref[0, :, lanes], query_ref[:, lanes]) * factor
        peak = jnp.max(scores, axis=0, keepdims=True)
        terms = jnp.exp2(scores - peak)
        summed = jnp.sum(terms, axis=0, keepdims=True)
        attended = (
            lax.dot_general(
                kv_ref[1, :, lanes],
                terms.astype(LOW),
                (((0,), (0,)), ((), ())),
                preferred_element_type=WIDE,
            )
            / summed
        )
        turned_ref[head] = attended
        out_ref[:, lanes] = jnp.transpose(attended).astype(LOW)
        total_ref[head] = peak + jnp.log2(summed)
        return carry

    lax.fori_loop(0, heads, step, 0)


def cross_attend(rows_low, text_all, query_weight, text_weights, bias, gains, ident):
    rows = rows_low.shape[0]
    tokens = text_all.shape[0]
    width = query_weight.shape[1]
    heads = width // HEAD_DIM
    count = lax.axis_size("tensor")
    vmem = pl.BlockSpec(memory_space=pltpu.VMEM)
    dma = pltpu.SemaphoreType.DMA
    return pl.pallas_call(
        cross_attend_kernel,
        out_shape=(
            jax.ShapeDtypeStruct((rows, width), WIDE),
            jax.ShapeDtypeStruct((tokens, width), WIDE),
            jax.ShapeDtypeStruct((rows, width), LOW),
            jax.ShapeDtypeStruct((2, tokens, width), LOW),
            jax.ShapeDtypeStruct((8, rows), WIDE),
            jax.ShapeDtypeStruct((rows, width), LOW),
            jax.ShapeDtypeStruct((heads, HEAD_DIM, rows), WIDE),
            jax.ShapeDtypeStruct((heads, 1, rows), WIDE),
        ),
        in_specs=[vmem] * 6,
        out_specs=(vmem,) * 8,
        scratch_shapes=[
            pltpu.VMEM((8, rows), WIDE),
            pltpu.VMEM((count, 8, rows), WIDE),
            dma((count - 1,)),
            dma((count - 1,)),
        ],
        compiler_params=pltpu.CompilerParams(
            collective_id=ident, has_side_effects=True, vmem_limit_bytes=56 << 20
        ),
        name="cross_attend",
    )(rows_low, text_all, query_weight, text_weights, bias, gains)


def cross_back_kernel(
    width, query_ref, kv_ref, turned_ref, total_ref, grad_ref, query_pre_ref, key_pre_ref,
    square_ref, text_square_ref, gain_ref, query_low_ref, text_low_ref, sums_ref,
    centre, query_turned, work, text_work, leaving, landing, stage, slots, text_send, text_recv,
    send, recv,
):
    heads = query_ref.shape[1] // HEAD_DIM
    tokens = key_pre_ref.shape[0]
    scale = 1.0 / math.sqrt(HEAD_DIM)
    places = plane_places()
    count = slots.shape[0]
    mine = lax.axis_index("tensor")
    barrier = pltpu.get_barrier_semaphore()
    for place in places[1:]:
        pl.semaphore_signal(
            barrier, inc=1, device_id={"seq": place}, device_id_type=pl.DeviceIdType.MESH
        )
    for hop in range(1, count):
        pl.semaphore_signal(
            barrier, inc=1, device_id={"tensor": lax.rem(mine + hop, count)},
            device_id_type=pl.DeviceIdType.MESH)
    pl.semaphore_wait(barrier, 3 + count - 1)

    for head in range(heads):
        lanes = slice(head * HEAD_DIM, (head + 1) * HEAD_DIM)
        grads = jnp.transpose(grad_ref[:, lanes].astype(WIDE))
        centre[head] = jnp.sum(grads * turned_ref[head], axis=0, keepdims=True)
    stage[...] = jnp.zeros(stage.shape, WIDE)
    sums_ref[...] = jnp.zeros(sums_ref.shape, WIDE)

    def step(head, carry):
        lanes = head_lanes(head)
        keys = kv_ref[0, :, lanes]
        query = query_ref[:, lanes]
        grads = grad_ref[:, lanes]
        probs = jnp.exp2(over_last(keys, query) * (scale * LOG2E) - total_ref[head])
        grad_probs = over_last(kv_ref[1, :, lanes], grads)
        grad_scores = (probs * (grad_probs - centre[head])).astype(LOW)
        key_grads = jnp.dot(grad_scores, query, preferred_element_type=WIDE) * scale
        leaving[0, :, lanes] = key_grads.astype(LOW)
        value_grads = jnp.dot(probs.astype(LOW), grads, preferred_element_type=WIDE)
        leaving[1, :, lanes] = value_grads.astype(LOW)
        query_turned[head] = lax.dot_general(
            keys, grad_scores, (((0,), (0,)), ((), ())), preferred_element_type=WIDE
        )
        return carry

    lax.fori_loop(0, heads, step, 0)

    def owned(place):
        return pl.ds(pl.multiple_of(place * tokens, 16), tokens)

    def text_copy(relation, part):
        place = places[relation + 1]
        return plane_copy(
            leaving.at[part, owned(place)],
            landing.at[relation, part],
            text_send.at[relation, part],
            text_recv.at[relation, part],
            place,
        )

    for relation in (2, 1, 0):
        for part in range(2):
            text_copy(relation, part).start()

    rate_row = lax.rsqrt(square_ref[0:1] / width + eps_norm)
    rate = lanes_to_rows(rate_row)
    terms = None
    for head in range(heads):
        lanes = slice(head * HEAD_DIM, (head + 1) * HEAD_DIM)
        grads = jnp.transpose(query_turned[head]) * scale
        pre = query_pre_ref[:, lanes]
        sums_ref[3:4, lanes] = jnp.sum(grads * pre * rate, axis=0, keepdims=True)
        grads = grads * gain_ref[0:1, lanes]
        work[:, lanes] = grads
        terms = grads * pre if terms is None else terms + grads * pre
    stage[0:1] = rows_to_lanes(terms)

    for relation in range(3):
        for part in range(2):
            text_copy(relation, part).wait_recv()
    for part in range(2):
        total = leaving[part, owned(places[0])].astype(WIDE)
        for relation in range(3):
            total = total + landing[relation, part].astype(WIDE)
        text_work[part] = total
    text_row = lax.rsqrt(text_square_ref[0:1] / width + eps_norm)
    text_rate = lanes_to_rows(text_row)
    terms = None
    for head in range(heads):
        lanes = slice(head * HEAD_DIM, (head + 1) * HEAD_DIM)
        grads = text_work[0, :, lanes]
        pre = key_pre_ref[:, lanes]
        sums_ref[4:5, lanes] = jnp.sum(grads * pre * text_rate, axis=0, keepdims=True)
        grads = grads * gain_ref[1:2, lanes]
        text_work[0, :, lanes] = grads
        terms = grads * pre if terms is None else terms + grads * pre
    stage[1:2, :tokens] = rows_to_lanes(terms)

    tensor_send(stage, slots, send, recv)
    sums_ref[2:3] = jnp.sum(text_work[1], axis=0, keepdims=True)
    text_low_ref[1] = text_work[1].astype(LOW)
    back_total = tensor_collect(stage, slots, send, recv)
    back = lanes_to_rows(rate_row * rate_row * rate_row * back_total[0:1] / width)
    text_back = lanes_to_rows(text_row * text_row * text_row * back_total[1:2, :tokens] / width)
    for head in range(heads):
        lanes = slice(head * HEAD_DIM, (head + 1) * HEAD_DIM)
        grads = work[:, lanes] * rate - query_pre_ref[:, lanes] * back
        sums_ref[0:1, lanes] = jnp.sum(grads, axis=0, keepdims=True)
        query_low_ref[:, lanes] = grads.astype(LOW)
        grads = text_work[0, :, lanes] * text_rate - key_pre_ref[:, lanes] * text_back
        sums_ref[1:2, lanes] = jnp.sum(grads, axis=0, keepdims=True)
        text_low_ref[0, :, lanes] = grads.astype(LOW)
    for relation in range(3):
        for part in range(2):
            text_copy(relation, part).wait_send()


def cross_back(saved, grad_low, key_pre_own, text_squares, gains, model_width, ident):
    query_pre, _, query_low, kv_low, squares, _, turned, total = saved
    rows, width = query_low.shape
    heads = width // HEAD_DIM
    tokens = key_pre_own.shape[0]
    count = lax.axis_size("tensor")
    vmem = pl.BlockSpec(memory_space=pltpu.VMEM)
    dma = pltpu.SemaphoreType.DMA
    return pl.pallas_call(
        functools.partial(cross_back_kernel, model_width),
        out_shape=(
            jax.ShapeDtypeStruct((rows, width), LOW),
            jax.ShapeDtypeStruct((2, tokens, width), LOW),
            jax.ShapeDtypeStruct((8, width), WIDE),
        ),
        in_specs=[vmem] * 10,
        out_specs=(vmem,) * 3,
        scratch_shapes=[
            pltpu.VMEM((heads, 1, rows), WIDE),
            pltpu.VMEM((heads, HEAD_DIM, rows), WIDE),
            pltpu.VMEM((rows, width), WIDE),
            pltpu.VMEM((2, tokens, width), WIDE),
            pltpu.VMEM(kv_low.shape, LOW),
            pltpu.VMEM((3, 2, tokens, width), LOW),
            pltpu.VMEM((8, rows), WIDE),
            pltpu.VMEM((count, 8, rows), WIDE),
            dma((3, 2)),
            dma((3, 2)),
            dma((count - 1,)),
            dma((count - 1,)),
        ],
        compiler_params=pltpu.CompilerParams(
            collective_id=ident, has_side_effects=True, vmem_limit_bytes=56 << 20
        ),
        name="cross_back",
    )(
        query_low, kv_low, turned, total, grad_low, query_pre, key_pre_own, squares, text_squares,
        gains,
    )


def head_forward(query, keys, values, key_ok, score_scale):
    scores = (
        jnp.einsum("csh,clh->csl", query, keys, preferred_element_type=jnp.float32) * score_scale
    )
    scores = jnp.where(key_ok[:, None, :], scores, -jnp.inf)
    row_peak = jnp.max(scores, axis=-1, keepdims=True)
    exp_terms = jnp.exp(scores - row_peak)
    summed = jnp.sum(exp_terms, axis=-1, keepdims=True)
    probs_low = (exp_terms / summed).astype(jnp.bfloat16)
    attended = jnp.einsum("csl,clh->csh", probs_low, values, preferred_element_type=jnp.float32)
    return (attended, row_peak[..., 0] + jnp.log(summed[..., 0]))


def head_backward(query, keys, values, key_ok, log_total, grad_att, score_scale):
    scores = (
        jnp.einsum("csh,clh->csl", query, keys, preferred_element_type=jnp.float32) * score_scale
    )
    probs = jnp.where(key_ok[:, None, :], jnp.exp(scores - log_total[..., None]), 0.0)
    grad_probs = jnp.einsum("csh,clh->csl", grad_att, values, preferred_element_type=jnp.float32)
    centre = jnp.sum(probs * grad_probs, axis=-1)
    grad_scores = (probs * (grad_probs - centre[..., None])).astype(jnp.bfloat16)
    grad_query = (
        jnp.einsum("csl,clh->csh", grad_scores, keys, preferred_element_type=jnp.float32)
        * score_scale
    )
    grad_keys = (
        jnp.einsum("csl,csh->clh", grad_scores, query, preferred_element_type=jnp.float32)
        * score_scale
    )
    grad_values = jnp.einsum(
        "csl,csh->clh", probs.astype(jnp.bfloat16), grad_att, preferred_element_type=jnp.float32
    )
    return (grad_query, centre, grad_keys, grad_values)


def shards(
    hidden,
    teacher,
    text,
    time_embed,
    lengths,
    positions,
    modulation,
    self_in,
    self_bias,
    self_out,
    norm_gains,
    cross_gain,
    cross_shift,
    cross_q,
    cross_kv,
    cross_bias,
    cross_out,
    ffn_in,
    ffn_in_bias,
    ffn_out,
    out_bias,
):
    low_type = jnp.bfloat16
    wide_type = jnp.float32
    clip_count, seq_rows, model_width = hidden.shape
    local_width = self_in.shape[2]
    local_heads = local_width // HEAD_DIM
    text_local = text.shape[1]
    seq_count = lax.axis_size("seq")
    slot_count = seq_rows * seq_count
    text_count = text_local * seq_count
    flat_rows = clip_count * seq_rows
    score_scale = 1.0 / math.sqrt(HEAD_DIM)
    seq_place = lax.axis_index("seq")
    clip_first = lax.axis_index("dp") * clip_count
    clip_lengths = lax.dynamic_slice_in_dim(lengths, clip_first, clip_count)
    key_valid = jnp.arange(slot_count, dtype=jnp.int32)[None, :] < clip_lengths[:, None]
    row_ids = seq_place * seq_rows + jnp.arange(seq_rows, dtype=jnp.int32)
    row_valid = row_ids[None, :] < clip_lengths[:, None]
    text_valid = jnp.ones((clip_count, text_count), dtype=jnp.bool_)
    valid_total = jnp.sum(lengths).astype(wide_type)
    modulated = modulation[None] + time_embed
    cosine_rep, sine_rep = rope_tables(positions, HEAD_DIM)
    rotate_now = functools.partial(
        rotate, cosine_rep=cosine_rep, sine_rep=sine_rep, swap_matrix=swap_table(HEAD_DIM)
    )
    head_shape = (clip_count, seq_rows, local_heads, HEAD_DIM)
    clip_ids = jnp.arange(flat_rows, dtype=jnp.int32) // seq_rows
    clip_table = (clip_ids[:, None] == jnp.arange(clip_count, dtype=jnp.int32)[None, :]).astype(
        wide_type
    )
    valid_rows = row_valid.reshape(flat_rows)
    hidden_rows = hidden.reshape(flat_rows, model_width)
    teacher_rows = teacher.reshape(flat_rows, model_width)

    def per_row(index_no):
        if clip_count == 1:
            return modulated[:, index_no]
        return jnp.dot(clip_table, modulated[:, index_no], precision=lax.Precision.HIGHEST)

    def per_clip(values):
        if clip_count == 1:
            return jnp.sum(values, axis=0, keepdims=True)
        return jnp.dot(clip_table.T, values, precision=lax.Precision.HIGHEST)

    scale_one = per_row(1)
    gate_one = per_row(2)
    scale_two = per_row(4)
    gate_two = per_row(5)
    normed_one = layer_norm(hidden_rows)
    query_pad = -flat_rows % 128
    key_pad = -flat_rows % 16

    def pad_queries(values):
        return jnp.pad(values, ((0, query_pad), (0, 0)))

    attn_in = pad_queries((normed_one * (1.0 + scale_one) + per_row(0)).astype(low_type))
    cosine_flat = pad_queries(cosine_rep.reshape(flat_rows, HEAD_DIM))
    sine_flat = pad_queries(sine_rep.reshape(flat_rows, HEAD_DIM)) * jnp.where(
        jnp.arange(HEAD_DIM) % 2 == 0, -1.0, 1.0
    )
    self_gains = norm_gains[:2]
    proj_pre, query_flat, own_kv, proj_squares = project(
        attn_in, self_in, self_bias, self_gains, cosine_flat, sine_flat, flat_rows + key_pad, 6
    )
    plane = seq_count == 4 and clip_count == 1
    if plane:
        attn_low, attn_turned, self_totals, got_kv = attend(
            query_flat, own_kv, clip_lengths, flat_rows, 10
        )
    else:
        query_low = query_flat[:flat_rows].reshape(head_shape)
        key_low = own_kv[0, :flat_rows]
        value_low = own_kv[1, :flat_rows]
        local_kv = jnp.stack(
            [
                key_low.reshape(clip_count, seq_rows, local_width),
                value_low.reshape(clip_count, seq_rows, local_width),
            ]
        )
        whole_kv = lax.all_gather(local_kv, "seq", axis=2, tiled=True)
        keys_all = whole_kv[0].reshape(clip_count, slot_count, local_heads, HEAD_DIM)
        values_all = whole_kv[1].reshape(clip_count, slot_count, local_heads, HEAD_DIM)
        att_heads = []
        total_heads = []
        for head_no in range(local_heads):
            attended, log_total = head_forward(
                query_low[:, :, head_no],
                keys_all[:, :, head_no],
                values_all[:, :, head_no],
                key_valid,
                score_scale,
            )
            att_heads.append(attended)
            total_heads.append(log_total)
        attn_low = jnp.stack(att_heads, axis=2).astype(low_type).reshape(flat_rows, local_width)
        attn_low = pad_queries(attn_low)
        self_totals = jnp.stack(total_heads)
    branch_one = (
        line_sum([attn_low], [self_out], False, 0, flat_rows) + out_bias[0]
    )
    after_one = hidden_rows + branch_one * gate_one
    normed_three = layer_norm(after_one)
    cross_in = (normed_three * cross_gain + cross_shift).astype(low_type)
    text_low = text.astype(low_type)
    text_start = seq_place * text_local
    text_all = lax.all_gather(text_low, "seq", axis=1, tiled=True)
    cross_plane = plane and text_local % 128 == 0 and text_count <= flat_rows
    if cross_plane:
        cross_in = pad_queries(cross_in)
        cross_saved = cross_attend(
            cross_in, text_all[0], cross_q, cross_kv, cross_bias, norm_gains[2:], 7
        )
        cross_att_low = cross_saved[5]
    else:
        cross_query_pre = jnp.dot(cross_in, cross_q, preferred_element_type=wide_type) + cross_bias[0]
        text_proj = (
            jnp.einsum("ctd,kde->kcte", text_all, cross_kv, preferred_element_type=wide_type)
            + cross_bias[1:, None, None, :]
        )
        cross_sq, text_sq = small_sum(
            [
                jnp.sum(cross_query_pre * cross_query_pre, axis=-1),
                jnp.sum(text_proj[0] * text_proj[0], axis=-1),
            ],
            7,
        )
        text_rate_all = lax.rsqrt(text_sq / model_width + eps_norm)[..., None]
        text_key_low = (text_proj[0] * text_rate_all * norm_gains[3]).astype(low_type)
        text_value_low = text_proj[1].astype(low_type)
        text_key_pre = lax.dynamic_slice_in_dim(text_proj[0], text_start, text_local, 1)
        text_key_rate = lax.dynamic_slice_in_dim(text_rate_all, text_start, text_local, 1)
        cross_rate = lax.rsqrt(cross_sq / model_width + eps_norm)[:, None]
        cross_query_low = (
            (cross_query_pre * cross_rate * norm_gains[2]).astype(low_type).reshape(head_shape)
        )
        text_key_heads = text_key_low.reshape(clip_count, text_count, local_heads, HEAD_DIM)
        text_value_heads = text_value_low.reshape(clip_count, text_count, local_heads, HEAD_DIM)
        cross_heads = []
        cross_total_heads = []
        for head_no in range(local_heads):
            attended, log_total = head_forward(
                cross_query_low[:, :, head_no],
                text_key_heads[:, :, head_no],
                text_value_heads[:, :, head_no],
                text_valid,
                score_scale,
            )
            cross_heads.append(attended)
            cross_total_heads.append(log_total)
        cross_att_low = jnp.stack(cross_heads, axis=2).astype(low_type).reshape(flat_rows, local_width)
        cross_totals = jnp.stack(cross_total_heads)
    branch_two = (
        line_sum([cross_att_low], [cross_out], False, 1, flat_rows)
        + out_bias[1]
    )
    after_two = after_one + branch_two
    normed_two = layer_norm(after_two)
    ffn_input = (normed_two * (1.0 + scale_two) + per_row(3)).astype(low_type)
    pre_act = jnp.dot(ffn_input, ffn_in, preferred_element_type=wide_type) + ffn_in_bias
    act_low = gelu_tanh(pre_act).astype(low_type)
    branch_three = (
        line_sum([act_low], [ffn_out], False, 2, flat_rows) + out_bias[2]
    )
    result = after_two + branch_three * gate_two
    residue = jnp.where(valid_rows[:, None], result - teacher_rows, 0.0)
    grad_three = residue * gate_two
    grad_three_low = grad_three.astype(low_type)
    ffn_out_mix = jnp.dot(grad_three_low.T, act_low, preferred_element_type=wide_type)
    grad_act = jnp.dot(grad_three_low, ffn_out.T, preferred_element_type=wide_type)
    grad_pre = jax.vjp(gelu_tanh, pre_act)[1](grad_act)[0]
    grad_pre_low = grad_pre.astype(low_type)
    grad_pre_low, ffn_out_mix = lax.optimization_barrier(
        (grad_pre_low, row_major(ffn_out_mix.astype(low_type)))
    )
    part_ffn_out = scatter_rows(ffn_out_mix, 0)
    ffn_in_mix = jnp.dot(ffn_input.T, grad_pre_low, preferred_element_type=wide_type)
    grad_ffn_bias = jnp.sum(grad_pre, axis=0)
    grad_ffn_input = line_sum([grad_pre_low], [ffn_in.T], False, 3, flat_rows)
    grad_after_two = (
        residue + jax.vjp(layer_norm, after_two)[1](grad_ffn_input * (1.0 + scale_two))[0]
    )
    grad_two_low = grad_after_two.astype(low_type)
    cross_out_mix = jnp.dot(grad_two_low.T, cross_att_low[:flat_rows], preferred_element_type=wide_type)
    grad_cross_att = (
        jnp.dot(grad_two_low, cross_out.T, preferred_element_type=wide_type).astype(low_type)
    )
    if cross_plane:
        grad_cross_query_low, text_grad_low, cross_sums = cross_back(
            cross_saved,
            pad_queries(grad_cross_att),
            lax.dynamic_slice_in_dim(cross_saved[1], text_start, text_local, 0),
            lax.dynamic_slice_in_dim(
                jnp.broadcast_to(cross_saved[4][1:2, :text_count], (8, text_count)),
                text_start,
                text_local,
                1,
            ),
            norm_gains[2:],
            model_width,
            8,
        )
        text_grad_low = text_grad_low[:, None]
        grad_cross_bias = cross_sums[:3]
        gain_cross_query = cross_sums[3]
        gain_text_key = cross_sums[4]
    else:
        grad_cross_att = grad_cross_att.reshape(head_shape)
        cross_query_grads = []
        text_key_grads = []
        text_value_grads = []
        for head_no in range(local_heads):
            head_grads = head_backward(
                cross_query_low[:, :, head_no],
                text_key_heads[:, :, head_no],
                text_value_heads[:, :, head_no],
                text_valid,
                cross_totals[head_no],
                grad_cross_att[:, :, head_no],
                score_scale,
            )
            cross_query_grads.append(head_grads[0])
            text_key_grads.append(head_grads[2])
            text_value_grads.append(head_grads[3])
        grad_cross_query = jnp.stack(cross_query_grads, axis=2).reshape(flat_rows, local_width)
        text_grads_all = jnp.stack(
            [
                jnp.stack(text_key_grads, axis=2).reshape(clip_count, text_count, local_width),
                jnp.stack(text_value_grads, axis=2).reshape(clip_count, text_count, local_width),
            ]
        )
        text_blocks = text_grads_all.astype(low_type).reshape(
            2, clip_count, seq_count, text_local, local_width
        )
        text_blocks = jnp.transpose(text_blocks, (2, 1, 3, 0, 4)).reshape(
            seq_count, clip_count * text_local, 2 * local_width
        )
        text_rows = seq_scatter(text_blocks, 14)
        text_grads = [
            text_rows[:, j * local_width : (j + 1) * local_width].reshape(
                clip_count, text_local, local_width
            )
            for j in range(2)
        ]
        query_term, key_term = small_sum(
            [
                jnp.sum(grad_cross_query * norm_gains[2] * cross_query_pre, axis=-1),
                jnp.sum(text_grads[0] * norm_gains[3] * text_key_pre, axis=-1),
            ],
            8,
        )
        grad_cross_query_pre = (
            grad_cross_query * norm_gains[2] * cross_rate
            - cross_query_pre * cross_rate**3 * query_term[:, None] / model_width
        )
        gain_cross_query = jnp.sum(grad_cross_query * cross_query_pre * cross_rate, axis=0)
        grad_cross_query_low = grad_cross_query_pre.astype(low_type)
        grad_text_key_pre = (
            text_grads[0] * norm_gains[3] * text_key_rate
            - text_key_pre * text_key_rate**3 * key_term[..., None] / model_width
        )
        gain_text_key = jnp.sum(text_grads[0] * text_key_pre * text_key_rate, axis=(0, 1))
        grad_cross_bias = jnp.stack(
            [
                jnp.sum(grad_cross_query_pre, axis=0),
                jnp.sum(grad_text_key_pre, axis=(0, 1)),
                jnp.sum(text_grads[1], axis=(0, 1)),
            ]
        )
        text_grad_low = jnp.stack([grad_text_key_pre, text_grads[1]]).astype(low_type)
    grad_cross_query_low, ffn_in_mix, part_ffn_out = lax.optimization_barrier(
        (grad_cross_query_low, row_major(ffn_in_mix.astype(low_type)), part_ffn_out)
    )
    part_ffn_in = scatter_rows(ffn_in_mix, 0)
    cross_q_mix = jnp.dot(cross_in.T, grad_cross_query_low, preferred_element_type=wide_type)
    grad_cross_in = line_sum([grad_cross_query_low], [cross_q], True, 4, flat_rows)
    cross_kv_mix = jnp.einsum(
        "ctd,kcte->kde", text_low, text_grad_low, preferred_element_type=wide_type
    )
    grad_text = lax.psum(
        jnp.einsum(
            "kcte,kde->ctd", text_grad_low, cross_kv, preferred_element_type=wide_type
        ).astype(jnp.bfloat16),
        "tensor",
    ).astype(jnp.float32)
    grad_cross_gain = jnp.sum(grad_cross_in * normed_three, axis=0)
    grad_cross_shift = jnp.sum(grad_cross_in, axis=0)
    grad_after_one = (
        grad_after_two + jax.vjp(layer_norm, after_one)[1](grad_cross_in * cross_gain)[0]
    )
    grad_one = grad_after_one * gate_one
    grad_one_low = grad_one.astype(low_type)
    self_out_mix = jnp.dot(grad_one_low.T, attn_low[:flat_rows], preferred_element_type=wide_type)
    grad_attn = (
        jnp.dot(grad_one_low, self_out.T, preferred_element_type=wide_type)
        .astype(low_type)
        .reshape(head_shape)
    )
    group_mix = jnp.concatenate(
        [cross_out_mix, cross_q_mix, self_out_mix, cross_kv_mix[0], cross_kv_mix[1]], axis=-1
    ).astype(low_type)
    grad_attn, group_mix = lax.optimization_barrier((grad_attn, row_major(group_mix)))
    part_group = scatter_rows(group_mix, 0)
    if plane:
        query_grads, kv_grads = attend_back(
            query_flat,
            own_kv,
            got_kv,
            attn_turned,
            self_totals,
            pad_queries(grad_attn.reshape(flat_rows, local_width)),
            clip_lengths,
            flat_rows,
            11,
        )
    else:
        query_grads = []
        key_grads = []
        value_grads = []
        for head_no in range(local_heads):
            head_grads = head_backward(
                query_low[:, :, head_no],
                keys_all[:, :, head_no],
                values_all[:, :, head_no],
                key_valid,
                self_totals[head_no],
                grad_attn[:, :, head_no],
                score_scale,
            )
            query_grads.append(head_grads[0])
            key_grads.append(head_grads[2])
            value_grads.append(head_grads[3])
        owner_grads = [
            jnp.stack(parts, axis=2)
            .astype(jnp.bfloat16)
            .reshape(clip_count, seq_count, seq_rows, local_width)
            for parts in (key_grads, value_grads)
        ]
        owner_grads = jnp.concatenate(
            [
                jnp.swapaxes(part, 0, 1).reshape(seq_count, flat_rows, local_width)
                for part in owner_grads
            ],
            axis=-1,
        )
        pad_rows = -flat_rows % 16
        owner_grads = jnp.pad(owner_grads, ((0, 0), (0, pad_rows), (0, 0)))
        kv_rows = lax.psum_scatter(
            owner_grads.reshape(seq_count * (flat_rows + pad_rows), 2 * local_width),
            "seq",
            scatter_dimension=0,
            tiled=True,
        )[:flat_rows].astype(jnp.float32)
        kv_grads = jnp.stack(
            [pad_queries(kv_rows[:, :local_width]), pad_queries(kv_rows[:, local_width:])]
        )
        query_grads = pad_queries(
            jnp.stack(query_grads, axis=2).reshape(flat_rows, local_width)
        )
    query_grads, part_ffn_in = lax.optimization_barrier((query_grads, part_ffn_in))
    *grad_proj_low, proj_sums = unproject(
        query_grads,
        kv_grads,
        proj_pre,
        proj_squares,
        self_gains,
        cosine_flat,
        sine_flat,
        model_width,
        9,
    )
    grad_self_bias = proj_sums[:3]
    self_in_mix = jnp.concatenate(
        [
            jnp.dot(attn_in.T, grad_proj_low[j], preferred_element_type=wide_type).astype(low_type)
            for j in range(3)
        ],
        axis=-1,
    )
    grad_proj_low, self_in_mix, part_group = lax.optimization_barrier(
        (grad_proj_low, row_major(self_in_mix), part_group)
    )
    part_self_in = scatter_rows(self_in_mix, 0)
    grad_attn_in = line_sum(grad_proj_low, [self_in], True, 5, flat_rows)
    grad_hidden = (
        grad_after_one + jax.vjp(layer_norm, hidden_rows)[1](grad_attn_in * (1.0 + scale_one))[0]
    )
    grad_time_local = jnp.stack(
        [
            per_clip(grad_attn_in),
            per_clip(grad_attn_in * normed_one),
            per_clip(grad_after_one * branch_one),
            per_clip(grad_ffn_input),
            per_clip(grad_ffn_input * normed_two),
            per_clip(residue * branch_three),
        ],
        axis=1,
    )
    grad_out_bias = jnp.stack(
        [jnp.sum(grad_one, axis=0), jnp.sum(grad_after_two, axis=0), jnp.sum(grad_three, axis=0)]
    )
    stream_values = (
        grad_time_local,
        grad_cross_gain,
        grad_cross_shift,
        grad_out_bias,
        jnp.sum(residue * residue),
    )
    grad_time_local, grad_cross_gain, grad_cross_shift, grad_out_bias, square_local = stream_values
    grad_norm_gains = jnp.concatenate(
        [proj_sums[3:5], gain_cross_query[None], gain_text_key[None]]
    )
    time_pair, sums = plane_sum(
        grad_time_local,
        [
            grad_self_bias,
            grad_norm_gains,
            grad_cross_gain,
            grad_cross_shift,
            grad_cross_bias,
            grad_ffn_bias,
            grad_out_bias,
            square_local,
        ],
        13,
    )
    grad_time, time_all = time_pair
    sum_modulation = jnp.sum(time_all, axis=0)
    (
        sum_self_bias,
        sum_gains,
        sum_cross_gain,
        sum_cross_shift,
        sum_cross_bias,
        sum_ffn_bias,
        sum_out_bias,
        square_sum,
    ) = sums
    loss = square_sum / (valid_total * model_width)
    part_ffn_in = part_ffn_in.astype(wide_type)
    part_ffn_out = part_ffn_out.T.astype(wide_type)
    pieces = [
        part_group[:, j * local_width : (j + 1) * local_width].astype(wide_type) for j in range(5)
    ]
    part_cross_out = pieces[0].T
    part_cross_q = pieces[1]
    part_self_out = pieces[2].T
    part_cross_kv = jnp.stack([pieces[3], pieces[4]])
    part_self_in = jnp.stack(
        [part_self_in[:, j * local_width : (j + 1) * local_width] for j in range(3)]
    ).astype(wide_type)
    result_out = result.reshape(clip_count, seq_rows, model_width)
    grad_hidden_out = grad_hidden.reshape(clip_count, seq_rows, model_width)
    return (
        result_out,
        loss,
        grad_hidden_out,
        grad_text,
        grad_time,
        sum_modulation,
        part_self_in,
        sum_self_bias,
        part_self_out,
        sum_gains,
        sum_cross_gain,
        sum_cross_shift,
        part_cross_q,
        part_cross_kv,
        sum_cross_bias,
        part_cross_out,
        part_ffn_in,
        sum_ffn_bias,
        part_ffn_out,
        sum_out_bias,
    )


def solution(mesh):
    placed = (
        P("dp", "seq", None),
        P("dp", "seq", None),
        P("dp", "seq", None),
        P("dp", None, None),
        P(),
        P(None, "dp", "seq"),
        P(),
        P(None, None, "tensor"),
        P(None, "tensor"),
        P("tensor", None),
        P(None, "tensor"),
        P(),
        P(),
        P(None, "tensor"),
        P(None, None, "tensor"),
        P(None, "tensor"),
        P("tensor", None),
        P(None, "tensor"),
        P("tensor"),
        P("tensor", None),
        P(),
    )
    return jax.shard_map(
        shards,
        mesh=mesh,
        in_specs=placed,
        out_specs=(
            P("dp", "seq", None),
            P(),
            P("dp", "seq", None),
            P("dp", "seq", None),
            P("dp", None, None),
            P(),
            P(None, ("dp", "seq"), "tensor"),
            P(None, "tensor"),
            P("tensor", ("dp", "seq")),
            P(None, "tensor"),
            P(),
            P(),
            P(("dp", "seq"), "tensor"),
            P(None, ("dp", "seq"), "tensor"),
            P(None, "tensor"),
            P("tensor", ("dp", "seq")),
            P(("dp", "seq"), "tensor"),
            P("tensor"),
            P("tensor", ("dp", "seq")),
            P(),
        ),
        check_vma=False,
    )
```

```python
import functools
import math

import jax
import jax.numpy as jnp
from jax import lax
from jax.experimental import pallas as pl
from jax.experimental.pallas import tpu as pltpu
from jax.experimental.layout import Layout, with_layout_constraint
from jax.sharding import PartitionSpec as P

HEAD_DIM = 128
LOW = jnp.bfloat16
WIDE = jnp.float32


eps_norm = 1e-06


def layer_norm(values):
    centred = values - jnp.mean(values, axis=-1, keepdims=True)
    return centred * lax.rsqrt(jnp.mean(centred * centred, axis=-1, keepdims=True) + eps_norm)


def gelu_tanh(values):
    return (
        0.5
        * values
        * (1.0 + jnp.tanh(0.7978845608028654 * (values + 0.044715 * values * values * values)))
    )


def rope_tables(positions, head_size):
    sixth_part = head_size // 6
    part_spans = (head_size - 4 * sixth_part, 2 * sixth_part, 2 * sixth_part)
    pieces = []
    for axis_no in range(3):
        span_now = part_spans[axis_no]
        inverse = 1.0 / 10000.0 ** (jnp.arange(0, span_now, 2).astype(jnp.float32) / span_now)
        pieces.append(positions[axis_no].astype(jnp.float32)[..., None] * inverse)
    angles = jnp.concatenate(pieces, axis=-1)
    cosine_rep = jnp.repeat(jnp.cos(angles), 2, axis=-1)[..., None, :]
    sine_rep = jnp.repeat(jnp.sin(angles), 2, axis=-1)[..., None, :]
    return (cosine_rep, sine_rep)


def swap_table(head_size):
    row_no = jnp.arange(head_size)[:, None]
    col_no = jnp.arange(head_size)[None, :]
    upward = jnp.where((row_no % 2 == 0) & (col_no == row_no + 1), 1.0, 0.0)
    downward = jnp.where((row_no % 2 == 1) & (col_no == row_no - 1), -1.0, 0.0)
    return (upward + downward).astype(jnp.float32)


def rotate(values, cosine_rep, sine_rep, swap_matrix):
    swapped = jnp.matmul(values, swap_matrix, precision=lax.Precision.HIGHEST)
    return values * cosine_rep + swapped * sine_rep


def line_kernel(count, block, group, lag, lag2, turned, *refs):
    lhs_refs = refs[:count]
    stacked = len(refs[count].shape) == 3
    rhs_count = 1 if stacked else count
    rhs_refs = [refs[count].at[j] for j in range(count)] if stacked else refs[count : 2 * count]
    out_ref, raw, part, stage, cross, raw_s, raw_r, mid_s, mid_r, far_s, far_r, near_s, near_r = refs[count + rhs_count :]
    steps = out_ref.shape[0] // block
    me = lax.axis_index("tensor")
    inner = (me == 1) | (me == 2)
    outer = jnp.logical_not(inner)
    leaf = jnp.where(me < 2, 0, 3)
    hub = jnp.where(me < 2, 1, 2)
    mate = 3 - me
    side = jnp.where(me < 2, 0, 1)

    def signal(where):
        pl.semaphore_signal(
            pltpu.get_barrier_semaphore(), inc=1, device_id={"tensor": where},
            device_id_type=pl.DeviceIdType.MESH)

    @pl.when(outer)
    def _():
        signal(hub)
        pl.semaphore_wait(pltpu.get_barrier_semaphore(), 1)

    @pl.when(inner)
    def _():
        signal(leaf)
        signal(mate)
        pl.semaphore_wait(pltpu.get_barrier_semaphore(), 2)

    def rows_of(step):
        return pl.ds(pl.multiple_of(step * block, 16), block)

    def remote(src, dst, send, recv, step, where):
        at = rows_of(step)
        return pltpu.make_async_remote_copy(
            src_ref=src.at[at], dst_ref=dst.at[at], send_sem=send.at[step], recv_sem=recv.at[step],
            device_id={"tensor": where}, device_id_type=pl.DeviceIdType.MESH)

    def raw_copy(step):
        return remote(raw, raw, raw_s, raw_r, step, hub)

    def mid_copy(step):
        return remote(stage, cross, mid_s, mid_r, step, mate)

    def far_copy(step):
        return remote(out_ref, out_ref, far_s, far_r, step, mate)

    def near_copy(step):
        return remote(out_ref, out_ref, near_s, near_r, step, leaf)

    def body(step, carry):
        @pl.when((step < steps) & (lax.rem(step, group) == 0))
        def _():
            at = pl.ds(pl.multiple_of(step * block, 16), block * group)
            total = None
            for lhs, rhs in zip(lhs_refs, rhs_refs):
                term = lax.dot_general(lhs[at], rhs[...], (((1,), (1 if turned else 0,)), ((), ())),
                    preferred_element_type=WIDE)
                total = term if total is None else total + term
            part[at] = total

        @pl.when(outer & (step < steps))
        def _():
            at = rows_of(step)
            raw[at] = part[at].astype(LOW)
            raw_copy(step).start()

        late = step - lag2
        @pl.when(inner & (late >= 0) & (late < steps) & (lax.rem(late + 2 * lag2, 2) != side))
        def _():
            far_copy(late).wait_recv()
            near_copy(late).start()

        near = step - lag
        @pl.when(inner & (near >= 0) & (near < steps) & (lax.rem(near + 2 * lag2, 2) == side))
        def _():
            at = rows_of(near)
            mid_copy(near).wait_recv()
            out_ref[at] = (part[at] + cross[at].astype(WIDE)).astype(LOW)
            far_copy(near).start()
            near_copy(near).start()

        @pl.when(inner & (step < steps))
        def _():
            at = rows_of(step)
            raw_copy(step).wait_recv()

            @pl.when(lax.rem(step, 2) == side)
            def _():
                part[at] = part[at] + raw[at].astype(WIDE)

            @pl.when(lax.rem(step, 2) != side)
            def _():
                stage[at] = (part[at] + raw[at].astype(WIDE)).astype(LOW)
                mid_copy(step).start()

        return carry

    lax.fori_loop(0, steps + lag2, body, 0)

    def drain(step, carry):
        @pl.when(outer)
        def _():
            near_copy(step).wait_recv()
            raw_copy(step).wait_send()

        @pl.when(inner)
        def _():
            near_copy(step).wait_send()

            @pl.when(lax.rem(step, 2) == side)
            def _():
                far_copy(step).wait_send()

            @pl.when(lax.rem(step, 2) != side)
            def _():
                mid_copy(step).wait_send()

        return carry

    lax.fori_loop(0, steps, drain, 0)

def line_sum(sources, weights, turned, ident, true_rows, block=16, group=7, lag=4, lag2=8):
    width = weights[0].shape[-2 if turned else -1]
    unit = block * group
    rows = -(-true_rows // unit) * unit
    sources = [jnp.pad(lhs, ((0, max(rows - lhs.shape[0], 0)), (0, 0))) for lhs in sources]
    steps = rows // block
    dma = pltpu.SemaphoreType.DMA
    depth = sum(lhs.shape[1] for lhs in sources)
    return pl.pallas_call(
        functools.partial(line_kernel, len(sources), block, group, lag, lag2, turned),
        out_shape=jax.ShapeDtypeStruct((rows, width), LOW),
        in_specs=[pl.BlockSpec(memory_space=pltpu.VMEM)] * (len(sources) + len(weights)),
        out_specs=pl.BlockSpec(memory_space=pltpu.VMEM),
        scratch_shapes=[
            pltpu.VMEM((rows, width), LOW),
            pltpu.VMEM((rows, width), WIDE),
            pltpu.VMEM((rows, width), LOW),
            pltpu.VMEM((rows, width), LOW),
        ] + [dma((steps,))] * 8,
        compiler_params=pltpu.CompilerParams(collective_id=ident, has_side_effects=True, vmem_limit_bytes=60 << 20),
        cost_estimate=pl.CostEstimate(flops=2 * rows * width * depth, bytes_accessed=230 * 10**6, transcendentals=0),
        name=f"line_sum_{ident}",
    )(*sources, *weights)[:true_rows].astype(WIDE)

def row_major(values):
    return with_layout_constraint(values, Layout((0, 1)))


def scatter_rows(mix, dimension):
    return lax.psum_scatter(mix, ("dp", "seq"), scatter_dimension=dimension, tiled=True)


def plane_sum_kernel(seq_count, value_ref, seq_ref, all_ref, slots, send_sem, recv_sem):
    count = slots.shape[0]
    dp = lax.axis_index("dp")
    me = dp * seq_count + lax.axis_index("seq")

    def device(place):
        return {"dp": place // seq_count, "seq": lax.rem(place, seq_count)}

    barrier = pltpu.get_barrier_semaphore()
    for hop in range(1, count):
        pl.semaphore_signal(
            barrier, inc=1, device_id=device(lax.rem(me + hop, count)),
            device_id_type=pl.DeviceIdType.MESH)
    pl.semaphore_wait(barrier, count - 1)

    def copy(slot, hop, place):
        return pltpu.make_async_remote_copy(
            src_ref=value_ref, dst_ref=slots.at[slot], send_sem=send_sem.at[hop - 1],
            recv_sem=recv_sem.at[hop - 1], device_id=device(place),
            device_id_type=pl.DeviceIdType.MESH)

    for hop in range(1, count):
        copy(me, hop, lax.rem(me + hop, count)).start()
    slots[pl.ds(me, 1)] = value_ref[...][None]
    for hop in range(1, count):
        origin = lax.rem(me + count - hop, count)
        copy(origin, hop, origin).wait_recv()
    for hop in range(1, count):
        copy(me, hop, lax.rem(me + hop, count)).wait_send()

    def span(start):
        total = slots[start].astype(WIDE)
        for slot in range(1, seq_count):
            total = total + slots[start + slot].astype(WIDE)
        return total

    seq_ref[...] = span(dp * seq_count)
    total = span(0)
    for part in range(1, count // seq_count):
        total = total + span(part * seq_count)
    all_ref[...] = total


def plane_sum(first, values, ident):
    seq_count = lax.axis_size("seq")
    count = lax.axis_size("dp") * seq_count
    flat = jnp.concatenate([value.reshape(-1).astype(LOW) for value in [first] + values])
    size = flat.shape[0]
    lines = -(-size // 2048) * 16
    packed = jnp.pad(flat, (0, lines * 128 - size)).reshape(lines, 128)
    vmem = pl.BlockSpec(memory_space=pltpu.VMEM)
    seq_total, all_total = pl.pallas_call(
        functools.partial(plane_sum_kernel, seq_count),
        out_shape=(jax.ShapeDtypeStruct((lines, 128), WIDE),) * 2,
        in_specs=[vmem],
        out_specs=(vmem, vmem),
        scratch_shapes=[
            pltpu.VMEM((count, lines, 128), LOW),
            pltpu.SemaphoreType.DMA((count - 1,)),
            pltpu.SemaphoreType.DMA((count - 1,)),
        ],
        compiler_params=pltpu.CompilerParams(collective_id=ident, has_side_effects=True),
        name="plane_sum",
    )(packed)
    all_total = all_total.reshape(-1)
    first_pair = (
        seq_total.reshape(-1)[: first.size].reshape(first.shape),
        all_total[: first.size].reshape(first.shape),
    )
    outs = []
    start = first.size
    for value in values:
        outs.append(all_total[start : start + value.size].reshape(value.shape))
        start += value.size
    return first_pair, outs


def small_kernel(value_ref, out_ref, slots, send_sem, recv_sem):
    count = slots.shape[0]
    me = lax.axis_index("tensor")
    barrier = pltpu.get_barrier_semaphore()
    for hop in range(1, count):
        pl.semaphore_signal(
            barrier, inc=1, device_id={"tensor": lax.rem(me + hop, count)},
            device_id_type=pl.DeviceIdType.MESH)
    pl.semaphore_wait(barrier, count - 1)
    copies = []
    for hop in range(1, count):
        copy = pltpu.make_async_remote_copy(
            src_ref=value_ref, dst_ref=slots.at[me], send_sem=send_sem.at[hop - 1],
            recv_sem=recv_sem.at[hop - 1], device_id={"tensor": lax.rem(me + hop, count)},
            device_id_type=pl.DeviceIdType.MESH)
        copy.start()
        copies.append(copy)
    slots[pl.ds(me, 1)] = value_ref[...][None]
    for hop in range(1, count):
        origin = lax.rem(me + count - hop, count)
        pltpu.make_async_remote_copy(
            src_ref=value_ref, dst_ref=slots.at[origin], send_sem=send_sem.at[hop - 1],
            recv_sem=recv_sem.at[hop - 1], device_id={"tensor": origin},
            device_id_type=pl.DeviceIdType.MESH).wait_recv()
    for copy in copies:
        copy.wait_send()
    total = slots[0]
    for slot in range(1, count):
        total = total + slots[slot]
    out_ref[...] = total


def small_sum(values, ident):
    count = lax.axis_size("tensor")
    flat = jnp.concatenate([value.reshape(-1) for value in values])
    size = flat.shape[0]
    lines = -(-size // 1024) * 8
    packed = jnp.pad(flat, (0, lines * 128 - size)).reshape(lines, 128)
    summed = pl.pallas_call(
        small_kernel,
        out_shape=jax.ShapeDtypeStruct((lines, 128), WIDE),
        in_specs=[pl.BlockSpec(memory_space=pltpu.VMEM)],
        out_specs=pl.BlockSpec(memory_space=pltpu.VMEM),
        scratch_shapes=[
            pltpu.VMEM((count, lines, 128), WIDE),
            pltpu.SemaphoreType.DMA((count - 1,)),
            pltpu.SemaphoreType.DMA((count - 1,)),
        ],
        compiler_params=pltpu.CompilerParams(collective_id=ident, has_side_effects=True),
        name=f"small_sum_{ident}",
    )(packed).reshape(-1)
    outs = []
    start = 0
    for value in values:
        outs.append(summed[start : start + value.size].reshape(value.shape))
        start += value.size
    return outs


LOG2E = 1.4426950408889634
HIDDEN_SCORE = -1e30


def plane_places():
    me = lax.axis_index("seq")
    column = lax.rem(me, 2)
    line = me // 2
    return (me, me + 1 - 2 * column, me + 2 - 4 * line, 3 - me)


def plane_barrier(places):
    barrier = pltpu.get_barrier_semaphore()
    for place in places[1:]:
        pl.semaphore_signal(
            barrier, inc=1, device_id={"seq": place}, device_id_type=pl.DeviceIdType.MESH
        )
    pl.semaphore_wait(barrier, 3)


def plane_copy(src, dst, send, recv, place):
    return pltpu.make_async_remote_copy(
        src_ref=src,
        dst_ref=dst,
        send_sem=send,
        recv_sem=recv,
        device_id={"seq": place},
        device_id_type=pl.DeviceIdType.MESH,
    )


def head_lanes(head):
    return pl.ds(pl.multiple_of(head * HEAD_DIM, 128), HEAD_DIM)


def block_valid(key_rows, owner, true_rows, length):
    row = lax.broadcasted_iota(jnp.int32, (key_rows, 1), 0)
    return (row < true_rows) & (owner * true_rows + row < length)


def over_last(lhs, rhs):
    return lax.dot_general(lhs, rhs, (((1,), (1,)), ((), ())), preferred_element_type=WIDE)


def attend_kernel(
    true_rows, length_ref, query_ref, kv_ref, out_ref, turned_ref, total_ref, got_ref, peak, summed, send, recv
):
    places = plane_places()
    plane_barrier(places)
    heads = query_ref.shape[1] // HEAD_DIM
    key_rows = kv_ref.shape[1]
    length = length_ref[0]
    factor = LOG2E / math.sqrt(HEAD_DIM)

    def own_copy(relation, part):
        index = 2 * relation + part
        return plane_copy(
            kv_ref.at[part], got_ref.at[relation, part], send.at[index], recv.at[index], places[relation + 1]
        )

    key_pass = plane_copy(got_ref.at[0, 0], got_ref.at[2, 0], send.at[4], recv.at[4], places[2])
    value_pass = plane_copy(got_ref.at[1, 1], got_ref.at[2, 1], send.at[5], recv.at[5], places[1])
    for part in range(2):
        for relation in range(2):
            own_copy(relation, part).start()

    peak[...] = jnp.full(peak.shape, HIDDEN_SCORE, WIDE)
    summed[...] = jnp.zeros(summed.shape, WIDE)
    turned_ref[...] = jnp.zeros(turned_ref.shape, WIDE)

    def block(source, owner):
        def step(head, carry):
            lanes = head_lanes(head)
            scores = over_last(source(0, lanes), query_ref[:, lanes]) * factor
            scores = jnp.where(block_valid(key_rows, owner, true_rows, length), scores, HIDDEN_SCORE)
            before = peak[head]
            after = jnp.maximum(before, jnp.max(scores, axis=0, keepdims=True))
            shrink = jnp.exp2(before - after)
            terms = jnp.exp2(scores - after)
            peak[head] = after
            summed[head] = summed[head] * shrink + jnp.sum(terms, axis=0, keepdims=True)
            turned_ref[head] = turned_ref[head] * shrink + lax.dot_general(
                source(1, lanes),
                terms.astype(LOW),
                (((0,), (0,)), ((), ())),
                preferred_element_type=WIDE,
            )

            return carry

        lax.fori_loop(0, heads, step, 0)

    block(lambda part, lanes: kv_ref[part, :, lanes], places[0])
    own_copy(0, 0).wait_recv()
    key_pass.start()
    own_copy(0, 1).wait_recv()
    own_copy(1, 1).wait_recv()
    value_pass.start()
    own_copy(1, 0).wait_recv()
    for relation in range(3):
        if relation == 2:
            key_pass.wait_recv()
            value_pass.wait_recv()
        block(
            lambda part, lanes, relation=relation: got_ref[relation, part, :, lanes],
            places[relation + 1],
        )

    for head in range(heads):
        lanes = slice(head * HEAD_DIM, (head + 1) * HEAD_DIM)
        attended = turned_ref[head] / summed[head]
        turned_ref[head] = attended
        out_ref[:, lanes] = jnp.transpose(attended).astype(LOW)
        total_ref[head] = peak[head] + jnp.log2(summed[head])
    for part in range(2):
        for relation in range(2):
            own_copy(relation, part).wait_send()
    key_pass.wait_send()
    value_pass.wait_send()


def attend(query_low, kv_low, length, true_rows, ident):
    rows, width = query_low.shape
    heads = width // HEAD_DIM
    key_rows = kv_low.shape[1]
    dma = pltpu.SemaphoreType.DMA
    vmem = pl.BlockSpec(memory_space=pltpu.VMEM)
    return pl.pallas_call(
        functools.partial(attend_kernel, true_rows),
        out_shape=(
            jax.ShapeDtypeStruct((rows, width), LOW),
            jax.ShapeDtypeStruct((heads, HEAD_DIM, rows), WIDE),
            jax.ShapeDtypeStruct((heads, 1, rows), WIDE),
            jax.ShapeDtypeStruct((3, 2, key_rows, width), LOW),
        ),
        in_specs=[pl.BlockSpec(memory_space=pltpu.SMEM), vmem, vmem],
        out_specs=(vmem,) * 4,
        scratch_shapes=[
            pltpu.VMEM((heads, 1, rows), WIDE),
            pltpu.VMEM((heads, 1, rows), WIDE),
            dma((6,)),
            dma((6,)),
        ],
        compiler_params=pltpu.CompilerParams(
            collective_id=ident, has_side_effects=True, vmem_limit_bytes=56 << 20
        ),
        cost_estimate=pl.CostEstimate(flops=10**9, bytes_accessed=150 * 10**6, transcendentals=0),
        name="attend",
    )(length, query_low, kv_low)


def attend_back_kernel(
    true_rows, length_ref, query_ref, kv_ref, got_ref, turned_ref, total_ref, grad_ref,
    query_grad_ref, kv_grad_ref, centre, query_turned, leaving, landing, send, recv,
):
    places = plane_places()
    plane_barrier(places)
    heads = query_ref.shape[1] // HEAD_DIM
    key_rows = kv_ref.shape[1]
    length = length_ref[0]
    scale = 1.0 / math.sqrt(HEAD_DIM)
    for head in range(heads):
        lanes = slice(head * HEAD_DIM, (head + 1) * HEAD_DIM)
        grads = jnp.transpose(grad_ref[:, lanes].astype(WIDE))
        centre[head] = jnp.sum(grads * turned_ref[head], axis=0, keepdims=True)
    query_turned[...] = jnp.zeros(query_turned.shape, WIDE)
    spare = query_ref.shape[0] - key_rows
    kv_grad_ref[:, pl.ds(key_rows, spare), :] = jnp.zeros((2, spare, query_ref.shape[1]), WIDE)

    def block(source, sink, owner):
        def step(head, carry):
            lanes = head_lanes(head)
            keys = source(0, lanes)
            query = query_ref[:, lanes]
            grads = grad_ref[:, lanes]
            probs = jnp.exp2(over_last(keys, query) * (scale * LOG2E) - total_ref[head])
            probs = jnp.where(block_valid(key_rows, owner, true_rows, length), probs, 0.0)
            grad_probs = over_last(source(1, lanes), grads)
            grad_scores = (probs * (grad_probs - centre[head])).astype(LOW)
            sink(0, lanes, jnp.dot(grad_scores, query, preferred_element_type=WIDE) * scale)
            sink(1, lanes, jnp.dot(probs.astype(LOW), grads, preferred_element_type=WIDE))
            query_turned[head] = query_turned[head] + lax.dot_general(
                keys, grad_scores, (((0,), (0,)), ((), ())), preferred_element_type=WIDE
            )

            return carry

        lax.fori_loop(0, heads, step, 0)

    def grad_copy(relation, part):
        return plane_copy(
            leaving.at[relation, part],
            landing.at[relation, part],
            send.at[relation, part],
            recv.at[relation, part],
            places[relation + 1],
        )

    for relation in (2, 1, 0):

        def sink(part, lanes, value, relation=relation):
            leaving[relation, part, :, lanes] = value.astype(LOW)

        block(
            lambda part, lanes, relation=relation: got_ref[relation, part, :, lanes],
            sink,
            places[relation + 1],
        )
        for part in range(2):
            grad_copy(relation, part).start()

    def own_sink(part, lanes, value):
        kv_grad_ref[part, pl.ds(0, key_rows), lanes] = value

    block(lambda part, lanes: kv_ref[part, :, lanes], own_sink, places[0])
    for head in range(heads):
        lanes = slice(head * HEAD_DIM, (head + 1) * HEAD_DIM)
        query_grad_ref[:, lanes] = jnp.transpose(query_turned[head]) * scale
    for relation in (2, 1, 0):
        for part in range(2):
            grad_copy(relation, part).wait_recv()

    def gather(tile, carry):
        rows = pl.ds(pl.multiple_of(tile * 16, 16), 16)
        for part in range(2):
            total = kv_grad_ref[part, rows]
            for relation in range(3):
                total = total + landing[relation, part, rows].astype(WIDE)
            kv_grad_ref[part, rows] = total
        return carry

    lax.fori_loop(0, key_rows // 16, gather, 0)
    for relation in range(3):
        for part in range(2):
            grad_copy(relation, part).wait_send()


def attend_back(query_low, kv_low, got, turned, total, grad_low, length, true_rows, ident):
    rows, width = query_low.shape
    heads = width // HEAD_DIM
    key_rows = kv_low.shape[1]
    dma = pltpu.SemaphoreType.DMA
    vmem = pl.BlockSpec(memory_space=pltpu.VMEM)
    return pl.pallas_call(
        functools.partial(attend_back_kernel, true_rows),
        out_shape=(
            jax.ShapeDtypeStruct((rows, width), WIDE),
            jax.ShapeDtypeStruct((2, rows, width), WIDE),
        ),
        in_specs=[pl.BlockSpec(memory_space=pltpu.SMEM)] + [vmem] * 6,
        out_specs=(vmem,) * 2,
        scratch_shapes=[
            pltpu.VMEM((heads, 1, rows), WIDE),
            pltpu.VMEM((heads, HEAD_DIM, rows), WIDE),
            pltpu.VMEM((3, 2, key_rows, width), LOW),
            pltpu.VMEM((3, 2, key_rows, width), LOW),
            dma((3, 2)),
            dma((3, 2)),
        ],
        compiler_params=pltpu.CompilerParams(
            collective_id=ident, has_side_effects=True, vmem_limit_bytes=56 << 20
        ),
        cost_estimate=pl.CostEstimate(flops=10**9, bytes_accessed=200 * 10**6, transcendentals=0),
        name="attend_back",
    )(length, query_low, kv_low, got, turned, total, grad_low)


def pair_swap(values):
    lane = lax.broadcasted_iota(jnp.int32, values.shape, 1)
    return jnp.where(
        lax.rem(lane, 2) == 0,
        pltpu.roll(values, HEAD_DIM - 1, axis=1),
        pltpu.roll(values, 1, axis=1),
    )


def rows_to_lanes(values):
    return jnp.sum(jnp.transpose(values), axis=0, keepdims=True)


def lanes_to_rows(row):
    return jnp.transpose(jnp.broadcast_to(row, (HEAD_DIM, row.shape[1])))


def tensor_barrier():
    count = lax.axis_size("tensor")
    me = lax.axis_index("tensor")
    barrier = pltpu.get_barrier_semaphore()
    for hop in range(1, count):
        pl.semaphore_signal(
            barrier, inc=1, device_id={"tensor": lax.rem(me + hop, count)},
            device_id_type=pl.DeviceIdType.MESH)
    pl.semaphore_wait(barrier, count - 1)


def tensor_copy(stage, slots, send, recv, slot, hop, place):
    return pltpu.make_async_remote_copy(
        src_ref=stage, dst_ref=slots.at[slot], send_sem=send.at[hop - 1],
        recv_sem=recv.at[hop - 1], device_id={"tensor": place},
        device_id_type=pl.DeviceIdType.MESH)


def tensor_send(stage, slots, send, recv):
    count = slots.shape[0]
    me = lax.axis_index("tensor")
    for hop in range(1, count):
        tensor_copy(stage, slots, send, recv, me, hop, lax.rem(me + hop, count)).start()
    slots[pl.ds(me, 1)] = stage[...][None]


def tensor_collect(stage, slots, send, recv):
    count = slots.shape[0]
    me = lax.axis_index("tensor")
    for hop in range(1, count):
        origin = lax.rem(me + count - hop, count)
        tensor_copy(stage, slots, send, recv, origin, hop, origin).wait_recv()
    for hop in range(1, count):
        tensor_copy(stage, slots, send, recv, me, hop, lax.rem(me + hop, count)).wait_send()
    total = slots[0]
    for slot in range(1, count):
        total = total + slots[slot]
    return total


def project_kernel(
    rows_ref, weight_ref, bias_ref, gain_ref, cosine_ref, sine_ref,
    pre_ref, query_ref, kv_ref, square_ref, stage, slots, send, recv,
):
    heads = query_ref.shape[1] // HEAD_DIM
    key_rows = kv_ref.shape[1]
    width = rows_ref.shape[1]
    tensor_barrier()
    stage[...] = jnp.zeros(stage.shape, WIDE)
    for part in range(2):
        pre_ref[part] = (
            jnp.dot(rows_ref[...], weight_ref[part], preferred_element_type=WIDE)
            + bias_ref[part : part + 1]
        )
        squares = None
        for head in range(heads):
            piece = pre_ref[part, :, head * HEAD_DIM : (head + 1) * HEAD_DIM]
            squares = piece * piece if squares is None else squares + piece * piece
        stage[part : part + 1] = rows_to_lanes(squares)
    tensor_send(stage, slots, send, recv)
    values = jnp.dot(rows_ref[...], weight_ref[2], preferred_element_type=WIDE) + bias_ref[2:3]
    kv_ref[1] = values[:key_rows].astype(LOW)
    total = tensor_collect(stage, slots, send, recv)
    square_ref[...] = total
    for part in range(2):
        rate = lanes_to_rows(lax.rsqrt(total[part : part + 1] / width + eps_norm))
        for head in range(heads):
            lanes = slice(head * HEAD_DIM, (head + 1) * HEAD_DIM)
            normed = pre_ref[part, :, lanes] * rate * gain_ref[part : part + 1, lanes]
            turned = normed * cosine_ref[...] + pair_swap(normed) * sine_ref[...]
            if part == 0:
                query_ref[:, lanes] = turned.astype(LOW)
            else:
                kv_ref[0, :, lanes] = turned[:key_rows].astype(LOW)


def project(rows_low, weights, bias, gains, cosine, sine, key_rows, ident):
    rows = rows_low.shape[0]
    width = weights.shape[2]
    count = lax.axis_size("tensor")
    vmem = pl.BlockSpec(memory_space=pltpu.VMEM)
    dma = pltpu.SemaphoreType.DMA
    return pl.pallas_call(
        project_kernel,
        out_shape=(
            jax.ShapeDtypeStruct((2, rows, width), WIDE),
            jax.ShapeDtypeStruct((rows, width), LOW),
            jax.ShapeDtypeStruct((2, key_rows, width), LOW),
            jax.ShapeDtypeStruct((8, rows), WIDE),
        ),
        in_specs=[vmem] * 6,
        out_specs=(vmem,) * 4,
        scratch_shapes=[
            pltpu.VMEM((8, rows), WIDE),
            pltpu.VMEM((count, 8, rows), WIDE),
            dma((count - 1,)),
            dma((count - 1,)),
        ],
        compiler_params=pltpu.CompilerParams(
            collective_id=ident, has_side_effects=True, vmem_limit_bytes=56 << 20
        ),
        name="project",
    )(rows_low, weights, bias, gains, cosine, sine)


def unproject_kernel(
    width, query_grad_ref, kv_grad_ref, pre_ref, square_ref, gain_ref, cosine_ref, sine_ref,
    query_low_ref, key_low_ref, value_low_ref, sums_ref, work, stage, slots, send, recv,
):
    heads = query_grad_ref.shape[1] // HEAD_DIM
    tensor_barrier()
    stage[...] = jnp.zeros(stage.shape, WIDE)
    sums_ref[...] = jnp.zeros(sums_ref.shape, WIDE)
    total = square_ref[...]
    for part in range(2):
        terms = None
        rate = lanes_to_rows(lax.rsqrt(total[part : part + 1] / width + eps_norm))
        for head in range(heads):
            lanes = slice(head * HEAD_DIM, (head + 1) * HEAD_DIM)
            grads = query_grad_ref[:, lanes] if part == 0 else kv_grad_ref[0, :, lanes]
            grads = grads * cosine_ref[...] - pair_swap(grads) * sine_ref[...]
            pre = pre_ref[part, :, lanes]
            sums_ref[3 + part : 4 + part, lanes] = jnp.sum(
                grads * pre * rate, axis=0, keepdims=True
            )
            grads = grads * gain_ref[part : part + 1, lanes]
            work[part, :, lanes] = grads
            terms = grads * pre if terms is None else terms + grads * pre
        stage[part : part + 1] = rows_to_lanes(terms)
    tensor_send(stage, slots, send, recv)
    values = kv_grad_ref[1]
    sums_ref[2:3] = jnp.sum(values, axis=0, keepdims=True)
    value_low_ref[...] = values.astype(LOW)
    back_total = tensor_collect(stage, slots, send, recv)
    for part in range(2):
        rate_row = lax.rsqrt(total[part : part + 1] / width + eps_norm)
        rate = lanes_to_rows(rate_row)
        back = lanes_to_rows(rate_row * rate_row * rate_row * back_total[part : part + 1] / width)
        for head in range(heads):
            lanes = slice(head * HEAD_DIM, (head + 1) * HEAD_DIM)
            grads = work[part, :, lanes] * rate - pre_ref[part, :, lanes] * back
            sums_ref[part : part + 1, lanes] = jnp.sum(grads, axis=0, keepdims=True)
            if part == 0:
                query_low_ref[:, lanes] = grads.astype(LOW)
            else:
                key_low_ref[:, lanes] = grads.astype(LOW)


def unproject(query_grads, kv_grads, pre, squares, gains, cosine, sine, model_width, ident):
    rows, width = query_grads.shape
    count = lax.axis_size("tensor")
    vmem = pl.BlockSpec(memory_space=pltpu.VMEM)
    dma = pltpu.SemaphoreType.DMA
    return pl.pallas_call(
        functools.partial(unproject_kernel, model_width),
        out_shape=(jax.ShapeDtypeStruct((rows, width), LOW),) * 3
        + (jax.ShapeDtypeStruct((8, width), WIDE),),
        in_specs=[vmem] * 7,
        out_specs=(vmem,) * 4,
        scratch_shapes=[
            pltpu.VMEM((2, rows, width), WIDE),
            pltpu.VMEM((8, rows), WIDE),
            pltpu.VMEM((count, 8, rows), WIDE),
            dma((count - 1,)),
            dma((count - 1,)),
        ],
        compiler_params=pltpu.CompilerParams(
            collective_id=ident, has_side_effects=True, vmem_limit_bytes=56 << 20
        ),
        name="unproject",
    )(query_grads, kv_grads, pre, squares, gains, cosine, sine)


def seq_scatter_kernel(blocks_ref, out_ref, slots, send_sem, recv_sem):
    count = slots.shape[0]
    me = lax.axis_index("seq")
    barrier = pltpu.get_barrier_semaphore()
    for hop in range(1, count):
        pl.semaphore_signal(
            barrier, inc=1, device_id={"seq": lax.rem(me + hop, count)},
            device_id_type=pl.DeviceIdType.MESH)
    pl.semaphore_wait(barrier, count - 1)

    def copy(block, slot, hop, place):
        return pltpu.make_async_remote_copy(
            src_ref=blocks_ref.at[block], dst_ref=slots.at[slot], send_sem=send_sem.at[hop - 1],
            recv_sem=recv_sem.at[hop - 1], device_id={"seq": place},
            device_id_type=pl.DeviceIdType.MESH)

    for hop in range(1, count):
        place = lax.rem(me + hop, count)
        copy(place, me, hop, place).start()
    slots[pl.ds(me, 1)] = blocks_ref[pl.ds(me, 1)]
    for hop in range(1, count):
        origin = lax.rem(me + count - hop, count)
        copy(me, origin, hop, origin).wait_recv()
    for hop in range(1, count):
        place = lax.rem(me + hop, count)
        copy(place, me, hop, place).wait_send()
    total = slots[0].astype(WIDE)
    for slot in range(1, count):
        total = total + slots[slot].astype(WIDE)
    out_ref[...] = total


def seq_scatter(blocks, ident):
    count, rows, width = blocks.shape
    vmem = pl.BlockSpec(memory_space=pltpu.VMEM)
    return pl.pallas_call(
        seq_scatter_kernel,
        out_shape=jax.ShapeDtypeStruct((rows, width), WIDE),
        in_specs=[vmem],
        out_specs=vmem,
        scratch_shapes=[
            pltpu.VMEM((count, rows, width), LOW),
            pltpu.SemaphoreType.DMA((count - 1,)),
            pltpu.SemaphoreType.DMA((count - 1,)),
        ],
        compiler_params=pltpu.CompilerParams(collective_id=ident, has_side_effects=True),
        name="seq_scatter",
    )(blocks)


def head_sum(term):
    def add(heads):
        total = None
        for head in range(heads):
            piece = term(head, slice(head * HEAD_DIM, (head + 1) * HEAD_DIM))
            total = piece if total is None else total + piece
        return total

    return add


def cross_attend_kernel(
    rows_ref, text_ref, query_weight_ref, text_weight_ref, bias_ref, gain_ref,
    query_pre_ref, key_pre_ref, query_ref, kv_ref, square_ref, out_ref, turned_ref, total_ref,
    stage, slots, send, recv,
):
    heads = query_ref.shape[1] // HEAD_DIM
    width = rows_ref.shape[1]
    factor = LOG2E / math.sqrt(HEAD_DIM)
    tensor_barrier()
    stage[...] = jnp.zeros(stage.shape, WIDE)
    query_pre_ref[...] = (
        jnp.dot(rows_ref[...], query_weight_ref[...], preferred_element_type=WIDE)
        + bias_ref[0:1]
    )
    key_pre_ref[...] = (
        jnp.dot(text_ref[...], text_weight_ref[0], preferred_element_type=WIDE) + bias_ref[1:2]
    )
    for part, pre_ref in enumerate((query_pre_ref, key_pre_ref)):
        squares = head_sum(lambda head, lanes: pre_ref[:, lanes] * pre_ref[:, lanes])(heads)
        stage[part : part + 1, : pre_ref.shape[0]] = rows_to_lanes(squares)
    tensor_send(stage, slots, send, recv)
    values = jnp.dot(text_ref[...], text_weight_ref[1], preferred_element_type=WIDE)
    kv_ref[1] = (values + bias_ref[2:3]).astype(LOW)
    total = tensor_collect(stage, slots, send, recv)
    square_ref[...] = total
    for part, pre_ref in enumerate((query_pre_ref, key_pre_ref)):
        square = total[part : part + 1, : pre_ref.shape[0]]
        rate = lanes_to_rows(lax.rsqrt(square / width + eps_norm))
        for head in range(heads):
            lanes = slice(head * HEAD_DIM, (head + 1) * HEAD_DIM)
            normed = (pre_ref[:, lanes] * rate * gain_ref[part : part + 1, lanes]).astype(LOW)
            if part == 0:
                query_ref[:, lanes] = normed
            else:
                kv_ref[0, :, lanes] = normed

    def step(head, carry):
        lanes = head_lanes(head)
        scores = over_last(kv_ref[0, :, lanes], query_ref[:, lanes]) * factor
        peak = jnp.max(scores, axis=0, keepdims=True)
        terms = jnp.exp2(scores - peak)
        summed = jnp.sum(terms, axis=0, keepdims=True)
        attended = (
            lax.dot_general(
                kv_ref[1, :, lanes],
                terms.astype(LOW),
                (((0,), (0,)), ((), ())),
                preferred_element_type=WIDE,
            )
            / summed
        )
        turned_ref[head] = attended
        out_ref[:, lanes] = jnp.transpose(attended).astype(LOW)
        total_ref[head] = peak + jnp.log2(summed)
        return carry

    lax.fori_loop(0, heads, step, 0)


def cross_attend(rows_low, text_all, query_weight, text_weights, bias, gains, ident):
    rows = rows_low.shape[0]
    tokens = text_all.shape[0]
    width = query_weight.shape[1]
    heads = width // HEAD_DIM
    count = lax.axis_size("tensor")
    vmem = pl.BlockSpec(memory_space=pltpu.VMEM)
    dma = pltpu.SemaphoreType.DMA
    return pl.pallas_call(
        cross_attend_kernel,
        out_shape=(
            jax.ShapeDtypeStruct((rows, width), WIDE),
            jax.ShapeDtypeStruct((tokens, width), WIDE),
            jax.ShapeDtypeStruct((rows, width), LOW),
            jax.ShapeDtypeStruct((2, tokens, width), LOW),
            jax.ShapeDtypeStruct((8, rows), WIDE),
            jax.ShapeDtypeStruct((rows, width), LOW),
            jax.ShapeDtypeStruct((heads, HEAD_DIM, rows), WIDE),
            jax.ShapeDtypeStruct((heads, 1, rows), WIDE),
        ),
        in_specs=[vmem] * 6,
        out_specs=(vmem,) * 8,
        scratch_shapes=[
            pltpu.VMEM((8, rows), WIDE),
            pltpu.VMEM((count, 8, rows), WIDE),
            dma((count - 1,)),
            dma((count - 1,)),
        ],
        compiler_params=pltpu.CompilerParams(
            collective_id=ident, has_side_effects=True, vmem_limit_bytes=56 << 20
        ),
        name="cross_attend",
    )(rows_low, text_all, query_weight, text_weights, bias, gains)


def cross_back_kernel(
    width, query_ref, kv_ref, turned_ref, total_ref, grad_ref, query_pre_ref, key_pre_ref,
    square_ref, text_square_ref, gain_ref, query_low_ref, text_low_ref, sums_ref,
    centre, query_turned, work, text_work, leaving, landing, stage, slots, text_send, text_recv,
    send, recv,
):
    heads = query_ref.shape[1] // HEAD_DIM
    tokens = key_pre_ref.shape[0]
    scale = 1.0 / math.sqrt(HEAD_DIM)
    places = plane_places()
    count = slots.shape[0]
    mine = lax.axis_index("tensor")
    barrier = pltpu.get_barrier_semaphore()
    for place in places[1:]:
        pl.semaphore_signal(
            barrier, inc=1, device_id={"seq": place}, device_id_type=pl.DeviceIdType.MESH
        )
    for hop in range(1, count):
        pl.semaphore_signal(
            barrier, inc=1, device_id={"tensor": lax.rem(mine + hop, count)},
            device_id_type=pl.DeviceIdType.MESH)
    pl.semaphore_wait(barrier, 3 + count - 1)

    for head in range(heads):
        lanes = slice(head * HEAD_DIM, (head + 1) * HEAD_DIM)
        grads = jnp.transpose(grad_ref[:, lanes].astype(WIDE))
        centre[head] = jnp.sum(grads * turned_ref[head], axis=0, keepdims=True)
    stage[...] = jnp.zeros(stage.shape, WIDE)
    sums_ref[...] = jnp.zeros(sums_ref.shape, WIDE)

    def step(head, carry):
        lanes = head_lanes(head)
        keys = kv_ref[0, :, lanes]
        query = query_ref[:, lanes]
        grads = grad_ref[:, lanes]
        probs = jnp.exp2(over_last(keys, query) * (scale * LOG2E) - total_ref[head])
        grad_probs = over_last(kv_ref[1, :, lanes], grads)
        grad_scores = (probs * (grad_probs - centre[head])).astype(LOW)
        key_grads = jnp.dot(grad_scores, query, preferred_element_type=WIDE) * scale
        leaving[0, :, lanes] = key_grads.astype(LOW)
        value_grads = jnp.dot(probs.astype(LOW), grads, preferred_element_type=WIDE)
        leaving[1, :, lanes] = value_grads.astype(LOW)
        query_turned[head] = lax.dot_general(
            keys, grad_scores, (((0,), (0,)), ((), ())), preferred_element_type=WIDE
        )
        return carry

    lax.fori_loop(0, heads, step, 0)

    def owned(place):
        return pl.ds(pl.multiple_of(place * tokens, 16), tokens)

    def text_copy(relation, part):
        place = places[relation + 1]
        return plane_copy(
            leaving.at[part, owned(place)],
            landing.at[relation, part],
            text_send.at[relation, part],
            text_recv.at[relation, part],
            place,
        )

    for relation in (2, 1, 0):
        for part in range(2):
            text_copy(relation, part).start()

    rate_row = lax.rsqrt(square_ref[0:1] / width + eps_norm)
    rate = lanes_to_rows(rate_row)
    terms = None
    for head in range(heads):
        lanes = slice(head * HEAD_DIM, (head + 1) * HEAD_DIM)
        grads = jnp.transpose(query_turned[head]) * scale
        pre = query_pre_ref[:, lanes]
        sums_ref[3:4, lanes] = jnp.sum(grads * pre * rate, axis=0, keepdims=True)
        grads = grads * gain_ref[0:1, lanes]
        work[:, lanes] = grads
        terms = grads * pre if terms is None else terms + grads * pre
    stage[0:1] = rows_to_lanes(terms)

    for relation in range(3):
        for part in range(2):
            text_copy(relation, part).wait_recv()
    for part in range(2):
        total = leaving[part, owned(places[0])].astype(WIDE)
        for relation in range(3):
            total = total + landing[relation, part].astype(WIDE)
        text_work[part] = total
    text_row = lax.rsqrt(text_square_ref[0:1] / width + eps_norm)
    text_rate = lanes_to_rows(text_row)
    terms = None
    for head in range(heads):
        lanes = slice(head * HEAD_DIM, (head + 1) * HEAD_DIM)
        grads = text_work[0, :, lanes]
        pre = key_pre_ref[:, lanes]
        sums_ref[4:5, lanes] = jnp.sum(grads * pre * text_rate, axis=0, keepdims=True)
        grads = grads * gain_ref[1:2, lanes]
        text_work[0, :, lanes] = grads
        terms = grads * pre if terms is None else terms + grads * pre
    stage[1:2, :tokens] = rows_to_lanes(terms)

    tensor_send(stage, slots, send, recv)
    sums_ref[2:3] = jnp.sum(text_work[1], axis=0, keepdims=True)
    text_low_ref[1] = text_work[1].astype(LOW)
    back_total = tensor_collect(stage, slots, send, recv)
    back = lanes_to_rows(rate_row * rate_row * rate_row * back_total[0:1] / width)
    text_back = lanes_to_rows(text_row * text_row * text_row * back_total[1:2, :tokens] / width)
    for head in range(heads):
        lanes = slice(head * HEAD_DIM, (head + 1) * HEAD_DIM)
        grads = work[:, lanes] * rate - query_pre_ref[:, lanes] * back
        sums_ref[0:1, lanes] = jnp.sum(grads, axis=0, keepdims=True)
        query_low_ref[:, lanes] = grads.astype(LOW)
        grads = text_work[0, :, lanes] * text_rate - key_pre_ref[:, lanes] * text_back
        sums_ref[1:2, lanes] = jnp.sum(grads, axis=0, keepdims=True)
        text_low_ref[0, :, lanes] = grads.astype(LOW)
    for relation in range(3):
        for part in range(2):
            text_copy(relation, part).wait_send()


def cross_back(saved, grad_low, key_pre_own, text_squares, gains, model_width, ident):
    query_pre, _, query_low, kv_low, squares, _, turned, total = saved
    rows, width = query_low.shape
    heads = width // HEAD_DIM
    tokens = key_pre_own.shape[0]
    count = lax.axis_size("tensor")
    vmem = pl.BlockSpec(memory_space=pltpu.VMEM)
    dma = pltpu.SemaphoreType.DMA
    return pl.pallas_call(
        functools.partial(cross_back_kernel, model_width),
        out_shape=(
            jax.ShapeDtypeStruct((rows, width), LOW),
            jax.ShapeDtypeStruct((2, tokens, width), LOW),
            jax.ShapeDtypeStruct((8, width), WIDE),
        ),
        in_specs=[vmem] * 10,
        out_specs=(vmem,) * 3,
        scratch_shapes=[
            pltpu.VMEM((heads, 1, rows), WIDE),
            pltpu.VMEM((heads, HEAD_DIM, rows), WIDE),
            pltpu.VMEM((rows, width), WIDE),
            pltpu.VMEM((2, tokens, width), WIDE),
            pltpu.VMEM(kv_low.shape, LOW),
            pltpu.VMEM((3, 2, tokens, width), LOW),
            pltpu.VMEM((8, rows), WIDE),
            pltpu.VMEM((count, 8, rows), WIDE),
            dma((3, 2)),
            dma((3, 2)),
            dma((count - 1,)),
            dma((count - 1,)),
        ],
        compiler_params=pltpu.CompilerParams(
            collective_id=ident, has_side_effects=True, vmem_limit_bytes=56 << 20
        ),
        name="cross_back",
    )(
        query_low, kv_low, turned, total, grad_low, query_pre, key_pre_own, squares, text_squares,
        gains,
    )


def head_forward(query, keys, values, key_ok, score_scale):
    scores = (
        jnp.einsum("csh,clh->csl", query, keys, preferred_element_type=jnp.float32) * score_scale
    )
    scores = jnp.where(key_ok[:, None, :], scores, -jnp.inf)
    row_peak = jnp.max(scores, axis=-1, keepdims=True)
    exp_terms = jnp.exp(scores - row_peak)
    summed = jnp.sum(exp_terms, axis=-1, keepdims=True)
    probs_low = (exp_terms / summed).astype(jnp.bfloat16)
    attended = jnp.einsum("csl,clh->csh", probs_low, values, preferred_element_type=jnp.float32)
    return (attended, row_peak[..., 0] + jnp.log(summed[..., 0]))


def head_backward(query, keys, values, key_ok, log_total, grad_att, score_scale):
    scores = (
        jnp.einsum("csh,clh->csl", query, keys, preferred_element_type=jnp.float32) * score_scale
    )
    probs = jnp.where(key_ok[:, None, :], jnp.exp(scores - log_total[..., None]), 0.0)
    grad_probs = jnp.einsum("csh,clh->csl", grad_att, values, preferred_element_type=jnp.float32)
    centre = jnp.sum(probs * grad_probs, axis=-1)
    grad_scores = (probs * (grad_probs - centre[..., None])).astype(jnp.bfloat16)
    grad_query = (
        jnp.einsum("csl,clh->csh", grad_scores, keys, preferred_element_type=jnp.float32)
        * score_scale
    )
    grad_keys = (
        jnp.einsum("csl,csh->clh", grad_scores, query, preferred_element_type=jnp.float32)
        * score_scale
    )
    grad_values = jnp.einsum(
        "csl,csh->clh", probs.astype(jnp.bfloat16), grad_att, preferred_element_type=jnp.float32
    )
    return (grad_query, centre, grad_keys, grad_values)


def shards(
    hidden,
    teacher,
    text,
    time_embed,
    lengths,
    positions,
    modulation,
    self_in,
    self_bias,
    self_out,
    norm_gains,
    cross_gain,
    cross_shift,
    cross_q,
    cross_kv,
    cross_bias,
    cross_out,
    ffn_in,
    ffn_in_bias,
    ffn_out,
    out_bias,
):
    low_type = jnp.bfloat16
    wide_type = jnp.float32
    clip_count, seq_rows, model_width = hidden.shape
    local_width = self_in.shape[2]
    local_heads = local_width // HEAD_DIM
    text_local = text.shape[1]
    seq_count = lax.axis_size("seq")
    slot_count = seq_rows * seq_count
    text_count = text_local * seq_count
    flat_rows = clip_count * seq_rows
    score_scale = 1.0 / math.sqrt(HEAD_DIM)
    seq_place = lax.axis_index("seq")
    clip_first = lax.axis_index("dp") * clip_count
    clip_lengths = lax.dynamic_slice_in_dim(lengths, clip_first, clip_count)
    key_valid = jnp.arange(slot_count, dtype=jnp.int32)[None, :] < clip_lengths[:, None]
    row_ids = seq_place * seq_rows + jnp.arange(seq_rows, dtype=jnp.int32)
    row_valid = row_ids[None, :] < clip_lengths[:, None]
    text_valid = jnp.ones((clip_count, text_count), dtype=jnp.bool_)
    valid_total = jnp.sum(lengths).astype(wide_type)
    modulated = modulation[None] + time_embed
    cosine_rep, sine_rep = rope_tables(positions, HEAD_DIM)
    rotate_now = functools.partial(
        rotate, cosine_rep=cosine_rep, sine_rep=sine_rep, swap_matrix=swap_table(HEAD_DIM)
    )
    head_shape = (clip_count, seq_rows, local_heads, HEAD_DIM)
    clip_ids = jnp.arange(flat_rows, dtype=jnp.int32) // seq_rows
    clip_table = (clip_ids[:, None] == jnp.arange(clip_count, dtype=jnp.int32)[None, :]).astype(
        wide_type
    )
    valid_rows = row_valid.reshape(flat_rows)
    hidden_rows = hidden.reshape(flat_rows, model_width)
    teacher_rows = teacher.reshape(flat_rows, model_width)

    def per_row(index_no):
        if clip_count == 1:
            return modulated[:, index_no]
        return jnp.dot(clip_table, modulated[:, index_no], precision=lax.Precision.HIGHEST)

    def per_clip(values):
        if clip_count == 1:
            return jnp.sum(values, axis=0, keepdims=True)
        return jnp.dot(clip_table.T, values, precision=lax.Precision.HIGHEST)

    scale_one = per_row(1)
    gate_one = per_row(2)
    scale_two = per_row(4)
    gate_two = per_row(5)
    normed_one = layer_norm(hidden_rows)
    query_pad = -flat_rows % 128
    key_pad = -flat_rows % 16

    def pad_queries(values):
        return jnp.pad(values, ((0, query_pad), (0, 0)))

    attn_in = pad_queries((normed_one * (1.0 + scale_one) + per_row(0)).astype(low_type))
    cosine_flat = pad_queries(cosine_rep.reshape(flat_rows, HEAD_DIM))
    sine_flat = pad_queries(sine_rep.reshape(flat_rows, HEAD_DIM)) * jnp.where(
        jnp.arange(HEAD_DIM) % 2 == 0, -1.0, 1.0
    )
    self_gains = norm_gains[:2]
    proj_pre, query_flat, own_kv, proj_squares = project(
        attn_in, self_in, self_bias, self_gains, cosine_flat, sine_flat, flat_rows + key_pad, 6
    )
    plane = seq_count == 4 and clip_count == 1
    if plane:
        attn_low, attn_turned, self_totals, got_kv = attend(
            query_flat, own_kv, clip_lengths, flat_rows, 10
        )
    else:
        query_low = query_flat[:flat_rows].reshape(head_shape)
        key_low = own_kv[0, :flat_rows]
        value_low = own_kv[1, :flat_rows]
        local_kv = jnp.stack(
            [
                key_low.reshape(clip_count, seq_rows, local_width),
                value_low.reshape(clip_count, seq_rows, local_width),
            ]
        )
        whole_kv = lax.all_gather(local_kv, "seq", axis=2, tiled=True)
        keys_all = whole_kv[0].reshape(clip_count, slot_count, local_heads, HEAD_DIM)
        values_all = whole_kv[1].reshape(clip_count, slot_count, local_heads, HEAD_DIM)
        att_heads = []
        total_heads = []
        for head_no in range(local_heads):
            attended, log_total = head_forward(
                query_low[:, :, head_no],
                keys_all[:, :, head_no],
                values_all[:, :, head_no],
                key_valid,
                score_scale,
            )
            att_heads.append(attended)
            total_heads.append(log_total)
        attn_low = jnp.stack(att_heads, axis=2).astype(low_type).reshape(flat_rows, local_width)
        attn_low = pad_queries(attn_low)
        self_totals = jnp.stack(total_heads)
    branch_one = (
        line_sum([attn_low], [self_out], False, 0, flat_rows) + out_bias[0]
    )
    after_one = hidden_rows + branch_one * gate_one
    normed_three = layer_norm(after_one)
    cross_in = (normed_three * cross_gain + cross_shift).astype(low_type)
    text_low = text.astype(low_type)
    text_start = seq_place * text_local
    text_all = lax.all_gather(text_low, "seq", axis=1, tiled=True)
    cross_plane = plane and text_local % 128 == 0 and text_count <= flat_rows
    if cross_plane:
        cross_in = pad_queries(cross_in)
        cross_saved = cross_attend(
            cross_in, text_all[0], cross_q, cross_kv, cross_bias, norm_gains[2:], 7
        )
        cross_att_low = cross_saved[5]
    else:
        cross_query_pre = jnp.dot(cross_in, cross_q, preferred_element_type=wide_type) + cross_bias[0]
        text_proj = (
            jnp.einsum("ctd,kde->kcte", text_all, cross_kv, preferred_element_type=wide_type)
            + cross_bias[1:, None, None, :]
        )
        cross_sq, text_sq = small_sum(
            [
                jnp.sum(cross_query_pre * cross_query_pre, axis=-1),
                jnp.sum(text_proj[0] * text_proj[0], axis=-1),
            ],
            7,
        )
        text_rate_all = lax.rsqrt(text_sq / model_width + eps_norm)[..., None]
        text_key_low = (text_proj[0] * text_rate_all * norm_gains[3]).astype(low_type)
        text_value_low = text_proj[1].astype(low_type)
        text_key_pre = lax.dynamic_slice_in_dim(text_proj[0], text_start, text_local, 1)
        text_key_rate = lax.dynamic_slice_in_dim(text_rate_all, text_start, text_local, 1)
        cross_rate = lax.rsqrt(cross_sq / model_width + eps_norm)[:, None]
        cross_query_low = (
            (cross_query_pre * cross_rate * norm_gains[2]).astype(low_type).reshape(head_shape)
        )
        text_key_heads = text_key_low.reshape(clip_count, text_count, local_heads, HEAD_DIM)
        text_value_heads = text_value_low.reshape(clip_count, text_count, local_heads, HEAD_DIM)
        cross_heads = []
        cross_total_heads = []
        for head_no in range(local_heads):
            attended, log_total = head_forward(
                cross_query_low[:, :, head_no],
                text_key_heads[:, :, head_no],
                text_value_heads[:, :, head_no],
                text_valid,
                score_scale,
            )
            cross_heads.append(attended)
            cross_total_heads.append(log_total)
        cross_att_low = jnp.stack(cross_heads, axis=2).astype(low_type).reshape(flat_rows, local_width)
        cross_totals = jnp.stack(cross_total_heads)
    branch_two = (
        line_sum([cross_att_low], [cross_out], False, 1, flat_rows)
        + out_bias[1]
    )
    after_two = after_one + branch_two
    normed_two = layer_norm(after_two)
    ffn_input = (normed_two * (1.0 + scale_two) + per_row(3)).astype(low_type)
    pre_act = jnp.dot(ffn_input, ffn_in, preferred_element_type=wide_type) + ffn_in_bias
    act_low = gelu_tanh(pre_act).astype(low_type)
    branch_three = (
        line_sum([act_low], [ffn_out], False, 2, flat_rows) + out_bias[2]
    )
    result = after_two + branch_three * gate_two
    residue = jnp.where(valid_rows[:, None], result - teacher_rows, 0.0)
    grad_three = residue * gate_two
    grad_three_low = grad_three.astype(low_type)
    ffn_out_mix = jnp.dot(grad_three_low.T, act_low, preferred_element_type=wide_type)
    grad_act = jnp.dot(grad_three_low, ffn_out.T, preferred_element_type=wide_type)
    grad_pre = jax.vjp(gelu_tanh, pre_act)[1](grad_act)[0]
    grad_pre_low = grad_pre.astype(low_type)
    grad_pre_low, ffn_out_mix = lax.optimization_barrier(
        (grad_pre_low, row_major(ffn_out_mix.astype(low_type)))
    )
    part_ffn_out = scatter_rows(ffn_out_mix, 0)
    ffn_in_mix = jnp.dot(ffn_input.T, grad_pre_low, preferred_element_type=wide_type)
    grad_ffn_bias = jnp.sum(grad_pre, axis=0)
    grad_ffn_input = line_sum([grad_pre_low], [ffn_in.T], False, 3, flat_rows)
    grad_after_two = (
        residue + jax.vjp(layer_norm, after_two)[1](grad_ffn_input * (1.0 + scale_two))[0]
    )
    grad_two_low = grad_after_two.astype(low_type)
    cross_out_mix = jnp.dot(grad_two_low.T, cross_att_low[:flat_rows], preferred_element_type=wide_type)
    grad_cross_att = (
        jnp.dot(grad_two_low, cross_out.T, preferred_element_type=wide_type).astype(low_type)
    )
    if cross_plane:
        grad_cross_query_low, text_grad_low, cross_sums = cross_back(
            cross_saved,
            pad_queries(grad_cross_att),
            lax.dynamic_slice_in_dim(cross_saved[1], text_start, text_local, 0),
            lax.dynamic_slice_in_dim(
                jnp.broadcast_to(cross_saved[4][1:2, :text_count], (8, text_count)),
                text_start,
                text_local,
                1,
            ),
            norm_gains[2:],
            model_width,
            8,
        )
        text_grad_low = text_grad_low[:, None]
        grad_cross_bias = cross_sums[:3]
        gain_cross_query = cross_sums[3]
        gain_text_key = cross_sums[4]
    else:
        grad_cross_att = grad_cross_att.reshape(head_shape)
        cross_query_grads = []
        text_key_grads = []
        text_value_grads = []
        for head_no in range(local_heads):
            head_grads = head_backward(
                cross_query_low[:, :, head_no],
                text_key_heads[:, :, head_no],
                text_value_heads[:, :, head_no],
                text_valid,
                cross_totals[head_no],
                grad_cross_att[:, :, head_no],
                score_scale,
            )
            cross_query_grads.append(head_grads[0])
            text_key_grads.append(head_grads[2])
            text_value_grads.append(head_grads[3])
        grad_cross_query = jnp.stack(cross_query_grads, axis=2).reshape(flat_rows, local_width)
        text_grads_all = jnp.stack(
            [
                jnp.stack(text_key_grads, axis=2).reshape(clip_count, text_count, local_width),
                jnp.stack(text_value_grads, axis=2).reshape(clip_count, text_count, local_width),
            ]
        )
        text_blocks = text_grads_all.astype(low_type).reshape(
            2, clip_count, seq_count, text_local, local_width
        )
        text_blocks = jnp.transpose(text_blocks, (2, 1, 3, 0, 4)).reshape(
            seq_count, clip_count * text_local, 2 * local_width
        )
        text_rows = seq_scatter(text_blocks, 14)
        text_grads = [
            text_rows[:, j * local_width : (j + 1) * local_width].reshape(
                clip_count, text_local, local_width
            )
            for j in range(2)
        ]
        query_term, key_term = small_sum(
            [
                jnp.sum(grad_cross_query * norm_gains[2] * cross_query_pre, axis=-1),
                jnp.sum(text_grads[0] * norm_gains[3] * text_key_pre, axis=-1),
            ],
            8,
        )
        grad_cross_query_pre = (
            grad_cross_query * norm_gains[2] * cross_rate
            - cross_query_pre * cross_rate**3 * query_term[:, None] / model_width
        )
        gain_cross_query = jnp.sum(grad_cross_query * cross_query_pre * cross_rate, axis=0)
        grad_cross_query_low = grad_cross_query_pre.astype(low_type)
        grad_text_key_pre = (
            text_grads[0] * norm_gains[3] * text_key_rate
            - text_key_pre * text_key_rate**3 * key_term[..., None] / model_width
        )
        gain_text_key = jnp.sum(text_grads[0] * text_key_pre * text_key_rate, axis=(0, 1))
        grad_cross_bias = jnp.stack(
            [
                jnp.sum(grad_cross_query_pre, axis=0),
                jnp.sum(grad_text_key_pre, axis=(0, 1)),
                jnp.sum(text_grads[1], axis=(0, 1)),
            ]
        )
        text_grad_low = jnp.stack([grad_text_key_pre, text_grads[1]]).astype(low_type)
    grad_cross_query_low, ffn_in_mix, part_ffn_out = lax.optimization_barrier(
        (grad_cross_query_low, row_major(ffn_in_mix.astype(low_type)), part_ffn_out)
    )
    part_ffn_in = scatter_rows(ffn_in_mix, 0)
    cross_q_mix = jnp.dot(cross_in.T, grad_cross_query_low, preferred_element_type=wide_type)
    grad_cross_in = line_sum([grad_cross_query_low], [cross_q], True, 4, flat_rows)
    cross_kv_mix = jnp.einsum(
        "ctd,kcte->kde", text_low, text_grad_low, preferred_element_type=wide_type
    )
    grad_text = lax.psum(
        jnp.einsum(
            "kcte,kde->ctd", text_grad_low, cross_kv, preferred_element_type=wide_type
        ).astype(jnp.bfloat16),
        "tensor",
    ).astype(jnp.float32)
    grad_cross_gain = jnp.sum(grad_cross_in * normed_three, axis=0)
    grad_cross_shift = jnp.sum(grad_cross_in, axis=0)
    grad_after_one = (
        grad_after_two + jax.vjp(layer_norm, after_one)[1](grad_cross_in * cross_gain)[0]
    )
    grad_one = grad_after_one * gate_one
    grad_one_low = grad_one.astype(low_type)
    self_out_mix = jnp.dot(grad_one_low.T, attn_low[:flat_rows], preferred_element_type=wide_type)
    grad_attn = (
        jnp.dot(grad_one_low, self_out.T, preferred_element_type=wide_type)
        .astype(low_type)
        .reshape(head_shape)
    )
    group_mix = jnp.concatenate(
        [cross_out_mix, cross_q_mix, self_out_mix, cross_kv_mix[0], cross_kv_mix[1]], axis=-1
    ).astype(low_type)
    grad_attn, group_mix = lax.optimization_barrier((grad_attn, row_major(group_mix)))
    part_group = scatter_rows(group_mix, 0)
    if plane:
        query_grads, kv_grads = attend_back(
            query_flat,
            own_kv,
            got_kv,
            attn_turned,
            self_totals,
            pad_queries(grad_attn.reshape(flat_rows, local_width)),
            clip_lengths,
            flat_rows,
            11,
        )
    else:
        query_grads = []
        key_grads = []
        value_grads = []
        for head_no in range(local_heads):
            head_grads = head_backward(
                query_low[:, :, head_no],
                keys_all[:, :, head_no],
                values_all[:, :, head_no],
                key_valid,
                self_totals[head_no],
                grad_attn[:, :, head_no],
                score_scale,
            )
            query_grads.append(head_grads[0])
            key_grads.append(head_grads[2])
            value_grads.append(head_grads[3])
        owner_grads = [
            jnp.stack(parts, axis=2)
            .astype(jnp.bfloat16)
            .reshape(clip_count, seq_count, seq_rows, local_width)
            for parts in (key_grads, value_grads)
        ]
        owner_grads = jnp.concatenate(
            [
                jnp.swapaxes(part, 0, 1).reshape(seq_count, flat_rows, local_width)
                for part in owner_grads
            ],
            axis=-1,
        )
        pad_rows = -flat_rows % 16
        owner_grads = jnp.pad(owner_grads, ((0, 0), (0, pad_rows), (0, 0)))
        kv_rows = lax.psum_scatter(
            owner_grads.reshape(seq_count * (flat_rows + pad_rows), 2 * local_width),
            "seq",
            scatter_dimension=0,
            tiled=True,
        )[:flat_rows].astype(jnp.float32)
        kv_grads = jnp.stack(
            [pad_queries(kv_rows[:, :local_width]), pad_queries(kv_rows[:, local_width:])]
        )
        query_grads = pad_queries(
            jnp.stack(query_grads, axis=2).reshape(flat_rows, local_width)
        )
    query_grads, part_ffn_in = lax.optimization_barrier((query_grads, part_ffn_in))
    *grad_proj_low, proj_sums = unproject(
        query_grads,
        kv_grads,
        proj_pre,
        proj_squares,
        self_gains,
        cosine_flat,
        sine_flat,
        model_width,
        9,
    )
    grad_self_bias = proj_sums[:3]
    self_in_mix = jnp.dot(
        attn_in.T, jnp.concatenate(grad_proj_low, axis=-1), preferred_element_type=wide_type
    ).astype(low_type)
    grad_proj_low, self_in_mix, part_group = lax.optimization_barrier(
        (grad_proj_low, row_major(self_in_mix), part_group)
    )
    part_self_in = scatter_rows(self_in_mix, 0)
    grad_attn_in = line_sum(grad_proj_low, [self_in], True, 5, flat_rows)
    grad_hidden = (
        grad_after_one + jax.vjp(layer_norm, hidden_rows)[1](grad_attn_in * (1.0 + scale_one))[0]
    )
    grad_time_local = jnp.stack(
        [
            per_clip(grad_attn_in),
            per_clip(grad_attn_in * normed_one),
            per_clip(grad_after_one * branch_one),
            per_clip(grad_ffn_input),
            per_clip(grad_ffn_input * normed_two),
            per_clip(residue * branch_three),
        ],
        axis=1,
    )
    grad_out_bias = jnp.stack(
        [jnp.sum(grad_one, axis=0), jnp.sum(grad_after_two, axis=0), jnp.sum(grad_three, axis=0)]
    )
    stream_values = (
        grad_time_local,
        grad_cross_gain,
        grad_cross_shift,
        grad_out_bias,
        jnp.sum(residue * residue),
    )
    grad_time_local, grad_cross_gain, grad_cross_shift, grad_out_bias, square_local = stream_values
    grad_norm_gains = jnp.concatenate(
        [proj_sums[3:5], gain_cross_query[None], gain_text_key[None]]
    )
    time_pair, sums = plane_sum(
        grad_time_local,
        [
            grad_self_bias,
            grad_norm_gains,
            grad_cross_gain,
            grad_cross_shift,
            grad_cross_bias,
            grad_ffn_bias,
            grad_out_bias,
            square_local,
        ],
        13,
    )
    grad_time, time_all = time_pair
    sum_modulation = jnp.sum(time_all, axis=0)
    (
        sum_self_bias,
        sum_gains,
        sum_cross_gain,
        sum_cross_shift,
        sum_cross_bias,
        sum_ffn_bias,
        sum_out_bias,
        square_sum,
    ) = sums
    loss = square_sum / (valid_total * model_width)
    part_ffn_in = part_ffn_in.astype(wide_type)
    part_ffn_out = part_ffn_out.T.astype(wide_type)
    pieces = [
        part_group[:, j * local_width : (j + 1) * local_width].astype(wide_type) for j in range(5)
    ]
    part_cross_out = pieces[0].T
    part_cross_q = pieces[1]
    part_self_out = pieces[2].T
    part_cross_kv = jnp.stack([pieces[3], pieces[4]])
    part_self_in = jnp.stack(
        [part_self_in[:, j * local_width : (j + 1) * local_width] for j in range(3)]
    ).astype(wide_type)
    result_out = result.reshape(clip_count, seq_rows, model_width)
    grad_hidden_out = grad_hidden.reshape(clip_count, seq_rows, model_width)
    return (
        result_out,
        loss,
        grad_hidden_out,
        grad_text,
        grad_time,
        sum_modulation,
        part_self_in,
        sum_self_bias,
        part_self_out,
        sum_gains,
        sum_cross_gain,
        sum_cross_shift,
        part_cross_q,
        part_cross_kv,
        sum_cross_bias,
        part_cross_out,
        part_ffn_in,
        sum_ffn_bias,
        part_ffn_out,
        sum_out_bias,
    )


def solution(mesh):
    placed = (
        P("dp", "seq", None),
        P("dp", "seq", None),
        P("dp", "seq", None),
        P("dp", None, None),
        P(),
        P(None, "dp", "seq"),
        P(),
        P(None, None, "tensor"),
        P(None, "tensor"),
        P("tensor", None),
        P(None, "tensor"),
        P(),
        P(),
        P(None, "tensor"),
        P(None, None, "tensor"),
        P(None, "tensor"),
        P("tensor", None),
        P(None, "tensor"),
        P("tensor"),
        P("tensor", None),
        P(),
    )
    return jax.shard_map(
        shards,
        mesh=mesh,
        in_specs=placed,
        out_specs=(
            P("dp", "seq", None),
            P(),
            P("dp", "seq", None),
            P("dp", "seq", None),
            P("dp", None, None),
            P(),
            P(None, ("dp", "seq"), "tensor"),
            P(None, "tensor"),
            P("tensor", ("dp", "seq")),
            P(None, "tensor"),
            P(),
            P(),
            P(("dp", "seq"), "tensor"),
            P(None, ("dp", "seq"), "tensor"),
            P(None, "tensor"),
            P("tensor", ("dp", "seq")),
            P(("dp", "seq"), "tensor"),
            P("tensor"),
            P("tensor", ("dp", "seq")),
            P(),
        ),
        check_vma=False,
    )
```
